32 devices in a mesh: ctx: 8 (over y, x, core), head: 4 (over z).
Axes of the slice: x: 2, y: 2, z: 4, core: 2. Of those that a mesh axis runs over, the one named last changes fastest.
Arguments:
- tokens_x: bfloat16 [4096, 8192], P('ctx', 'head'), may hold values from -121 to 121
- raw_dt: float32 [128, 4096], P('head', 'ctx'), may hold values from -4 to 4
- in_b: bfloat16 [4096, 128], P('ctx'), may hold values from -0.5 to 0.5
- in_c: bfloat16 [4096, 128], P('ctx'), may hold values from -0.5 to 0.5
- decay_rate: float32 [128], P('head'), may hold values from 4.8828125e-06 to 2
- skip_gain: float32 [128], P('head'), may hold values from 0.5 to 1.5
- step_bias: float32 [128], P('head'), may hold values from -5 to -3
- grad_y: bfloat16 [4096, 8192], P('ctx', 'head'), may hold values from -121 to 121
Outputs:
- grad_x: bfloat16 [4096, 8192], P('ctx', 'head')
- grad_raw_dt: float32 [128, 4096], P('head', 'ctx')
- grad_b: float32 [4096, 128], P('ctx')
- grad_c: float32 [4096, 128], P('ctx')
- grad_rate: float32 [128], P('head')
- grad_skip: float32 [128], P('head')
- grad_bias: float32 [128], P('head')
The draws below stay inside these ranges and needn't reach their ends.
All inputs are finite; a program needn't handle non-finite values.
Results may differ from the reference program's by a relative error of at most 0.001.
Values sent between devices are 32-bit elements; how exact they have to be, the bound alone decides.
A program may use at most 128 MiB of HBM per device.

```python
import math
import jax
import jax.numpy as jnp
from jax import lax

HEADS = 128
HEAD_DIM = 64
STATE = 128
BLOCK = 256
TOK_DEV = 512
TOKENS = 4096


rise_level = 3.0


def head_kinds(key):
    kind_pick = jax.random.randint(jax.random.fold_in(key, 101), (HEADS,), 0, 8)
    balanced = kind_pick < 2
    quiet_heads = (kind_pick >= 2) & (kind_pick < 5)
    return (balanced, quiet_heads)


def bias_values(key):
    return jax.random.uniform(jax.random.fold_in(key, 102), (HEADS,), jnp.float32, -5.0, -3.0)


def column_spread(key, direction):
    balanced, quiet_heads = head_kinds(key)
    position = jnp.arange(TOKENS, dtype=jnp.float32) / max(TOKENS - 1, 1)
    level_curve = jnp.exp(direction * rise_level * (1.0 - 2.0 * position))
    column_scale = jnp.where(balanced[None, :], level_curve[:, None], 1.0)
    return jnp.repeat(column_scale, HEAD_DIM, axis=1)


def noise_field(noise_key):
    array_shape = (TOKENS, HEADS * HEAD_DIM)
    noise_values = jnp.clip(jax.random.normal(noise_key, array_shape, jnp.float32), -6.0, 6.0)
    return noise_values


def draw_tokens_x(key, part):
    return (noise_field(jax.random.fold_in(key, 105)) * column_spread(key, 1.0)).astype(jnp.bfloat16)


def draw_grad_y(key, part):
    return (noise_field(jax.random.fold_in(key, 106)) * column_spread(key, -1.0)).astype(jnp.bfloat16)


def draw_step_bias(key, part):
    return bias_values(key)


def draw_decay_rate(key, part):
    balanced, quiet_heads = head_kinds(key)
    head_bias = bias_values(key)
    pieces = TOKENS // TOK_DEV
    mean_step = TOK_DEV * jnp.exp(head_bias + 0.5)
    draw_keys = jax.random.split(jax.random.fold_in(key, 103), 3)
    drawn_rate = jnp.exp(jax.random.uniform(draw_keys[0], (HEADS,), jnp.float32, math.log(1.0 / (50 * TOKENS)), math.log(1.5)))
    growth = 2.0 * rise_level / max(pieces - 1, 1)
    balanced_rate = jax.random.uniform(draw_keys[1], (HEADS,), jnp.float32, 1.3, 1.7) * growth / mean_step
    quiet_rate = jnp.exp(jax.random.uniform(draw_keys[2], (HEADS,), jnp.float32, math.log(0.7), math.log(2.5))) / mean_step
    return jnp.where(balanced, balanced_rate, jnp.where(quiet_heads, quiet_rate, drawn_rate))


def draw_raw_dt(key, part):
    balanced, quiet_heads = head_kinds(key)
    draw_keys = jax.random.split(jax.random.fold_in(key, 104), 4)
    outside = jnp.clip(jax.random.normal(draw_keys[0], (HEADS, TOKENS), jnp.float32), -4.0, 4.0)
    inside = jax.random.uniform(draw_keys[1], (HEADS, TOKENS), jnp.float32, -4.0, -2.5)
    gap_start = jax.random.uniform(draw_keys[2], (HEADS, 1), jnp.float32, 0.1, 0.3) * TOKENS
    gap_end = jax.random.uniform(draw_keys[3], (HEADS, 1), jnp.float32, 0.7, 0.9) * TOKENS
    position = jnp.arange(TOKENS, dtype=jnp.float32)[None, :]
    in_gap = quiet_heads[:, None] & (position >= gap_start) & (position < gap_end)
    return jnp.where(in_gap, inside, outside)


def shard_levels(own_key, dims, cuts, least, high):
    level = 1.0
    for dim, parts in cuts:
        heights = jax.random.uniform(jax.random.fold_in(jax.random.fold_in(own_key, 6), dim), (parts,), jnp.float32, least / len(cuts), high / len(cuts))
        level = level * jnp.repeat(jnp.exp(heights), dims[dim] // parts).reshape((-1,) + (1,) * (len(dims) - 1 - dim))
    return level


def centred(key, shape, deviation, reach, shards=(), kind=jnp.bfloat16):
    entries = deviation * jax.random.normal(key, shape, jnp.float32)
    if shards:
        entries = entries * shard_levels(key, shape, shards, -0.22, 0.18)
    return jnp.clip(entries, -reach, reach).astype(kind)


def setup_inputs(seed: int = 0) -> dict:
    seeds = jax.random.split(jax.random.key(seed), 9)
    tokens_x = draw_tokens_x(jax.random.fold_in(seeds[8], 71), 0)
    raw_dt = draw_raw_dt(jax.random.fold_in(seeds[8], 71), 0)
    in_b = centred(seeds[2], (TOKENS, STATE), STATE ** -0.5, 0.5, ((0, 8),))
    in_c = centred(seeds[3], (TOKENS, STATE), STATE ** -0.5, 0.5, ((0, 8),))
    decay_rate = draw_decay_rate(jax.random.fold_in(seeds[8], 71), 0)
    skip_gain = jnp.clip(0.5 + 1.0 * jax.random.uniform(seeds[5], (HEADS,), jnp.float32) ** shard_levels(seeds[5], (HEADS,), ((0, 4),), -0.2, 0.2), 0.5, 1.5)
    step_bias = draw_step_bias(jax.random.fold_in(seeds[8], 71), 0)
    grad_y = draw_grad_y(jax.random.fold_in(seeds[8], 71), 0)
    return dict(tokens_x=tokens_x, raw_dt=raw_dt, in_b=in_b, in_c=in_c, decay_rate=decay_rate, skip_gain=skip_gain, step_bias=step_bias, grad_y=grad_y)


def layer_forward(values, raw_dt, in_b, in_c, decay_rate, skip_gain, step_bias, start_state):
    token_count, head_count, head_size = values.shape
    state_size = in_b.shape[1]
    block_count = token_count // BLOCK
    step_sizes = jax.nn.softplus(raw_dt + step_bias[:, None])
    log_decay = -decay_rate[:, None] * step_sizes
    x_blocks = values.reshape(block_count, BLOCK, head_count, head_size)
    step_blocks = step_sizes.reshape(head_count, block_count, BLOCK).transpose(1, 0, 2)
    decay_blocks = log_decay.reshape(head_count, block_count, BLOCK).transpose(1, 0, 2)
    b_blocks = in_b.reshape(block_count, BLOCK, state_size)
    c_blocks = in_c.reshape(block_count, BLOCK, state_size)
    positions = jnp.arange(BLOCK)
    causal = positions[:, None] >= positions[None, :]

    def one_block(carry_state, pieces):
        x_block, step_block, decay_block, b_block, c_block = pieces
        cum_decay = jnp.cumsum(decay_block, axis=1)
        scores = jnp.dot(c_block, b_block.T, precision=lax.Precision.HIGHEST)
        log_gap = cum_decay[:, :, None] - cum_decay[:, None, :]
        mixing = jnp.where(causal[None], jnp.exp(jnp.where(causal[None], log_gap, 0.0)), 0.0)
        mixing = mixing * scores[None] * step_block[:, None, :]
        within = jnp.einsum('hts,shp->thp', mixing, x_block, precision=lax.Precision.HIGHEST)
        carried = jnp.einsum('hpn,tn->thp', carry_state, c_block, precision=lax.Precision.HIGHEST)
        carried = carried * jnp.exp(cum_decay).T[:, :, None]
        block_out = within + carried + skip_gain[None, :, None] * x_block
        end_decay = cum_decay[:, -1]
        state_weight = jnp.exp(end_decay[:, None] - cum_decay) * step_block
        weighted = x_block * state_weight.T[:, :, None]
        next_state = jnp.exp(end_decay)[:, None, None] * carry_state
        next_state = next_state + jnp.einsum('shp,sn->hpn', weighted, b_block, precision=lax.Precision.HIGHEST)
        return (next_state, block_out)
    final_state, block_outs = lax.scan(jax.checkpoint(one_block), start_state, (x_blocks, step_blocks, decay_blocks, b_blocks, c_blocks))
    return (block_outs.reshape(token_count, head_count, head_size), final_state)

def reference(tokens_x, raw_dt, in_b, in_c, decay_rate, skip_gain, step_bias, grad_y):
    values = tokens_x.astype(jnp.float32).reshape(TOKENS, HEADS, HEAD_DIM)
    b_full = in_b.astype(jnp.float32)
    c_full = in_c.astype(jnp.float32)
    cotangent = grad_y.astype(jnp.float32).reshape(TOKENS, HEADS, HEAD_DIM)
    start_state = jnp.zeros((HEADS, HEAD_DIM, STATE), jnp.float32)

    def forward(values, raw_dt, b_full, c_full, decay_rate, skip_gain, step_bias):
        outputs, final_state = layer_forward(values, raw_dt, b_full, c_full, decay_rate, skip_gain, step_bias, start_state)
        return outputs
    outputs, pullback = jax.vjp(forward, values, raw_dt, b_full, c_full, decay_rate, skip_gain, step_bias)
    grad_v, grad_raw, grad_b, grad_c, grad_rate, grad_skip, grad_bias = pullback(cotangent)
    grad_x = grad_v.reshape(TOKENS, HEADS * HEAD_DIM).astype(jnp.bfloat16)
    return (grad_x, grad_raw, grad_b, grad_c, grad_rate, grad_skip, grad_bias)
```

```python
import functools
import types

import jax
import jax.numpy as jnp
from jax import lax
from jax.experimental import pallas as pl
from jax.experimental.pallas import tpu as pltpu
from jax.sharding import PartitionSpec as P

CHUNK = 128
GROUP = 8
F32 = jnp.float32
BF16 = jnp.bfloat16
HIGH = lax.Precision.HIGHEST
NT = (((1,), (1,)), ((), ()))
MESH = pl.DeviceIdType.MESH


def mm(a, b):
    return jnp.dot(a, b, preferred_element_type=F32)


def mm_nt(a, b):
    return lax.dot_general(a, b, NT, preferred_element_type=F32)


def split(a):
    high = a.astype(BF16)
    return high, (a - high.astype(F32)).astype(BF16)


def twice(a, axis):
    return jnp.concatenate([a, a], axis=axis)


def softplus(v):
    return jnp.maximum(v, 0.0) + jnp.log1p(jnp.exp(-jnp.abs(v)))


def lanes(column, width=CHUNK):
    return jnp.broadcast_to(column, (column.shape[0], width))


def per_head(rows, matrix):
    heads = rows.shape[0]
    shaped = matrix.reshape(heads, matrix.shape[0] // heads, matrix.shape[1])
    return (shaped * rows[:, None, :]).reshape(matrix.shape)


def head_sums(matrix, heads):
    return jnp.sum(matrix.reshape(heads, matrix.shape[0] // heads, matrix.shape[1]), axis=1)


def pair_blocks(first, second):
    zero = jnp.zeros_like(first)
    return jnp.concatenate(
        [jnp.concatenate([first, zero], axis=1), jnp.concatenate([zero, second], axis=1)], axis=0
    )


def triangle(lower):
    row = lax.broadcasted_iota(jnp.int32, (CHUNK, CHUNK), 0)
    col = lax.broadcasted_iota(jnp.int32, (CHUNK, CHUNK), 1)
    return (row >= col) if lower else (row <= col)


def eye(n):
    row = lax.broadcasted_iota(jnp.int32, (n, n), 0)
    col = lax.broadcasted_iota(jnp.int32, (n, n), 1)
    return row == col


def column_of(row):
    n = row.shape[1]
    return jnp.sum(jnp.where(eye(n), jnp.broadcast_to(row, (n, n)), 0.0), axis=1, keepdims=True)


def row_of(column):
    n = column.shape[0]
    return jnp.sum(jnp.where(eye(n), jnp.broadcast_to(column, (n, n)), 0.0), axis=0, keepdims=True)


def span_of(c):
    return slice(c * CHUNK, (c + 1) * CHUNK)


def inputs_and_outputs():
    return ("x_hbm", "g_hbm", "raw", "bias", "rate", "skip", "b", "c",
            "gx_hbm", "graw", "gb", "gc", "grate", "gskip", "gbias")


def scratch_of(heads, tokens, size, state, peers):
    groups, chunks, chips = heads // GROUP, tokens // CHUNK, peers // 2
    wide, half = GROUP * size, size // 2
    vmem = pltpu.VMEM
    dma = pltpu.SemaphoreType.DMA
    halves = (groups, GROUP, half, state)
    return dict(
        x=vmem((groups, tokens, wide), BF16),
        g=vmem((groups, tokens, wide), BF16),
        xt=vmem((groups, wide, tokens), BF16),
        gt=vmem((groups, wide, tokens), BF16),
        dt=vmem((heads, tokens), F32),
        cum=vmem((heads, tokens), F32),
        weight=vmem((heads, tokens), F32),
        reach=vmem((heads, tokens), F32),
        step=vmem((chunks, heads, CHUNK), F32),
        before=vmem((chunks + 1, heads, CHUNK), F32),
        after=vmem((chunks + 1, heads, CHUNK), F32),
        s=vmem((groups, chunks, wide, state), F32),
        r=vmem((groups, chunks, wide, state), F32),
        total=vmem((2, groups, GROUP, size, state), F32),
        ends=vmem((peers, heads, CHUNK), F32),
        coef=vmem((2, chips, heads, CHUNK), F32),
        pair_in=vmem((2,) + halves, F32),
        agg=vmem((2,) + halves, F32),
        chip_in=vmem((chips,) + halves, F32),
        give=vmem((2,) + halves, F32),
        state_in=vmem((2, groups, GROUP, size, state), F32),
        dxt=vmem((groups, chunks, wide, CHUNK), F32),
        row=vmem((groups, chunks, GROUP, CHUNK), F32),
        col=vmem((groups, chunks, GROUP, CHUNK), F32),
        cross=vmem((groups, GROUP, CHUNK), F32),
        dg=vmem((chunks, CHUNK, CHUNK), F32),
        parts=vmem((groups, chunks, 4, wide, state), BF16),
        gx=vmem((groups, chunks, CHUNK, wide), BF16),
        zown=vmem((chunks, 2, CHUNK, state), F32),
        zsum=vmem((chunks, 2, CHUNK, state), F32),
        zin=vmem((2, chunks, 2, CHUNK, state), F32),
        ztot=vmem((chunks, 2, CHUNK, state), F32),
        params=vmem((heads, CHUNK), F32),
        params_in=vmem((peers, heads, CHUNK), F32),
        load_sem=dma((2, groups)),
        end_send=dma((peers,)),
        end_recv=dma((peers,)),
        pair_send=dma((2, groups)),
        pair_recv=dma((2, groups)),
        chip_send=dma((chips, groups)),
        chip_recv=dma((chips, groups)),
        back_send=dma((2, groups)),
        back_recv=dma((2, groups)),
        in_send=dma((chunks, 2)),
        out_send=dma((chunks, 2)),
        z_recv=dma((2, chunks, 2)),
        param_send=dma((peers,)),
        param_recv=dma((peers,)),
        gx_sem=dma((groups, chunks)),
    )


def kernel(names, peers, line, *refs):
    k = types.SimpleNamespace(**dict(zip(names, refs)))
    heads, tokens = k.raw.shape
    state = k.b.shape[1]
    groups, chunks, chips = heads // GROUP, tokens // CHUNK, peers // 2
    wide = k.x.shape[2]
    size = wide // GROUP
    half = size // 2
    me, zpos = lax.axis_index("ctx"), lax.axis_index("head")
    odd, chip = me % 2, me // 2
    is_odd = odd == 1
    mate = me + 1 - 2 * odd

    left = zpos < line // 2
    inner = jnp.where(left, zpos + 1, zpos - 1)
    outer = jnp.where(left, zpos - 1, zpos + 1)
    has_outer = jnp.logical_and(zpos > 0, zpos < line - 1)
    is_mid = jnp.logical_or(zpos == line // 2 - 1, zpos == line // 2)
    in_slot = jnp.where(is_mid, 1, 0)

    barrier = pltpu.get_barrier_semaphore()
    for d in range(1, peers):
        pl.semaphore_signal(barrier, inc=1, device_id={"ctx": (me + d) % peers}, device_id_type=MESH)
    pl.semaphore_signal(barrier, inc=1, device_id={"head": inner}, device_id_type=MESH)

    @pl.when(has_outer)
    def _():
        pl.semaphore_signal(barrier, inc=1, device_id={"head": outer}, device_id_type=MESH)

    def load(i, group):
        src, dst = ((k.x_hbm, k.x), (k.g_hbm, k.g))[i]
        at = pl.ds(pl.multiple_of(group * wide, wide), wide)
        return pltpu.make_async_copy(src.at[:, at], dst.at[group], k.load_sem.at[i, group])

    for group in range(groups):
        load(0, group).start()
        load(1, group).start()

    dt = softplus(k.raw[...] + column_of(k.bias[...]))
    k.dt[...] = dt
    rate = column_of(k.rate[...])
    log_decay = -rate * dt
    ones = triangle(False).astype(F32)
    cums = [jnp.dot(log_decay[:, span_of(c)], ones, precision=HIGH) for c in range(chunks)]
    ends = [lanes(cum[:, CHUNK - 1:]) for cum in cums]
    before, after = jnp.zeros_like(ends[0]), jnp.zeros_like(ends[0])
    for c in range(chunks):
        k.before[c] = jnp.exp(before)
        before = before + ends[c]
        k.after[chunks - c] = jnp.exp(after)
        after = after + ends[chunks - 1 - c]
    k.before[chunks] = jnp.exp(before)
    k.after[0] = jnp.exp(after)
    k.ends[me] = before
    for c in range(chunks):
        k.cum[:, span_of(c)] = cums[c]
        k.reach[:, span_of(c)] = jnp.exp(cums[c])
        k.weight[:, span_of(c)] = jnp.exp(ends[c] - cums[c]) * dt[:, span_of(c)]
        k.step[c] = jnp.exp(ends[c])
    k.dg[...] = jnp.zeros_like(k.dg)

    pl.semaphore_wait(barrier, peers + jnp.where(has_outer, 1, 0))

    def send_end(d):
        return pltpu.make_async_remote_copy(
            src_ref=k.ends.at[me], dst_ref=k.ends.at[me],
            send_sem=k.end_send.at[d], recv_sem=k.end_recv.at[d],
            device_id={"ctx": (me + d) % peers}, device_id_type=MESH)

    def recv_end(d):
        place = (me - d + peers) % peers
        return pltpu.make_async_remote_copy(
            src_ref=k.ends.at[place], dst_ref=k.ends.at[place],
            send_sem=k.end_send.at[d], recv_sem=k.end_recv.at[d],
            device_id={"ctx": place}, device_id_type=MESH)

    for d in range(1, peers):
        send_end(d).start()

    mine = pl.ds(pl.multiple_of(odd * half, half), half)
    theirs = pl.ds(pl.multiple_of((1 - odd) * half, half), half)

    def pair_copy(i, group):
        return pltpu.make_async_remote_copy(
            src_ref=k.total.at[i, group, :, theirs, :], dst_ref=k.pair_in.at[i, group],
            send_sem=k.pair_send.at[i, group], recv_sem=k.pair_recv.at[i, group],
            device_id={"ctx": mate}, device_id_type=MESH)

    def chip_copy(step, group):
        what = jnp.where(chip + step < chips, 0, 1)
        return pltpu.make_async_remote_copy(
            src_ref=k.agg.at[what, group], dst_ref=k.chip_in.at[step, group],
            send_sem=k.chip_send.at[step, group], recv_sem=k.chip_recv.at[step, group],
            device_id={"ctx": (me + 2 * step) % peers}, device_id_type=MESH)

    def back_copy(i, group):
        return pltpu.make_async_remote_copy(
            src_ref=k.give.at[i, group], dst_ref=k.state_in.at[i, group, :, mine, :],
            send_sem=k.back_send.at[i, group], recv_sem=k.back_recv.at[i, group],
            device_id={"ctx": mate}, device_id_type=MESH)

    def back_arrival(i, group):
        return pltpu.make_async_remote_copy(
            src_ref=k.give.at[i, group], dst_ref=k.state_in.at[i, group, :, theirs, :],
            send_sem=k.back_send.at[i, group], recv_sem=k.back_recv.at[i, group],
            device_id={"ctx": mate}, device_id_type=MESH)

    def rows_of(group):
        return pl.ds(pl.multiple_of(group * GROUP, GROUP), GROUP)

    def states(group):
        at_rows = rows_of(group)
        load(0, group).wait()
        load(1, group).wait()
        k.xt[group] = k.x[group].T
        k.gt[group] = k.g[group].T
        value = None
        for c in range(chunks):
            at = span_of(c)
            k.s[group, c] = jnp.zeros((wide, state), F32) if value is None else value
            high, low = split(per_head(k.weight[at_rows, at], k.xt[group, :, at].astype(F32)))
            added = mm(jnp.concatenate([high, low], axis=1), twice(k.b[at, :], 0))
            value = added if value is None else per_head(k.step[c, at_rows], value) + added
        k.total[0, group] = value.reshape(GROUP, size, state)
        value = None
        for c in reversed(range(chunks)):
            at = span_of(c)
            k.r[group, c] = jnp.zeros((wide, state), F32) if value is None else value
            high, low = split(per_head(k.reach[at_rows, at], k.gt[group, :, at].astype(F32)))
            added = mm(jnp.concatenate([high, low], axis=1), twice(k.c[at, :], 0))
            value = added if value is None else per_head(k.step[c, at_rows], value) + added
        k.total[1, group] = value.reshape(GROUP, size, state)

    def make_coefs():
        for d in range(1, peers):
            recv_end(d).wait_recv()
        s_log = jnp.zeros((heads, CHUNK), F32)
        r_log = jnp.zeros((heads, CHUNK), F32)
        for step in range(1, chips):
            k.coef[0, step] = jnp.where(chip >= step, jnp.exp(s_log), 0.0)
            k.coef[1, step] = jnp.where(chip + step < chips, jnp.exp(r_log), 0.0)
            low = (chip - step + chips) % chips
            high = (chip + step) % chips
            s_log = s_log + (k.ends[2 * low] + k.ends[2 * low + 1])
            r_log = r_log + (k.ends[2 * high] + k.ends[2 * high + 1])

    def own_and_mate(group):
        at_rows = rows_of(group)
        return jnp.exp(k.ends[me, at_rows]), jnp.exp(k.ends[mate, at_rows])

    def scaled(coef, block):
        return coef[:, None, :] * block

    def combine(group):
        own_e, mate_e = own_and_mate(group)
        one = jnp.ones_like(own_e)
        pair_copy(0, group).wait_recv()
        k.agg[0, group] = (scaled(jnp.where(is_odd, one, mate_e), k.total[0, group, :, mine, :])
                           + scaled(jnp.where(is_odd, own_e, one), k.pair_in[0, group]))
        pair_copy(1, group).wait_recv()
        k.agg[1, group] = (scaled(jnp.where(is_odd, mate_e, one), k.total[1, group, :, mine, :])
                           + scaled(jnp.where(is_odd, one, own_e), k.pair_in[1, group]))
        for step in range(1, chips):
            chip_copy(step, group).start()

    def finalize(group):
        at_rows = rows_of(group)
        own_e, mate_e = own_and_mate(group)
        one, zero = jnp.ones_like(own_e), jnp.zeros_like(own_e)
        s_pre = jnp.zeros((GROUP, half, state), F32)
        r_pre = jnp.zeros((GROUP, half, state), F32)
        for step in range(1, chips):
            chip_copy(step, group).wait_recv()
            got = k.chip_in[step, group]
            s_pre = s_pre + scaled(k.coef[0, step, at_rows], got)
            r_pre = r_pre + scaled(k.coef[1, chips - step, at_rows], got)
        k.give[0, group] = (scaled(jnp.where(is_odd, one, own_e), s_pre)
                            + scaled(jnp.where(is_odd, zero, one), k.total[0, group, :, mine, :]))
        k.give[1, group] = (scaled(jnp.where(is_odd, own_e, one), r_pre)
                            + scaled(jnp.where(is_odd, one, zero), k.total[1, group, :, mine, :]))
        k.state_in[0, group, :, mine, :] = (scaled(jnp.where(is_odd, mate_e, one), s_pre)
                                            + scaled(jnp.where(is_odd, one, zero), k.pair_in[0, group]))
        back_copy(0, group).start()
        k.state_in[1, group, :, mine, :] = (scaled(jnp.where(is_odd, one, mate_e), r_pre)
                                            + scaled(jnp.where(is_odd, zero, one), k.pair_in[1, group]))
        back_copy(1, group).start()

    def first_step(group, carry):
        states(group)
        pair_copy(0, group).start()
        pair_copy(1, group).start()

        @pl.when(group == 0)
        def _():
            make_coefs()

        @pl.when(group > 0)
        def _():
            combine(group - 1)

        return carry

    lax.fori_loop(0, groups, first_step, 0)
    combine(groups - 1)

    causal = triangle(False)

    def within(group):
        def one_chunk(c, carry):
            at = pl.ds(pl.multiple_of(c * CHUNK, CHUNK), CHUNK)
            scores = mm_nt(k.b[at, :], k.c[at, :])
            cum = k.cum[rows_of(group), at]
            shifted = (cum - jnp.log(k.dt[rows_of(group), at])).T
            total = jnp.zeros((CHUNK, CHUNK), F32)
            rows, cols = [], []
            for pair in range(GROUP // 2):
                x_pair = k.x[group, at, pair * 2 * size:(pair + 1) * 2 * size]
                places = [slice((2 * pair + j) * size, (2 * pair + j + 1) * size) for j in range(2)]
                products = mm(x_pair, pair_blocks(k.gt[group, places[0], at], k.gt[group, places[1], at]))
                for j in range(2):
                    h = 2 * pair + j
                    gap = cum[h:h + 1, :] - shifted[:, h:h + 1]
                    decay = jnp.exp(jnp.where(causal, gap, -1e30))
                    both = products[:, j * CHUNK:(j + 1) * CHUNK] * decay
                    total = total + both
                    rows.append(jnp.sum(both * scores, axis=0, keepdims=True))
                    high, low = split(decay * scores)
                    dx_h = mm_nt(twice(k.gt[group, places[j], at], 1), jnp.concatenate([high, low], axis=1))
                    k.dxt[group, c, places[j], :] = dx_h
                    x_h = k.xt[group, places[j], at]
                    cols.append(jnp.sum(dx_h * x_h.astype(F32), axis=0, keepdims=True))
            k.row[group, c] = jnp.concatenate(rows, axis=0)
            k.col[group, c] = jnp.concatenate(cols, axis=0)
            k.dg[c] += total
            return carry

        lax.fori_loop(0, chunks, one_chunk, 0)

    def second_step(group, carry):
        within(group)

        @pl.when(group > 0)
        def _():
            finalize(group - 1)

        return carry

    lax.fori_loop(0, groups, second_step, 0)
    finalize(groups - 1)

    def inward(c, i, source):
        return pltpu.make_async_remote_copy(
            src_ref=source.at[c, i], dst_ref=k.zin.at[in_slot, c, i],
            send_sem=k.in_send.at[c, i], recv_sem=k.z_recv.at[in_slot, c, i],
            device_id={"head": inner}, device_id_type=MESH)

    def outward(c, i):
        return pltpu.make_async_remote_copy(
            src_ref=k.ztot.at[c, i], dst_ref=k.zin.at[1, c, i],
            send_sem=k.out_send.at[c, i], recv_sem=k.z_recv.at[1, c, i],
            device_id={"head": outer}, device_id_type=MESH)

    def arrival(slot, c, i):
        return pltpu.make_async_remote_copy(
            src_ref=k.ztot.at[c, i], dst_ref=k.zin.at[slot, c, i],
            send_sem=k.out_send.at[c, i], recv_sem=k.z_recv.at[slot, c, i],
            device_id={"head": inner}, device_id_type=MESH)

    def publish(c):
        @pl.when(jnp.logical_not(has_outer))
        def _():
            for i in range(2):
                inward(c, i, k.zown).start()

    def relay(c):
        @pl.when(has_outer)
        def _():
            for i in range(2):
                arrival(0, c, i).wait_recv()
                k.zsum[c, i] = k.zown[c, i] + k.zin[0, c, i]
                inward(c, i, k.zsum).start()

    def settle(c):
        for i in range(2):
            arrival(1, c, i).wait_recv()

            @pl.when(jnp.logical_and(is_mid, has_outer))
            def _():
                k.ztot[c, i] = k.zsum[c, i] + k.zin[1, c, i]

            @pl.when(jnp.logical_and(is_mid, jnp.logical_not(has_outer)))
            def _():
                k.ztot[c, i] = k.zown[c, i] + k.zin[1, c, i]

            @pl.when(jnp.logical_not(is_mid))
            def _():
                k.ztot[c, i] = k.zin[1, c, i]

            @pl.when(has_outer)
            def _():
                outward(c, i).start()

            (k.gb, k.gc)[i][span_of(c), :] = k.ztot[c, i]

    def projections(c):
        at = span_of(c)
        b, cc = k.b[at, :], k.c[at, :]
        high, low = split(k.dg[c])
        k.zown[c, 0] = mm(jnp.concatenate([high, low], axis=1), twice(cc, 0))
        high, low = split(k.dg[c].T)
        k.zown[c, 1] = mm(jnp.concatenate([high, low], axis=1), twice(b, 0))

        def one_group(group, carry):
            if c == 0:
                for i in range(2):
                    back_arrival(i, group).wait_recv()
            at_rows = rows_of(group)
            s_in = k.state_in[0, group].reshape(wide, state)
            r_in = k.state_in[1, group].reshape(wide, state)
            for i, (coef, incoming, local, scale, ref) in enumerate((
                    (k.before[c, at_rows], s_in, k.s, k.reach, k.g),
                    (k.after[c + 1, at_rows], r_in, k.r, k.weight, k.x))):
                high, low = split(per_head(coef, incoming) + local[group, c])
                k.parts[group, c, 2 * i] = high
                k.parts[group, c, 2 * i + 1] = low
                column = scale[at_rows, at].T
                total = jnp.zeros((CHUNK, state), F32)
                for pair in range(GROUP // 2):
                    wide_at = slice(pair * 2 * size, (pair + 1) * 2 * size)
                    one = slice(2 * pair * size, (2 * pair + 1) * size)
                    two = slice((2 * pair + 1) * size, (2 * pair + 2) * size)
                    both = mm(twice(ref[group, at, wide_at], 1),
                              jnp.concatenate([pair_blocks(high[one], high[two]),
                                               pair_blocks(low[one], low[two])], axis=0))
                    for j in range(2):
                        h = 2 * pair + j
                        total = total + both[:, j * state:(j + 1) * state] * column[:, h:h + 1]
                k.zown[c, 1 - i] += total
            return carry

        lax.fori_loop(0, groups, one_group, 0)

    def inputs_step(c):
        at = span_of(c)
        bb, cc = twice(k.b[at, :], 1), twice(k.c[at, :], 1)

        def one_group(group, carry):
            at_rows = rows_of(group)
            weight, reach = k.weight[at_rows, at], k.reach[at_rows, at]
            xt, gt = k.xt[group, :, at].astype(F32), k.gt[group, :, at].astype(F32)
            parts = [k.parts[group, c, i] for i in range(4)]
            y = mm_nt(jnp.concatenate(parts[:2], axis=1), cc)
            k.row[group, c] += head_sums(y * gt, GROUP) * reach
            dx = per_head(weight, mm_nt(jnp.concatenate(parts[2:], axis=1), bb))
            k.col[group, c] += head_sums(dx * xt, GROUP)
            product = head_sums(xt * gt, GROUP)
            k.cross[group] = product if c == 0 else k.cross[group] + product
            skip = lanes(column_of(k.skip[...]))
            k.params[...] = skip
            dx = dx + k.dxt[group, c] + per_head(k.params[at_rows], gt)
            k.gx[group, c] = dx.astype(BF16).T
            gx_copy(group, c).start()
            return carry

        lax.fori_loop(0, groups, one_group, 0)

    def gx_copy(group, c):
        at = pl.ds(pl.multiple_of(group * wide, wide), wide)
        return pltpu.make_async_copy(k.gx.at[group, c], k.gx_hbm.at[span_of(c), at], k.gx_sem.at[group, c])

    for c in range(chunks):
        projections(c)
        publish(c)
    for c in range(chunks):
        inputs_step(c)
        relay(c)
        if c > 0:
            settle(c - 1)

    beyond = []
    for group in range(groups):
        at_rows = rows_of(group)
        last = k.total[0, group].reshape(wide, state) + per_head(
            k.before[chunks, at_rows], k.state_in[0, group].reshape(wide, state))
        beyond.append(jnp.sum(head_sums(last * k.state_in[1, group].reshape(wide, state), GROUP),
                              axis=1, keepdims=True))
    beyond = lanes(jnp.concatenate(beyond, axis=0))
    suffix = triangle(True).astype(F32)
    bias = column_of(k.bias[...])
    g_rate = jnp.zeros((heads, 1), F32)
    g_bias = jnp.zeros((heads, 1), F32)
    for c in reversed(range(chunks)):
        at = span_of(c)
        row = jnp.concatenate([k.row[group, c] for group in range(groups)], axis=0)
        col = jnp.concatenate([k.col[group, c] for group in range(groups)], axis=0)
        change = row - col
        d_log = jnp.dot(change, suffix, precision=HIGH) + beyond
        beyond = beyond + lanes(jnp.sum(change, axis=1, keepdims=True))
        dt = k.dt[:, at]
        g_dt = col / dt - rate * d_log
        g_raw = g_dt / (1.0 + jnp.exp(-(k.raw[:, at] + bias)))
        k.graw[:, at] = g_raw
        g_rate = g_rate - jnp.sum(dt * d_log, axis=1, keepdims=True)
        g_bias = g_bias + jnp.sum(g_raw, axis=1, keepdims=True)
    cross = jnp.concatenate([k.cross[group] for group in range(groups)], axis=0)
    g_skip = jnp.sum(cross, axis=1, keepdims=True)
    lane = lax.broadcasted_iota(jnp.int32, (heads, CHUNK), 1)
    k.params_in[me] = jnp.where(lane == 0, g_rate, jnp.where(lane == 1, g_skip, g_bias))

    def send_params(d):
        return pltpu.make_async_remote_copy(
            src_ref=k.params_in.at[me], dst_ref=k.params_in.at[me],
            send_sem=k.param_send.at[d], recv_sem=k.param_recv.at[d],
            device_id={"ctx": (me + d) % peers}, device_id_type=MESH)

    def recv_params(d):
        place = (me - d + peers) % peers
        return pltpu.make_async_remote_copy(
            src_ref=k.params_in.at[place], dst_ref=k.params_in.at[place],
            send_sem=k.param_send.at[d], recv_sem=k.param_recv.at[d],
            device_id={"ctx": place}, device_id_type=MESH)

    for d in range(1, peers):
        send_params(d).start()
    settle(chunks - 1)
    for d in range(1, peers):
        recv_params(d).wait_recv()
    total = k.params_in[0]
    for d in range(1, peers):
        total = total + k.params_in[d]
    k.grate[...] = row_of(total[:, 0:1])
    k.gskip[...] = row_of(total[:, 1:2])
    k.gbias[...] = row_of(total[:, 2:3])

    for group in range(groups):
        for c in range(chunks):
            gx_copy(group, c).wait()
        for i in range(2):
            pair_copy(i, group).wait_send()
            back_copy(i, group).wait_send()
        for step in range(1, chips):
            chip_copy(step, group).wait_send()
    for c in range(chunks):
        for i in range(2):
            inward(c, i, k.zsum).wait_send()

            @pl.when(has_outer)
            def _():
                outward(c, i).wait_send()
    for d in range(1, peers):
        send_end(d).wait_send()
        send_params(d).wait_send()


def on_device(peers, line, tokens_x, raw_dt, in_b, in_c, decay_rate, skip_gain, step_bias, grad_y):
    heads, tokens = raw_dt.shape
    width = tokens_x.shape[1]
    size = width // heads
    state = in_b.shape[1]
    scratch = scratch_of(heads, tokens, size, state, peers)
    names = inputs_and_outputs() + tuple(scratch)

    def shape(*dims, dtype=F32):
        return jax.ShapeDtypeStruct(dims, dtype)

    hbm, vmem = pl.BlockSpec(memory_space=pl.ANY), pl.BlockSpec(memory_space=pltpu.VMEM)
    gx, graw, gb, gc, grate, gskip, gbias = pl.pallas_call(
        functools.partial(kernel, names, peers, line),
        in_specs=[hbm, hbm] + [vmem] * 6,
        out_specs=[hbm] + [vmem] * 6,
        out_shape=[shape(tokens, width, dtype=BF16), shape(heads, tokens), shape(tokens, state),
                   shape(tokens, state), shape(1, heads), shape(1, heads), shape(1, heads)],
        scratch_shapes=list(scratch.values()),
        compiler_params=pltpu.CompilerParams(
            collective_id=0, has_side_effects=True, vmem_limit_bytes=60 << 20),
        name="layer",
    )(tokens_x, grad_y, raw_dt, step_bias[None], decay_rate[None], skip_gain[None], in_b, in_c)
    return gx, graw, gb, gc, grate[0], gskip[0], gbias[0]


def solution(mesh):
    return jax.shard_map(
        functools.partial(on_device, mesh.shape["ctx"], mesh.shape["head"]),
        mesh=mesh,
        in_specs=(
            P("ctx", "head"),
            P("head", "ctx"),
            P("ctx", None),
            P("ctx", None),
            P("head"),
            P("head"),
            P("head"),
            P("ctx", "head"),
        ),
        out_specs=(
            P("ctx", "head"),
            P("head", "ctx"),
            P("ctx", None),
            P("ctx", None),
            P("head"),
            P("head"),
            P("head"),
        ),
        check_vma=False,
    )
```

```python
import functools
import types

import jax
import jax.numpy as jnp
from jax import lax
from jax.experimental import pallas as pl
from jax.experimental.pallas import tpu as pltpu
from jax.sharding import PartitionSpec as P

CHUNK = 128
GROUP = 8
F32 = jnp.float32
BF16 = jnp.bfloat16
HIGH = lax.Precision.HIGHEST
NT = (((1,), (1,)), ((), ()))
MESH = pl.DeviceIdType.MESH
VMEM_LIMIT = 50 << 20


def mm(a, b):
    return jnp.dot(a, b, preferred_element_type=F32)


def mm_nt(a, b):
    return lax.dot_general(a, b, NT, preferred_element_type=F32)


def split(a):
    high = a.astype(BF16)
    return high, (a - high.astype(F32)).astype(BF16)


def twice(a, axis):
    return jnp.concatenate([a, a], axis=axis)


def softplus(v):
    return jnp.maximum(v, 0.0) + jnp.log1p(jnp.exp(-jnp.abs(v)))


def lanes(column, width=CHUNK):
    return jnp.broadcast_to(column, (column.shape[0], width))


def per_head(rows, matrix):
    heads = rows.shape[0]
    shaped = matrix.reshape(heads, matrix.shape[0] // heads, matrix.shape[1])
    return (shaped * rows[:, None, :]).reshape(matrix.shape)


def head_sums(matrix, heads):
    return jnp.sum(matrix.reshape(heads, matrix.shape[0] // heads, matrix.shape[1]), axis=1)


def pair_blocks(first, second):
    zero = jnp.zeros_like(first)
    return jnp.concatenate(
        [jnp.concatenate([first, zero], axis=1), jnp.concatenate([zero, second], axis=1)], axis=0
    )


def triangle(lower):
    row = lax.broadcasted_iota(jnp.int32, (CHUNK, CHUNK), 0)
    col = lax.broadcasted_iota(jnp.int32, (CHUNK, CHUNK), 1)
    return (row >= col) if lower else (row <= col)


def eye(n):
    row = lax.broadcasted_iota(jnp.int32, (n, n), 0)
    col = lax.broadcasted_iota(jnp.int32, (n, n), 1)
    return row == col


def column_of(row):
    n = row.shape[1]
    return jnp.sum(jnp.where(eye(n), jnp.broadcast_to(row, (n, n)), 0.0), axis=1, keepdims=True)


def row_of(column):
    n = column.shape[0]
    return jnp.sum(jnp.where(eye(n), jnp.broadcast_to(column, (n, n)), 0.0), axis=0, keepdims=True)


def span_of(c):
    return slice(c * CHUNK, (c + 1) * CHUNK)


def inputs_and_outputs():
    return ("x_hbm", "g_hbm", "raw", "bias", "rate", "skip", "b", "c",
            "gx", "graw", "ztot", "grate", "gskip", "gbias")


def scratch_of(heads, tokens, size, state, peers):
    groups, chunks, chips = heads // GROUP, tokens // CHUNK, peers // 2
    wide, half = GROUP * size, size // 2
    vmem = pltpu.VMEM
    dma = pltpu.SemaphoreType.DMA
    halves = (2, groups, GROUP, half, state)
    segments = (2, chunks, CHUNK, state)
    return dict(
        src=vmem((2, groups, tokens, wide), BF16),
        xt=vmem((groups, wide, tokens), BF16),
        gt=vmem((groups, wide, tokens), BF16),
        dt=vmem((heads, tokens), F32),
        cum=vmem((heads, tokens), F32),
        scale=vmem((2, heads, tokens), F32),
        step=vmem((chunks, heads, CHUNK), F32),
        edge=vmem((2, chunks, heads, CHUNK), F32),
        whole=vmem((heads, CHUNK), F32),
        skips=vmem((heads, CHUNK), F32),
        local=vmem((2, groups, chunks, wide, state), F32),
        total=vmem((2, groups, GROUP, size, state), F32),
        ends=vmem((peers, heads, CHUNK), F32),
        coef=vmem((2, chips, heads, CHUNK), F32),
        pair_in=vmem(halves, F32),
        agg=vmem(halves, F32),
        chip_in=vmem((chips,) + halves[1:], F32),
        pre=vmem(halves, F32),
        give=vmem(halves, F32),
        state_in=vmem((2, groups, GROUP, size, state), F32),
        dxt=vmem((groups, chunks, wide, CHUNK), F32),
        row=vmem((groups, chunks, GROUP, CHUNK), F32),
        col=vmem((groups, chunks, GROUP, CHUNK), F32),
        cross=vmem((groups, GROUP, CHUNK), F32),
        dg=vmem((chunks, CHUNK, CHUNK), F32),
        parts=vmem((2, groups, chunks, 2, wide, state), BF16),
        zown=vmem(segments, F32),
        zsum=vmem(segments, F32),
        zin=vmem((2,) + segments, F32),
        params_in=vmem((peers, heads, CHUNK), F32),
        load_sem=dma((2, groups)),
        end_send=dma((peers,)),
        end_recv=dma((peers,)),
        pair_send=dma((2, groups)),
        pair_recv=dma((2, groups)),
        chip_send=dma((chips, groups)),
        chip_recv=dma((chips, groups)),
        back_send=dma((2, groups)),
        back_recv=dma((2, groups)),
        in_send=dma((2, chunks)),
        out_send=dma((2, chunks)),
        z_recv=dma((2, 2, chunks)),
        param_send=dma((peers,)),
        param_recv=dma((peers,)),
    )


def kernel(names, peers, line, *refs):
    k = types.SimpleNamespace(**dict(zip(names, refs)))
    heads, tokens = k.raw.shape
    state = k.b.shape[1]
    groups, chunks, chips = heads // GROUP, tokens // CHUNK, peers // 2
    wide = k.src.shape[3]
    size = wide // GROUP
    half = size // 2
    me, zpos = lax.axis_index("ctx"), lax.axis_index("head")
    odd, chip = me % 2, me // 2
    mate = me + 1 - 2 * odd
    early = jnp.where(chip < chips // 2, 0, 1)
    late = 1 - early

    left = zpos < line // 2
    inner = jnp.where(left, zpos + 1, zpos - 1)
    outer = jnp.where(left, zpos - 1, zpos + 1)
    has_outer = jnp.logical_and(zpos > 0, zpos < line - 1)
    is_mid = jnp.logical_or(zpos == line // 2 - 1, zpos == line // 2)
    in_slot = jnp.where(is_mid, 1, 0)

    barrier = pltpu.get_barrier_semaphore()

    def remote(src, dst, send, recv, **place):
        return pltpu.make_async_remote_copy(
            src_ref=src, dst_ref=dst, send_sem=send, recv_sem=recv,
            device_id=place, device_id_type=MESH)

    def greet():
        for d in range(1, peers):
            pl.semaphore_signal(barrier, inc=1, device_id={"ctx": (me + d) % peers}, device_id_type=MESH)
        pl.semaphore_signal(barrier, inc=1, device_id={"head": inner}, device_id_type=MESH)

        @pl.when(has_outer)
        def _():
            pl.semaphore_signal(barrier, inc=1, device_id={"head": outer}, device_id_type=MESH)

    def met():
        pl.semaphore_wait(barrier, peers + jnp.where(has_outer, 1, 0))

    def load(e, group):
        at = pl.ds(pl.multiple_of(group * wide, wide), wide)
        return pltpu.make_async_copy((k.g_hbm, k.x_hbm)[e].at[:, at], k.src.at[e, group], k.load_sem.at[e, group])

    def start_loads():
        for group in range(groups):
            load(1, group).start()
            load(0, group).start()

    def prepare():
        dt = softplus(k.raw[...] + column_of(k.bias[...]))
        k.dt[...] = dt
        log_decay = -column_of(k.rate[...]) * dt
        ones = triangle(False).astype(F32)
        cums = [jnp.dot(log_decay[:, span_of(c)], ones, precision=HIGH) for c in range(chunks)]
        ends = [lanes(cum[:, CHUNK - 1:]) for cum in cums]
        before, after = jnp.zeros_like(ends[0]), jnp.zeros_like(ends[0])
        for c in range(chunks):
            k.edge[0, c] = jnp.exp(before)
            before = before + ends[c]
            k.edge[1, chunks - 1 - c] = jnp.exp(after)
            after = after + ends[chunks - 1 - c]
        k.whole[...] = jnp.exp(before)
        k.ends[me] = before
        for c in range(chunks):
            k.cum[:, span_of(c)] = cums[c]
            k.scale[0, :, span_of(c)] = jnp.exp(cums[c])
            k.scale[1, :, span_of(c)] = jnp.exp(ends[c] - cums[c]) * dt[:, span_of(c)]
            k.step[c] = jnp.exp(ends[c])
        k.dg[...] = jnp.zeros_like(k.dg)
        k.skips[...] = lanes(column_of(k.skip[...]))

    def end_copy(d, place):
        return remote(k.ends.at[place], k.ends.at[place], k.end_send.at[d], k.end_recv.at[d],
                      ctx=(me + d) % peers)

    def send_ends():
        for d in range(1, peers):
            end_copy(d, me).start()

    mine = pl.ds(pl.multiple_of(odd * half, half), half)
    theirs = pl.ds(pl.multiple_of((1 - odd) * half, half), half)

    def pair_copy(e, group):
        return remote(k.total.at[e, group, :, theirs, :], k.pair_in.at[e, group],
                      k.pair_send.at[e, group], k.pair_recv.at[e, group], ctx=mate)

    def chip_copy(step, group):
        what = jnp.where(chip + step < chips, 0, 1)
        return remote(k.agg.at[what, group], k.chip_in.at[step, group],
                      k.chip_send.at[step, group], k.chip_recv.at[step, group], ctx=(me + 2 * step) % peers)

    def back_copy(e, group, rows):
        return remote(k.give.at[e, group], k.state_in.at[e, group, :, rows, :],
                      k.back_send.at[e, group], k.back_recv.at[e, group], ctx=mate)

    def rows_of(group):
        return pl.ds(pl.multiple_of(group * GROUP, GROUP), GROUP)

    def carry_local(e, group, order, source, operand):
        at_rows = rows_of(group)
        value = None
        for c in order:
            at = span_of(c)
            k.local[e, group, c] = jnp.zeros((wide, state), F32) if value is None else value
            high, low = split(per_head(k.scale[1 - e, at_rows, at], source[group, :, at].astype(F32)))
            added = mm(jnp.concatenate([high, low], axis=1), twice(operand[at, :], 0))
            value = added if value is None else per_head(k.step[c, at_rows], value) + added
        k.total[e, group] = value.reshape(GROUP, size, state)

    def states(group):
        load(1, group).wait()
        k.xt[group] = k.src[1, group].T
        carry_local(0, group, range(chunks), k.xt, k.b)

    def backs(group):
        load(0, group).wait()
        k.gt[group] = k.src[0, group].T
        carry_local(1, group, reversed(range(chunks)), k.gt, k.c)

    def make_coefs():
        for d in range(1, peers):
            @pl.when(d != mate_step)
            def _():
                end_copy(d, (me - d + peers) % peers).wait_recv()
        s_log = jnp.zeros((heads, CHUNK), F32)
        r_log = jnp.zeros((heads, CHUNK), F32)
        for step in range(1, chips):
            k.coef[0, step] = jnp.exp(s_log)
            k.coef[1, step] = jnp.exp(r_log)
            low = (chip - step + chips) % chips
            high = (chip + step) % chips
            s_log = s_log + (k.ends[2 * low] + k.ends[2 * low + 1])
            r_log = r_log + (k.ends[2 * high] + k.ends[2 * high + 1])

    def scaled(coef, block):
        return coef[:, None, :] * block

    def downstream(e):
        return jnp.where(e == 0, odd, 1 - odd) == 1

    def own_and_mate(group):
        at_rows = rows_of(group)
        own = jnp.exp(k.ends[me, at_rows])
        return own, jnp.exp(k.ends[mate, at_rows]), jnp.ones_like(own), jnp.zeros_like(own)

    def combine(group):
        @pl.when(group == 0)
        def _():
            end_copy(mate_step, mate).wait_recv()

        own_e, mate_e, one, _ = own_and_mate(group)
        for e in range(2):
            down = downstream(e)
            pair_copy(e, group).wait_recv()
            k.agg[e, group] = (scaled(jnp.where(down, one, mate_e), k.total[e, group, :, mine, :])
                               + scaled(jnp.where(down, own_e, one), k.pair_in[e, group]))

    def finalize(e, group):
        at_rows = rows_of(group)
        k.pre[e, group] = jnp.zeros((GROUP, half, state), F32)
        for step in range(1, chips):
            slot = jnp.where(e == 0, step, chips - step)

            @pl.when(jnp.where(e == 0, chip, chips - 1 - chip) >= step)
            def _():
                chip_copy(slot, group).wait_recv()
                k.pre[e, group] += scaled(k.coef[e, step, at_rows], k.chip_in[slot, group])

        own_e, mate_e, one, zero = own_and_mate(group)
        down = downstream(e)
        pre = k.pre[e, group]
        k.give[e, group] = (scaled(jnp.where(down, one, own_e), pre)
                            + scaled(jnp.where(down, zero, one), k.total[e, group, :, mine, :]))
        k.state_in[e, group, :, mine, :] = (scaled(jnp.where(down, mate_e, one), pre)
                                            + scaled(jnp.where(down, one, zero), k.pair_in[e, group]))
        back_copy(e, group, mine).start()

    causal = triangle(False)

    def within(group):
        def one_chunk(c, carry):
            at = pl.ds(pl.multiple_of(c * CHUNK, CHUNK), CHUNK)
            scores = mm_nt(k.b[at, :], k.c[at, :])
            cum = k.cum[rows_of(group), at]
            shifted = (cum - jnp.log(k.dt[rows_of(group), at])).T
            total = jnp.zeros((CHUNK, CHUNK), F32)
            rows, cols = [], []
            for pair in range(GROUP // 2):
                x_pair = k.src[1, group, at, pair * 2 * size:(pair + 1) * 2 * size]
                places = [slice((2 * pair + j) * size, (2 * pair + j + 1) * size) for j in range(2)]
                products = mm(x_pair, pair_blocks(k.gt[group, places[0], at], k.gt[group, places[1], at]))
                for j in range(2):
                    h = 2 * pair + j
                    gap = cum[h:h + 1, :] - shifted[:, h:h + 1]
                    decay = jnp.exp(jnp.where(causal, gap, -1e30))
                    both = products[:, j * CHUNK:(j + 1) * CHUNK] * decay
                    total = total + both
                    rows.append(jnp.sum(both * scores, axis=0, keepdims=True))
                    high, low = split(decay * scores)
                    dx_h = mm_nt(twice(k.gt[group, places[j], at], 1), jnp.concatenate([high, low], axis=1))
                    k.dxt[group, c, places[j], :] = dx_h
                    x_h = k.xt[group, places[j], at]
                    cols.append(jnp.sum(dx_h * x_h.astype(F32), axis=0, keepdims=True))
            k.row[group, c] = jnp.concatenate(rows, axis=0)
            k.col[group, c] = jnp.concatenate(cols, axis=0)
            k.dg[c] += total
            return carry

        lax.fori_loop(0, chunks, one_chunk, 0)

    def score_parts():
        for c in range(chunks):
            at = span_of(c)
            for e, dg, operand in ((0, k.dg[c].T, k.b), (1, k.dg[c], k.c)):
                high, low = split(dg)
                k.zown[e, c] = mm(jnp.concatenate([high, low], axis=1), twice(operand[at, :], 0))

    def projections(e, c):
        at = span_of(c)
        total = k.zown[e, c]
        for group in range(groups):
            if c == 0:
                back_copy(e, group, theirs).wait_recv()
            at_rows = rows_of(group)
            incoming = k.state_in[e, group].reshape(wide, state)
            high, low = split(per_head(k.edge[e, c, at_rows], incoming) + k.local[e, group, c])
            k.parts[e, group, c, 0] = high
            k.parts[e, group, c, 1] = low
            column = k.scale[e, at_rows, at].T
            for pair in range(GROUP // 2):
                wide_at = slice(pair * 2 * size, (pair + 1) * 2 * size)
                one = slice(2 * pair * size, (2 * pair + 1) * size)
                two = slice((2 * pair + 1) * size, (2 * pair + 2) * size)
                both = mm(twice(k.src[e, group, at, wide_at], 1),
                          jnp.concatenate([pair_blocks(high[one], high[two]),
                                           pair_blocks(low[one], low[two])], axis=0))
                for j in range(2):
                    h = 2 * pair + j
                    total = total + both[:, j * state:(j + 1) * state] * column[:, h:h + 1]
        k.zown[e, c] = total

    def inward(e, c, source):
        return remote(source.at[e, c], k.zin.at[in_slot, e, c],
                      k.in_send.at[e, c], k.z_recv.at[in_slot, e, c], head=inner)

    def outward(e, c, slot=1):
        return remote(k.ztot.at[e, c], k.zin.at[slot, e, c],
                      k.out_send.at[e, c], k.z_recv.at[slot, e, c], head=outer)

    def publish(e, c):
        @pl.when(jnp.logical_not(has_outer))
        def _():
            inward(e, c, k.zown).start()

    def relay(e, c):
        @pl.when(has_outer)
        def _():
            outward(e, c, 0).wait_recv()
            k.zsum[e, c] = k.zown[e, c] + k.zin[0, e, c]
            inward(e, c, k.zsum).start()

    def settle(e, c):
        outward(e, c).wait_recv()

        @pl.when(jnp.logical_and(is_mid, has_outer))
        def _():
            k.ztot[e, c] = k.zsum[e, c] + k.zin[1, e, c]

        @pl.when(jnp.logical_and(is_mid, jnp.logical_not(has_outer)))
        def _():
            k.ztot[e, c] = k.zown[e, c] + k.zin[1, e, c]

        @pl.when(jnp.logical_not(is_mid))
        def _():
            k.ztot[e, c] = k.zin[1, e, c]

        @pl.when(has_outer)
        def _():
            outward(e, c).start()

    def settle_mid(e, c):
        @pl.when(is_mid)
        def _():
            settle(e, c)

    def settle_rest(e, c):
        @pl.when(jnp.logical_not(is_mid))
        def _():
            settle(e, c)

    def inputs_step(c, group):
        at, at_rows = span_of(c), rows_of(group)
        bb, cc = twice(k.b[at, :], 1), twice(k.c[at, :], 1)
        reach, weight = k.scale[0, at_rows, at], k.scale[1, at_rows, at]
        xt, gt = k.xt[group, :, at].astype(F32), k.gt[group, :, at].astype(F32)
        parts = [jnp.concatenate([k.parts[e, group, c, 0], k.parts[e, group, c, 1]], axis=1) for e in range(2)]
        y = mm_nt(parts[0], cc)
        k.row[group, c] += head_sums(y * gt, GROUP) * reach
        dx = per_head(weight, mm_nt(parts[1], bb))
        k.col[group, c] += head_sums(dx * xt, GROUP)
        product = head_sums(xt * gt, GROUP)
        k.cross[group] = product if c == 0 else k.cross[group] + product
        dx = dx + k.dxt[group, c] + per_head(k.skips[at_rows], gt)
        k.gx[group, c] = dx.astype(BF16).T

    def step_sizes():
        rate, bias = column_of(k.rate[...]), column_of(k.bias[...])
        beyond = []
        for group in range(groups):
            last = k.total[0, group] + scaled(k.whole[rows_of(group)], k.state_in[0, group])
            sums = jnp.sum(last * k.state_in[1, group], axis=1)
            beyond.append(jnp.sum(sums, axis=1, keepdims=True))
        beyond = lanes(jnp.concatenate(beyond, axis=0))
        suffix = triangle(True).astype(F32)
        g_rate = jnp.zeros((heads, 1), F32)
        g_bias = jnp.zeros((heads, 1), F32)
        for c in reversed(range(chunks)):
            at = span_of(c)
            row = jnp.concatenate([k.row[group, c] for group in range(groups)], axis=0)
            col = jnp.concatenate([k.col[group, c] for group in range(groups)], axis=0)
            change = row - col
            d_log = jnp.dot(change, suffix, precision=HIGH) + beyond
            beyond = beyond + lanes(jnp.sum(change, axis=1, keepdims=True))
            dt = k.dt[:, at]
            g_dt = col / dt - rate * d_log
            g_raw = g_dt / (1.0 + jnp.exp(-(k.raw[:, at] + bias)))
            k.graw[:, at] = g_raw
            g_rate = g_rate - jnp.sum(dt * d_log, axis=1, keepdims=True)
            g_bias = g_bias + jnp.sum(g_raw, axis=1, keepdims=True)
        cross = jnp.concatenate([k.cross[group] for group in range(groups)], axis=0)
        g_skip = jnp.sum(cross, axis=1, keepdims=True)
        lane = lax.broadcasted_iota(jnp.int32, (heads, CHUNK), 1)
        k.params_in[me] = jnp.where(lane == 0, g_rate, jnp.where(lane == 1, g_skip, g_bias))

    def params_copy(d, place):
        return remote(k.params_in.at[place], k.params_in.at[place], k.param_send.at[d], k.param_recv.at[d],
                      ctx=(me + d) % peers)

    def gather_params():
        for d in range(1, peers):
            params_copy(d, (me - d + peers) % peers).wait_recv()
        total = k.params_in[0]
        for d in range(1, peers):
            total = total + k.params_in[d]
        k.grate[...] = row_of(total[:, 0:1])
        k.gskip[...] = row_of(total[:, 1:2])
        k.gbias[...] = row_of(total[:, 2:3])

    mate_step = jnp.where(odd == 1, 1, peers - 1)

    def nth_step(n):
        return jnp.where(chip < chips // 2, n, chips - n)

    def exchange(group):
        combine(group)
        for n in range(1, min(3, chips)):
            chip_copy(nth_step(n), group).start()

    def first_step(group, carry):
        states(group)
        pair_copy(0, group).start()
        backs(group)
        pair_copy(1, group).start()

        @pl.when(group > 0)
        def _():
            exchange(group - 1)

        return carry

    greet()
    start_loads()
    prepare()
    met()
    send_ends()
    lax.fori_loop(0, groups, first_step, 0)

    done = 0
    for group in range(groups):
        within(group)
        if group == 0:
            exchange(groups - 1)
            for n in range(3, chips):
                lax.fori_loop(0, groups, lambda group, carry: (chip_copy(nth_step(n), group).start(), carry)[1], 0)
            make_coefs()
        if group >= 1 or groups == 1:
            while done < min(group + 1, groups) and (group == groups - 1 or done < group):
                finalize(early, done)
                done += 1
    score_parts()

    pieces = [(e, c) for e in (early, late) for c in range(chunks)]
    relayed, settled = 0, 0

    def tend(relays, settles):
        nonlocal relayed, settled
        while relayed < min(relays, len(pieces)):
            relay(*pieces[relayed])
            relayed += 1
        while settled < min(settles, relayed):
            settle_mid(*pieces[settled])
            settled += 1

    for c in range(chunks):
        projections(early, c)
        publish(early, c)
    for group in range(groups):
        finalize(late, group)
        tend(min(group, 3), 0)
    for c in range(chunks):
        projections(late, c)
        publish(late, c)
        tend(chunks, (1, 2, 3, 4)[min(c, 3)])
    turns = [(c, group) for c in range(chunks) for group in range(groups)]
    for j, turn in enumerate(turns):
        inputs_step(*turn)
        part = 16 * (j + 1) // len(turns)
        tend(chunks + sum(part >= at for at in (2, 6, 10, 13)), chunks + sum(part >= at for at in (10, 14)))
    tend(len(pieces), 0)
    step_sizes()
    for d in range(1, peers):
        params_copy(d, me).start()
    tend(len(pieces), len(pieces))
    for piece in pieces:
        settle_rest(*piece)
    gather_params()

    def drain():
        for group in range(groups):
            for e in range(2):
                pair_copy(e, group).wait_send()
                back_copy(e, group, mine).wait_send()
            for step in range(1, chips):
                chip_copy(step, group).wait_send()
        for c in range(chunks):
            for e in range(2):
                inward(e, c, k.zsum).wait_send()

                @pl.when(has_outer)
                def _():
                    outward(e, c).wait_send()
        for d in range(1, peers):
            end_copy(d, me).wait_send()
            params_copy(d, me).wait_send()

    drain()


def finish_kernel(groups, chunks, gx, graw, ztot, grate, gskip, gbias,
                  gx_out, graw_out, gb_out, gc_out, grate_out, gskip_out, gbias_out, sems):
    wide = gx.shape[3]
    copies = [(gx.at[group, c], gx_out.at[span_of(c), group * wide:(group + 1) * wide])
              for group in range(groups) for c in range(chunks)]
    copies += [(ztot.at[1 - i, c], ref.at[span_of(c), :]) for i, ref in enumerate((gb_out, gc_out))
               for c in range(chunks)]
    copies += [(graw, graw_out), (grate, grate_out), (gskip, gskip_out), (gbias, gbias_out)]
    copies = [pltpu.make_async_copy(src, dst, sems.at[i]) for i, (src, dst) in enumerate(copies)]
    for copy in copies:
        copy.start()
    for copy in copies:
        copy.wait()


def on_device(peers, line, tokens_x, raw_dt, in_b, in_c, decay_rate, skip_gain, step_bias, grad_y):
    heads, tokens = raw_dt.shape
    width = tokens_x.shape[1]
    size = width // heads
    state = in_b.shape[1]
    groups, chunks = heads // GROUP, tokens // CHUNK
    scratch = scratch_of(heads, tokens, size, state, peers)
    names = inputs_and_outputs() + tuple(scratch)

    def shape(*dims, dtype=F32):
        return jax.ShapeDtypeStruct(dims, dtype)

    hbm, vmem = pl.BlockSpec(memory_space=pl.ANY), pl.BlockSpec(memory_space=pltpu.VMEM)
    row = shape(1, heads)
    results = pl.pallas_call(
        functools.partial(kernel, names, peers, line),
        in_specs=[hbm, hbm] + [vmem] * 6,
        out_specs=[vmem] * 6,
        out_shape=[shape(groups, chunks, CHUNK, GROUP * size, dtype=BF16), shape(heads, tokens),
                   shape(2, chunks, CHUNK, state), row, row, row],
        scratch_shapes=list(scratch.values()),
        compiler_params=pltpu.CompilerParams(
            collective_id=0, has_side_effects=True, vmem_limit_bytes=VMEM_LIMIT),
        name="layer",
    )(tokens_x, grad_y, raw_dt, step_bias[None], decay_rate[None], skip_gain[None], in_b, in_c)
    gx, graw, gb, gc, grate, gskip, gbias = pl.pallas_call(
        functools.partial(finish_kernel, groups, chunks),
        in_specs=[vmem] * 6,
        out_specs=[hbm] * 7,
        out_shape=[shape(tokens, width, dtype=BF16), shape(heads, tokens), shape(tokens, state),
                   shape(tokens, state), row, row, row],
        scratch_shapes=[pltpu.SemaphoreType.DMA((groups * chunks + 2 * chunks + 4,))],
        compiler_params=pltpu.CompilerParams(vmem_limit_bytes=4 << 20),
        name="finish",
    )(*results)
    return gx, graw, gb, gc, grate[0], gskip[0], gbias[0]


def solution(mesh):
    return jax.shard_map(
        functools.partial(on_device, mesh.shape["ctx"], mesh.shape["head"]),
        mesh=mesh,
        in_specs=(
            P("ctx", "head"),
            P("head", "ctx"),
            P("ctx", None),
            P("ctx", None),
            P("head"),
            P("head"),
            P("head"),
            P("ctx", "head"),
        ),
        out_specs=(
            P("ctx", "head"),
            P("head", "ctx"),
            P("ctx", None),
            P("ctx", None),
            P("head"),
            P("head"),
            P("head"),
        ),
        check_vma=False,
    )
```

```python
import functools
import types

import jax
import jax.numpy as jnp
from jax import lax
from jax.experimental import pallas as pl
from jax.experimental.pallas import tpu as pltpu
from jax.sharding import PartitionSpec as P

CHUNK = 128
GROUP = 8
F32 = jnp.float32
BF16 = jnp.bfloat16
HIGH = lax.Precision.HIGHEST
NT = (((1,), (1,)), ((), ()))
MESH = pl.DeviceIdType.MESH
VMEM_LIMIT = 50 << 20


def mm(a, b):
    return jnp.dot(a, b, preferred_element_type=F32)


def mm_nt(a, b):
    return lax.dot_general(a, b, NT, preferred_element_type=F32)


def split(a):
    high = a.astype(BF16)
    return high, (a - high.astype(F32)).astype(BF16)


def twice(a, axis):
    return jnp.concatenate([a, a], axis=axis)


def softplus(v):
    return jnp.maximum(v, 0.0) + jnp.log1p(jnp.exp(-jnp.abs(v)))


def lanes(column, width=CHUNK):
    return jnp.broadcast_to(column, (column.shape[0], width))


def per_head(rows, matrix):
    heads = rows.shape[0]
    shaped = matrix.reshape(heads, matrix.shape[0] // heads, matrix.shape[1])
    return (shaped * rows[:, None, :]).reshape(matrix.shape)


def head_sums(matrix, heads):
    return jnp.sum(matrix.reshape(heads, matrix.shape[0] // heads, matrix.shape[1]), axis=1)


def pair_blocks(first, second):
    zero = jnp.zeros_like(first)
    return jnp.concatenate(
        [jnp.concatenate([first, zero], axis=1), jnp.concatenate([zero, second], axis=1)], axis=0
    )


def triangle(lower):
    row = lax.broadcasted_iota(jnp.int32, (CHUNK, CHUNK), 0)
    col = lax.broadcasted_iota(jnp.int32, (CHUNK, CHUNK), 1)
    return (row >= col) if lower else (row <= col)


def eye(n):
    row = lax.broadcasted_iota(jnp.int32, (n, n), 0)
    col = lax.broadcasted_iota(jnp.int32, (n, n), 1)
    return row == col


def column_of(row):
    n = row.shape[1]
    return jnp.sum(jnp.where(eye(n), jnp.broadcast_to(row, (n, n)), 0.0), axis=1, keepdims=True)


def row_of(column):
    n = column.shape[0]
    return jnp.sum(jnp.where(eye(n), jnp.broadcast_to(column, (n, n)), 0.0), axis=0, keepdims=True)


def span_of(c):
    return slice(c * CHUNK, (c + 1) * CHUNK)


def inputs_and_outputs():
    return ("x_hbm", "g_hbm", "raw_hbm", "bias_hbm", "rate_hbm", "skip_hbm", "b_hbm", "c_hbm",
            "gx", "graw", "ztot", "grate", "gskip", "gbias")


def scratch_of(heads, tokens, size, state, peers):
    groups, chunks, chips = heads // GROUP, tokens // CHUNK, peers // 2
    wide, half = GROUP * size, size // 2
    vmem = pltpu.VMEM
    dma = pltpu.SemaphoreType.DMA
    halves = (2, groups, GROUP, half, state)
    segments = (2, chunks, CHUNK, state)
    return dict(
        raw=vmem((heads, tokens), F32),
        bias=vmem((1, heads), F32),
        rate=vmem((1, heads), F32),
        skip=vmem((1, heads), F32),
        b=vmem((tokens, state), BF16),
        c=vmem((tokens, state), BF16),
        src=vmem((2, groups, tokens, wide), BF16),
        xt=vmem((groups, wide, tokens), BF16),
        gt=vmem((groups, wide, tokens), BF16),
        dt=vmem((heads, tokens), F32),
        cum=vmem((heads, tokens), F32),
        scale=vmem((2, heads, tokens), F32),
        step=vmem((chunks, heads, CHUNK), F32),
        edge=vmem((2, chunks, heads, CHUNK), F32),
        whole=vmem((heads, CHUNK), F32),
        skips=vmem((heads, CHUNK), F32),
        local=vmem((2, groups, chunks, wide, state), F32),
        total=vmem((2, groups, GROUP, size, state), F32),
        ends=vmem((peers, heads, CHUNK), F32),
        coef=vmem((2, chips, heads, CHUNK), F32),
        pair_in=vmem(halves, F32),
        agg=vmem(halves, F32),
        chip_in=vmem((chips,) + halves[1:], F32),
        pre=vmem(halves, F32),
        post=vmem(halves[1:], F32),
        link=vmem((heads, CHUNK), F32),
        give=vmem(halves, F32),
        state_in=vmem((2, groups, GROUP, size, state), F32),
        dxt=vmem((groups, chunks, wide, CHUNK), F32),
        row=vmem((groups, chunks, GROUP, CHUNK), F32),
        col=vmem((groups, chunks, GROUP, CHUNK), F32),
        cross=vmem((groups, GROUP, CHUNK), F32),
        dg=vmem((chunks, CHUNK, CHUNK), F32),
        parts=vmem((2, groups, chunks, 2, wide, state), BF16),
        zown=vmem(segments, F32),
        zsum=vmem(segments, F32),
        zin=vmem((2,) + segments, F32),
        params_in=vmem((peers, heads, CHUNK), F32),
        small_sem=dma((6,)),
        load_sem=dma((2, groups)),
        end_send=dma((peers,)),
        end_recv=dma((peers,)),
        pair_send=dma((2, groups)),
        pair_recv=dma((2, groups)),
        chip_send=dma((chips, groups)),
        chip_recv=dma((chips, groups)),
        back_send=dma((2, groups)),
        back_recv=dma((2, groups)),
        in_send=dma((2, chunks)),
        out_send=dma((2, chunks)),
        z_recv=dma((2, 2, chunks)),
        param_send=dma((peers,)),
        param_recv=dma((peers,)),
    )


def kernel(names, peers, line, *refs):
    k = types.SimpleNamespace(**dict(zip(names, refs)))
    heads, tokens = k.raw.shape
    state = k.b.shape[1]
    groups, chunks, chips = heads // GROUP, tokens // CHUNK, peers // 2
    wide = k.src.shape[3]
    size = wide // GROUP
    half = size // 2
    me, zpos = lax.axis_index("ctx"), lax.axis_index("head")
    odd, chip = me % 2, me // 2
    mate = me + 1 - 2 * odd
    early = jnp.where(chip < chips // 2, 0, 1)
    late = 1 - early

    tree = chips == 4
    is_inner = jnp.logical_or(chip == 1, chip == 2)
    is_outer = jnp.logical_not(is_inner)
    inner_chip = jnp.where(chip < 2, 1, 2)
    pair_place = me + 2 - 4 * (chip % 2)
    across_place = me + 4 - 8 * (chip // 2)
    forwarded = groups // 2

    left = zpos < line // 2
    inner = jnp.where(left, zpos + 1, zpos - 1)
    outer = jnp.where(left, zpos - 1, zpos + 1)
    has_outer = jnp.logical_and(zpos > 0, zpos < line - 1)
    is_mid = jnp.logical_or(zpos == line // 2 - 1, zpos == line // 2)
    in_slot = jnp.where(is_mid, 1, 0)

    barrier = pltpu.get_barrier_semaphore()

    def remote(src, dst, send, recv, **place):
        return pltpu.make_async_remote_copy(
            src_ref=src, dst_ref=dst, send_sem=send, recv_sem=recv,
            device_id=place, device_id_type=MESH)

    def greet():
        for d in range(1, peers):
            pl.semaphore_signal(barrier, inc=1, device_id={"ctx": (me + d) % peers}, device_id_type=MESH)
        pl.semaphore_signal(barrier, inc=1, device_id={"head": inner}, device_id_type=MESH)

        @pl.when(has_outer)
        def _():
            pl.semaphore_signal(barrier, inc=1, device_id={"head": outer}, device_id_type=MESH)

    def met():
        pl.semaphore_wait(barrier, peers + jnp.where(has_outer, 1, 0))

    def load(e, group):
        at = pl.ds(pl.multiple_of(group * wide, wide), wide)
        return pltpu.make_async_copy((k.g_hbm, k.x_hbm)[e].at[:, at], k.src.at[e, group], k.load_sem.at[e, group])

    def small_loads():
        pairs = ((k.raw_hbm, k.raw), (k.bias_hbm, k.bias), (k.rate_hbm, k.rate), (k.skip_hbm, k.skip),
                 (k.b_hbm, k.b), (k.c_hbm, k.c))
        return [pltpu.make_async_copy(src, dst, k.small_sem.at[i]) for i, (src, dst) in enumerate(pairs)]

    def start_small():
        for copy in small_loads():
            copy.start()

    def start_loads(first, last):
        for group in range(first, last):
            load(1, group).start()
            load(0, group).start()

    def prepare():
        for copy in small_loads():
            copy.wait()
        start_loads(1, groups)
        dt = softplus(k.raw[...] + column_of(k.bias[...]))
        k.dt[...] = dt
        log_decay = -column_of(k.rate[...]) * dt
        ones = triangle(False).astype(F32)
        cums = [jnp.dot(log_decay[:, span_of(c)], ones, precision=HIGH) for c in range(chunks)]
        ends = [lanes(cum[:, CHUNK - 1:]) for cum in cums]
        before, after = jnp.zeros_like(ends[0]), jnp.zeros_like(ends[0])
        for c in range(chunks):
            k.edge[0, c] = jnp.exp(before)
            before = before + ends[c]
            k.edge[1, chunks - 1 - c] = jnp.exp(after)
            after = after + ends[chunks - 1 - c]
        k.whole[...] = jnp.exp(before)
        k.ends[me] = before
        for c in range(chunks):
            k.cum[:, span_of(c)] = cums[c]
            k.scale[0, :, span_of(c)] = jnp.exp(cums[c])
            k.scale[1, :, span_of(c)] = jnp.exp(ends[c] - cums[c]) * dt[:, span_of(c)]
            k.step[c] = jnp.exp(ends[c])
        k.dg[...] = jnp.zeros_like(k.dg)
        k.skips[...] = lanes(column_of(k.skip[...]))

    def end_copy(d, place):
        return remote(k.ends.at[place], k.ends.at[place], k.end_send.at[d], k.end_recv.at[d],
                      ctx=(me + d) % peers)

    def send_ends():
        for d in range(1, peers):
            end_copy(d, me).start()

    mine = pl.ds(pl.multiple_of(odd * half, half), half)
    theirs = pl.ds(pl.multiple_of((1 - odd) * half, half), half)

    def pair_copy(e, group):
        return remote(k.total.at[e, group, :, theirs, :], k.pair_in.at[e, group],
                      k.pair_send.at[e, group], k.pair_recv.at[e, group], ctx=mate)

    def chip_copy(step, group):
        what = jnp.where(chip + step < chips, 0, 1)
        return remote(k.agg.at[what, group], k.chip_in.at[step, group],
                      k.chip_send.at[step, group], k.chip_recv.at[step, group], ctx=(me + 2 * step) % peers)

    def tree_copy(slot, group, source):
        place = across_place if slot == 2 else pair_place
        return remote(source, k.chip_in.at[slot, group],
                      k.chip_send.at[slot, group], k.chip_recv.at[slot, group], ctx=place)

    def tree_arrival(slot, group):
        tree_copy(slot, group, k.post.at[group]).wait_recv()

    def tree_exchange(group):
        near = jnp.where(is_outer, early, late)
        if group < forwarded:
            tree_copy(1, group, k.agg.at[near, group]).start()
            return

        @pl.when(is_outer)
        def _():
            tree_copy(1, group, k.agg.at[early, group]).start()

        @pl.when(is_inner)
        def _():
            tree_copy(3, group, k.agg.at[early, group]).start()
            if group == groups - 1:
                for other in range(forwarded, groups):
                    tree_copy(1, other, k.agg.at[late, other]).start()

    def hand(group):
        link = k.link[rows_of(group)]

        @pl.when(is_inner)
        def _():
            tree_arrival(1, group)
            k.post[group] = k.agg[early, group] + scaled(link, k.chip_in[1, group])
            tree_copy(2, group, k.post.at[group]).start()

        if group >= forwarded:
            @pl.when(is_outer)
            def _():
                tree_arrival(3, group)
                k.post[group] = k.chip_in[3, group] + scaled(link, k.agg[early, group])
                tree_copy(2, group, k.post.at[group]).start()

    def forward(group):
        @pl.when(is_outer)
        def _():
            tree_arrival(2, group)
            tree_copy(3, group, k.chip_in.at[2, group]).start()

    def tree_early(group):
        @pl.when(is_inner)
        def _():
            k.pre[early, group] = k.chip_in[1, group]

        @pl.when(is_outer)
        def _():
            k.pre[early, group] = jnp.zeros((GROUP, half, state), F32)

        hand_back(early, group)

    def tree_late(group):
        @pl.when(is_inner)
        def _():
            slot = 3 if group < forwarded else 2
            tree_arrival(slot, group)
            k.pre[late, group] = k.chip_in[slot, group]

        @pl.when(is_outer)
        def _():
            tree_arrival(1, group)
            if group >= forwarded:
                tree_arrival(2, group)
            k.pre[late, group] = k.chip_in[1, group] + scaled(k.link[rows_of(group)], k.chip_in[2, group])

        hand_back(late, group)

    def tree_drain(group):
        tree_copy(1, group, k.post.at[group]).wait_send()

        @pl.when(is_inner)
        def _():
            tree_copy(2, group, k.post.at[group]).wait_send()
            if group >= forwarded:
                tree_copy(3, group, k.post.at[group]).wait_send()

        @pl.when(is_outer)
        def _():
            tree_copy(3 if group < forwarded else 2, group, k.post.at[group]).wait_send()

    def back_copy(e, group, rows):
        return remote(k.give.at[e, group], k.state_in.at[e, group, :, rows, :],
                      k.back_send.at[e, group], k.back_recv.at[e, group], ctx=mate)

    def rows_of(group):
        return pl.ds(pl.multiple_of(group * GROUP, GROUP), GROUP)

    def carry_local(e, group, order, source, operand):
        at_rows = rows_of(group)
        value = None
        for c in order:
            at = span_of(c)
            k.local[e, group, c] = jnp.zeros((wide, state), F32) if value is None else value
            high, low = split(per_head(k.scale[1 - e, at_rows, at], source[group, :, at].astype(F32)))
            added = mm(jnp.concatenate([high, low], axis=1), twice(operand[at, :], 0))
            value = added if value is None else per_head(k.step[c, at_rows], value) + added
        k.total[e, group] = value.reshape(GROUP, size, state)

    def states(group):
        load(1, group).wait()
        k.xt[group] = k.src[1, group].T
        carry_local(0, group, range(chunks), k.xt, k.b)

    def backs(group):
        load(0, group).wait()
        k.gt[group] = k.src[0, group].T
        carry_local(1, group, reversed(range(chunks)), k.gt, k.c)

    def make_coefs():
        for d in range(1, peers):
            @pl.when(d != mate_step)
            def _():
                end_copy(d, (me - d + peers) % peers).wait_recv()
        s_log = jnp.zeros((heads, CHUNK), F32)
        r_log = jnp.zeros((heads, CHUNK), F32)
        for step in range(1, chips):
            k.coef[0, step] = jnp.exp(s_log)
            k.coef[1, step] = jnp.exp(r_log)
            low = (chip - step + chips) % chips
            high = (chip + step) % chips
            s_log = s_log + (k.ends[2 * low] + k.ends[2 * low + 1])
            r_log = r_log + (k.ends[2 * high] + k.ends[2 * high + 1])
        if tree:
            k.link[...] = jnp.exp(k.ends[2 * inner_chip] + k.ends[2 * inner_chip + 1])

    def scaled(coef, block):
        return coef[:, None, :] * block

    def downstream(e):
        return jnp.where(e == 0, odd, 1 - odd) == 1

    def own_and_mate(group):
        at_rows = rows_of(group)
        own = jnp.exp(k.ends[me, at_rows])
        return own, jnp.exp(k.ends[mate, at_rows]), jnp.ones_like(own), jnp.zeros_like(own)

    def combine(group):
        if group == 0:
            end_copy(mate_step, mate).wait_recv()

        own_e, mate_e, one, _ = own_and_mate(group)
        for e in range(2):
            down = downstream(e)
            pair_copy(e, group).wait_recv()
            k.agg[e, group] = (scaled(jnp.where(down, one, mate_e), k.total[e, group, :, mine, :])
                               + scaled(jnp.where(down, own_e, one), k.pair_in[e, group]))

    def gather(e, group):
        at_rows = rows_of(group)
        k.pre[e, group] = jnp.zeros((GROUP, half, state), F32)
        for step in range(1, chips):
            slot = jnp.where(e == 0, step, chips - step)

            @pl.when(jnp.where(e == 0, chip, chips - 1 - chip) >= step)
            def _():
                chip_copy(slot, group).wait_recv()
                k.pre[e, group] += scaled(k.coef[e, step, at_rows], k.chip_in[slot, group])

        hand_back(e, group)

    def hand_back(e, group):
        own_e, mate_e, one, zero = own_and_mate(group)
        down = downstream(e)
        pre = k.pre[e, group]
        k.give[e, group] = (scaled(jnp.where(down, one, own_e), pre)
                            + scaled(jnp.where(down, zero, one), k.total[e, group, :, mine, :]))
        k.state_in[e, group, :, mine, :] = (scaled(jnp.where(down, mate_e, one), pre)
                                            + scaled(jnp.where(down, one, zero), k.pair_in[e, group]))
        back_copy(e, group, mine).start()

    causal = triangle(False)

    def within(group):
        def one_chunk(c, carry):
            at = pl.ds(pl.multiple_of(c * CHUNK, CHUNK), CHUNK)
            scores = mm_nt(k.b[at, :], k.c[at, :])
            cum = k.cum[rows_of(group), at]
            shifted = (cum - jnp.log(k.dt[rows_of(group), at])).T
            total = jnp.zeros((CHUNK, CHUNK), F32)
            rows, cols = [], []
            for pair in range(GROUP // 2):
                x_pair = k.src[1, group, at, pair * 2 * size:(pair + 1) * 2 * size]
                places = [slice((2 * pair + j) * size, (2 * pair + j + 1) * size) for j in range(2)]
                products = mm(x_pair, pair_blocks(k.gt[group, places[0], at], k.gt[group, places[1], at]))
                for j in range(2):
                    h = 2 * pair + j
                    gap = cum[h:h + 1, :] - shifted[:, h:h + 1]
                    decay = jnp.exp(jnp.where(causal, gap, -1e30))
                    both = products[:, j * CHUNK:(j + 1) * CHUNK] * decay
                    total = total + both
                    rows.append(jnp.sum(both * scores, axis=0, keepdims=True))
                    high, low = split(decay * scores)
                    dx_h = mm_nt(twice(k.gt[group, places[j], at], 1), jnp.concatenate([high, low], axis=1))
                    k.dxt[group, c, places[j], :] = dx_h
                    x_h = k.xt[group, places[j], at]
                    cols.append(jnp.sum(dx_h * x_h.astype(F32), axis=0, keepdims=True))
            k.row[group, c] = jnp.concatenate(rows, axis=0)
            k.col[group, c] = jnp.concatenate(cols, axis=0)
            k.dg[c] += total
            return carry

        lax.fori_loop(0, chunks, one_chunk, 0)

    def score_parts():
        for c in range(chunks):
            at = span_of(c)
            for e, dg, operand in ((0, k.dg[c].T, k.b), (1, k.dg[c], k.c)):
                high, low = split(dg)
                k.zown[e, c] = mm(jnp.concatenate([high, low], axis=1), twice(operand[at, :], 0))

    def projections(e, c):
        at = span_of(c)
        total = k.zown[e, c]
        for group in range(groups):
            if c == 0:
                back_copy(e, group, theirs).wait_recv()
            at_rows = rows_of(group)
            incoming = k.state_in[e, group].reshape(wide, state)
            high, low = split(per_head(k.edge[e, c, at_rows], incoming) + k.local[e, group, c])
            k.parts[e, group, c, 0] = high
            k.parts[e, group, c, 1] = low
            column = k.scale[e, at_rows, at].T
            for pair in range(GROUP // 2):
                wide_at = slice(pair * 2 * size, (pair + 1) * 2 * size)
                one = slice(2 * pair * size, (2 * pair + 1) * size)
                two = slice((2 * pair + 1) * size, (2 * pair + 2) * size)
                both = mm(twice(k.src[e, group, at, wide_at], 1),
                          jnp.concatenate([pair_blocks(high[one], high[two]),
                                           pair_blocks(low[one], low[two])], axis=0))
                for j in range(2):
                    h = 2 * pair + j
                    total = total + both[:, j * state:(j + 1) * state] * column[:, h:h + 1]
        k.zown[e, c] = total

    def inward(e, c, source):
        return remote(source.at[e, c], k.zin.at[in_slot, e, c],
                      k.in_send.at[e, c], k.z_recv.at[in_slot, e, c], head=inner)

    def outward(e, c, slot=1):
        return remote(k.ztot.at[e, c], k.zin.at[slot, e, c],
                      k.out_send.at[e, c], k.z_recv.at[slot, e, c], head=outer)

    def publish(e, c):
        @pl.when(jnp.logical_not(has_outer))
        def _():
            inward(e, c, k.zown).start()

    def relay(e, c):
        @pl.when(has_outer)
        def _():
            outward(e, c, 0).wait_recv()
            k.zsum[e, c] = k.zown[e, c] + k.zin[0, e, c]
            inward(e, c, k.zsum).start()

    def settle(e, c):
        outward(e, c).wait_recv()

        @pl.when(jnp.logical_and(is_mid, has_outer))
        def _():
            k.ztot[e, c] = k.zsum[e, c] + k.zin[1, e, c]

        @pl.when(jnp.logical_and(is_mid, jnp.logical_not(has_outer)))
        def _():
            k.ztot[e, c] = k.zown[e, c] + k.zin[1, e, c]

        @pl.when(jnp.logical_not(is_mid))
        def _():
            k.ztot[e, c] = k.zin[1, e, c]

        @pl.when(has_outer)
        def _():
            outward(e, c).start()

    def settle_mid(e, c):
        @pl.when(is_mid)
        def _():
            settle(e, c)

    def settle_rest(e, c):
        @pl.when(jnp.logical_not(is_mid))
        def _():
            settle(e, c)

    def inputs_step(c, group):
        at, at_rows = span_of(c), rows_of(group)
        bb, cc = twice(k.b[at, :], 1), twice(k.c[at, :], 1)
        reach, weight = k.scale[0, at_rows, at], k.scale[1, at_rows, at]
        xt, gt = k.xt[group, :, at].astype(F32), k.gt[group, :, at].astype(F32)
        parts = [jnp.concatenate([k.parts[e, group, c, 0], k.parts[e, group, c, 1]], axis=1) for e in range(2)]
        y = mm_nt(parts[0], cc)
        k.row[group, c] += head_sums(y * gt, GROUP) * reach
        dx = per_head(weight, mm_nt(parts[1], bb))
        k.col[group, c] += head_sums(dx * xt, GROUP)
        product = head_sums(xt * gt, GROUP)
        k.cross[group] = product if c == 0 else k.cross[group] + product
        dx = dx + k.dxt[group, c] + per_head(k.skips[at_rows], gt)
        k.gx[group, c] = dx.astype(BF16).T

    def step_sizes():
        rate, bias = column_of(k.rate[...]), column_of(k.bias[...])
        beyond = []
        for group in range(groups):
            last = k.total[0, group] + scaled(k.whole[rows_of(group)], k.state_in[0, group])
            sums = jnp.sum(last * k.state_in[1, group], axis=1)
            beyond.append(jnp.sum(sums, axis=1, keepdims=True))
        beyond = lanes(jnp.concatenate(beyond, axis=0))
        suffix = triangle(True).astype(F32)
        g_rate = jnp.zeros((heads, 1), F32)
        g_bias = jnp.zeros((heads, 1), F32)
        for c in reversed(range(chunks)):
            at = span_of(c)
            row = jnp.concatenate([k.row[group, c] for group in range(groups)], axis=0)
            col = jnp.concatenate([k.col[group, c] for group in range(groups)], axis=0)
            change = row - col
            d_log = jnp.dot(change, suffix, precision=HIGH) + beyond
            beyond = beyond + lanes(jnp.sum(change, axis=1, keepdims=True))
            dt = k.dt[:, at]
            g_dt = col / dt - rate * d_log
            g_raw = g_dt / (1.0 + jnp.exp(-(k.raw[:, at] + bias)))
            k.graw[:, at] = g_raw
            g_rate = g_rate - jnp.sum(dt * d_log, axis=1, keepdims=True)
            g_bias = g_bias + jnp.sum(g_raw, axis=1, keepdims=True)
        cross = jnp.concatenate([k.cross[group] for group in range(groups)], axis=0)
        g_skip = jnp.sum(cross, axis=1, keepdims=True)
        lane = lax.broadcasted_iota(jnp.int32, (heads, CHUNK), 1)
        k.params_in[me] = jnp.where(lane == 0, g_rate, jnp.where(lane == 1, g_skip, g_bias))

    def params_copy(d, place):
        return remote(k.params_in.at[place], k.params_in.at[place], k.param_send.at[d], k.param_recv.at[d],
                      ctx=(me + d) % peers)

    def gather_params():
        for d in range(1, peers):
            params_copy(d, (me - d + peers) % peers).wait_recv()
        total = k.params_in[0]
        for d in range(1, peers):
            total = total + k.params_in[d]
        k.grate[...] = row_of(total[:, 0:1])
        k.gskip[...] = row_of(total[:, 1:2])
        k.gbias[...] = row_of(total[:, 2:3])

    mate_step = jnp.where(odd == 1, 1, peers - 1)

    def nth_step(n):
        return jnp.where(chip < chips // 2, n, chips - n)

    def exchange(group):
        combine(group)
        if tree:
            tree_exchange(group)
            return
        for n in range(1, chips):
            chip_copy(nth_step(n), group).start()

    start_small()
    start_loads(0, 1)
    greet()
    prepare()
    met()
    send_ends()
    for group in range(groups):
        states(group)
        pair_copy(0, group).start()
        backs(group)
        pair_copy(1, group).start()
        if group > 0:
            exchange(group - 1)
    for group in range(groups):
        within(group)
        if group == 0:
            exchange(groups - 1)
            make_coefs()
        if tree:
            hand(group)
            if 2 <= group < forwarded + 2:
                forward(group - 2)
            if group > 0:
                tree_early(group - 1)
    if tree:
        for group in range(max(groups - 2, 0), forwarded):
            forward(group)
        tree_early(groups - 1)
    else:
        for group in range(groups):
            gather(early, group)
    score_parts()

    pieces = [(e, c) for e in (early, late) for c in range(chunks)]
    relayed, settled = 0, 0

    def tend(relays, settles):
        nonlocal relayed, settled
        while relayed < min(relays, len(pieces)):
            relay(*pieces[relayed])
            relayed += 1
        while settled < min(settles, relayed):
            settle_mid(*pieces[settled])
            settled += 1

    for c in range(chunks):
        projections(early, c)
        publish(early, c)
    for group in range(groups):
        (tree_late if tree else functools.partial(gather, late))(group)
    tend(1, 0)
    for c in range(chunks):
        projections(late, c)
        publish(late, c)
        tend((2, 2, 3, 4)[min(c, 3)], (0, 0, 1, 2)[min(c, 3)])
    turns = [(c, group) for c in range(chunks) for group in range(groups)]
    for j, turn in enumerate(turns):
        inputs_step(*turn)
        part = 16 * (j + 1) // len(turns)
        tend(chunks + sum(part >= at for at in (3, 9, 16)), chunks - 2 + sum(part >= at for at in (5, 12, 16)))
    step_sizes()
    for d in range(1, peers):
        params_copy(d, me).start()
    tend(len(pieces), len(pieces))
    for piece in pieces:
        settle_rest(*piece)
    gather_params()

    def drain():
        for group in range(groups):
            for e in range(2):
                pair_copy(e, group).wait_send()
                back_copy(e, group, mine).wait_send()
            if tree:
                tree_drain(group)
            else:
                for step in range(1, chips):
                    chip_copy(step, group).wait_send()
        for c in range(chunks):
            for e in range(2):
                inward(e, c, k.zsum).wait_send()

                @pl.when(has_outer)
                def _():
                    outward(e, c).wait_send()
        for d in range(1, peers):
            end_copy(d, me).wait_send()
            params_copy(d, me).wait_send()

    drain()


def finish_kernel(groups, chunks, gx, graw, ztot, grate, gskip, gbias,
                  gx_out, graw_out, gb_out, gc_out, grate_out, gskip_out, gbias_out, sems):
    wide = gx.shape[3]
    copies = [(gx.at[group, c], gx_out.at[span_of(c), group * wide:(group + 1) * wide])
              for group in range(groups) for c in range(chunks)]
    copies += [(ztot.at[1 - i, c], ref.at[span_of(c), :]) for i, ref in enumerate((gb_out, gc_out))
               for c in range(chunks)]
    copies += [(graw, graw_out), (grate, grate_out), (gskip, gskip_out), (gbias, gbias_out)]
    copies = [pltpu.make_async_copy(src, dst, sems.at[i]) for i, (src, dst) in enumerate(copies)]
    for copy in copies:
        copy.start()
    for copy in copies:
        copy.wait()


def on_device(peers, line, tokens_x, raw_dt, in_b, in_c, decay_rate, skip_gain, step_bias, grad_y):
    heads, tokens = raw_dt.shape
    width = tokens_x.shape[1]
    size = width // heads
    state = in_b.shape[1]
    groups, chunks = heads // GROUP, tokens // CHUNK
    scratch = scratch_of(heads, tokens, size, state, peers)
    names = inputs_and_outputs() + tuple(scratch)

    def shape(*dims, dtype=F32):
        return jax.ShapeDtypeStruct(dims, dtype)

    hbm, vmem = pl.BlockSpec(memory_space=pl.ANY), pl.BlockSpec(memory_space=pltpu.VMEM)
    row = shape(1, heads)
    results = pl.pallas_call(
        functools.partial(kernel, names, peers, line),
        in_specs=[pl.BlockSpec(memory_space=pltpu.HBM)] * 8,
        out_specs=[vmem] * 6,
        out_shape=[shape(groups, chunks, CHUNK, GROUP * size, dtype=BF16), shape(heads, tokens),
                   shape(2, chunks, CHUNK, state), row, row, row],
        scratch_shapes=list(scratch.values()),
        compiler_params=pltpu.CompilerParams(
            collective_id=0, has_side_effects=True, vmem_limit_bytes=VMEM_LIMIT),
        name="layer",
    )(*[pltpu.with_memory_space_constraint(a, pltpu.HBM) for a in (
        tokens_x, grad_y, raw_dt, step_bias[None], decay_rate[None], skip_gain[None], in_b, in_c)])
    gx, graw, gb, gc, grate, gskip, gbias = pl.pallas_call(
        functools.partial(finish_kernel, groups, chunks),
        in_specs=[vmem] * 6,
        out_specs=[hbm] * 7,
        out_shape=[shape(tokens, width, dtype=BF16), shape(heads, tokens), shape(tokens, state),
                   shape(tokens, state), row, row, row],
        scratch_shapes=[pltpu.SemaphoreType.DMA((groups * chunks + 2 * chunks + 4,))],
        compiler_params=pltpu.CompilerParams(vmem_limit_bytes=4 << 20),
        name="finish",
    )(*results)
    return gx, graw, gb, gc, grate[0], gskip[0], gbias[0]


def solution(mesh):
    return jax.shard_map(
        functools.partial(on_device, mesh.shape["ctx"], mesh.shape["head"]),
        mesh=mesh,
        in_specs=(
            P("ctx", "head"),
            P("head", "ctx"),
            P("ctx", None),
            P("ctx", None),
            P("head"),
            P("head"),
            P("head"),
            P("ctx", "head"),
        ),
        out_specs=(
            P("ctx", "head"),
            P("head", "ctx"),
            P("ctx", None),
            P("ctx", None),
            P("head"),
            P("head"),
            P("head"),
        ),
        check_vma=False,
    )
```

```python
import functools
import types

import jax
import jax.numpy as jnp
from jax import lax
from jax.experimental import pallas as pl
from jax.experimental.pallas import tpu as pltpu
from jax.sharding import PartitionSpec as P

CHUNK = 128
GROUP = 8
F32 = jnp.float32
BF16 = jnp.bfloat16
HIGH = lax.Precision.HIGHEST
NT = (((1,), (1,)), ((), ()))
MESH = pl.DeviceIdType.MESH
VMEM_LIMIT = 50 << 20
LOG2_E = 1.4426950408889634
HANDS = (0, 1, 1, 2)


def mm(a, b):
    return jnp.dot(a, b, preferred_element_type=F32)


def mm_nt(a, b):
    return lax.dot_general(a, b, NT, preferred_element_type=F32)


def split(a):
    high = a.astype(BF16)
    return high, (a - high.astype(F32)).astype(BF16)


def twice(a, axis):
    return jnp.concatenate([a, a], axis=axis)


def softplus(v):
    return jnp.maximum(v, 0.0) + jnp.log1p(jnp.exp(-jnp.abs(v)))


def lanes(column, width=CHUNK):
    return jnp.broadcast_to(column, (column.shape[0], width))


def per_head(rows, matrix):
    heads = rows.shape[0]
    shaped = matrix.reshape(heads, matrix.shape[0] // heads, matrix.shape[1])
    return (shaped * rows[:, None, :]).reshape(matrix.shape)


def head_sums(matrix, heads):
    return jnp.sum(matrix.reshape(heads, matrix.shape[0] // heads, matrix.shape[1]), axis=1)


def pair_blocks(first, second):
    zero = jnp.zeros_like(first)
    return jnp.concatenate(
        [jnp.concatenate([first, zero], axis=1), jnp.concatenate([zero, second], axis=1)], axis=0
    )


def triangle(lower):
    row = lax.broadcasted_iota(jnp.int32, (CHUNK, CHUNK), 0)
    col = lax.broadcasted_iota(jnp.int32, (CHUNK, CHUNK), 1)
    return (row >= col) if lower else (row <= col)


def eye(n):
    row = lax.broadcasted_iota(jnp.int32, (n, n), 0)
    col = lax.broadcasted_iota(jnp.int32, (n, n), 1)
    return row == col


def column_of(row):
    n = row.shape[1]
    return jnp.sum(jnp.where(eye(n), jnp.broadcast_to(row, (n, n)), 0.0), axis=1, keepdims=True)


def row_of(column):
    n = column.shape[0]
    return jnp.sum(jnp.where(eye(n), jnp.broadcast_to(column, (n, n)), 0.0), axis=0, keepdims=True)


def span_of(c):
    return slice(c * CHUNK, (c + 1) * CHUNK)


def inputs_and_outputs():
    return ("x_hbm", "g_hbm", "raw_hbm", "bias_hbm", "rate_hbm", "skip_hbm", "b_hbm", "c_hbm",
            "gx", "graw", "ztot", "grate", "gskip", "gbias")


def scratch_of(heads, tokens, size, state, peers):
    groups, chunks, chips = heads // GROUP, tokens // CHUNK, peers // 2
    wide, half = GROUP * size, size // 2
    vmem = pltpu.VMEM
    dma = pltpu.SemaphoreType.DMA
    halves = (2, groups, GROUP, half, state)
    segments = (2, chunks, CHUNK, state)
    return dict(
        raw=vmem((heads, tokens), F32),
        bias=vmem((1, heads), F32),
        rate=vmem((1, heads), F32),
        skip=vmem((1, heads), F32),
        b=vmem((tokens, state), BF16),
        c=vmem((tokens, state), BF16),
        src=vmem((2, groups, tokens, wide), BF16),
        xt=vmem((groups, wide, tokens), BF16),
        gt=vmem((groups, wide, tokens), BF16),
        dt=vmem((heads, tokens), F32),
        cum=vmem((heads, tokens), F32),
        scale=vmem((2, heads, tokens), F32),
        step=vmem((chunks, heads, CHUNK), F32),
        edge=vmem((2, chunks, heads, CHUNK), F32),
        whole=vmem((heads, CHUNK), F32),
        skips=vmem((heads, CHUNK), F32),
        local=vmem((2, groups, chunks, wide, state), F32),
        total=vmem((2, groups, GROUP, size, state), F32),
        ends=vmem((peers, heads, CHUNK), F32),
        end_rows=vmem((peers, 1, heads), F32),
        coef=vmem((2, chips, heads, CHUNK), F32),
        pair_in=vmem(halves, F32),
        agg=vmem(halves, F32),
        chip_in=vmem((chips,) + halves[1:], F32),
        pre=vmem(halves, F32),
        post=vmem(halves[1:], F32),
        link=vmem((heads, CHUNK), F32),
        give=vmem(halves, F32),
        state_in=vmem((2, groups, GROUP, size, state), F32),
        dxt=vmem((groups, chunks, wide, CHUNK), F32),
        row=vmem((groups, chunks, GROUP, CHUNK), F32),
        col=vmem((groups, chunks, GROUP, CHUNK), F32),
        cross=vmem((groups, GROUP, CHUNK), F32),
        dg=vmem((chunks, CHUNK, CHUNK), F32),
        parts=vmem((2, groups, chunks, 2, wide, state), BF16),
        zown=vmem(segments, F32),
        zsum=vmem(segments, F32),
        zin=vmem((2,) + segments, F32),
        params_in=vmem((peers, heads, CHUNK), F32),
        small_sem=dma((6,)),
        load_sem=dma((2, groups)),
        end_send=dma(()),
        end_recv=dma((2,)),
        pair_send=dma(()),
        pair_recv=dma((2, groups)),
        chip_send=dma((chips,)),
        chip_recv=dma((chips - 1, groups)),
        back_send=dma(()),
        back_recv=dma((2, groups)),
        in_send=dma(()),
        out_send=dma(()),
        z_recv=dma((2, 2, chunks)),
        param_send=dma(()),
        param_recv=dma(()),
    )


def kernel(names, peers, line, *refs):
    k = types.SimpleNamespace(**dict(zip(names, refs)))
    heads, tokens = k.raw.shape
    state = k.b.shape[1]
    groups, chunks, chips = heads // GROUP, tokens // CHUNK, peers // 2
    wide = k.src.shape[3]
    size = wide // GROUP
    half = size // 2
    me, zpos = lax.axis_index("ctx"), lax.axis_index("head")
    odd, chip = me % 2, me // 2
    mate = me + 1 - 2 * odd
    mate_step = jnp.where(odd == 1, 1, peers - 1)
    early = jnp.where(chip < chips // 2, 0, 1)
    late = 1 - early

    tree = chips == 4
    is_inner = jnp.logical_or(chip == 1, chip == 2)
    is_outer = jnp.logical_not(is_inner)
    inner_chip = jnp.where(chip < 2, 1, 2)
    pair_place = me + 2 - 4 * (chip % 2)
    across_place = me + 4 - 8 * (chip // 2)
    forwarded = groups // 2

    left = zpos < line // 2
    inner = jnp.where(left, zpos + 1, zpos - 1)
    outer = jnp.where(left, zpos - 1, zpos + 1)
    has_outer = jnp.logical_and(zpos > 0, zpos < line - 1)
    is_mid = jnp.logical_or(zpos == line // 2 - 1, zpos == line // 2)
    in_slot = jnp.where(is_mid, 1, 0)

    barrier = pltpu.get_barrier_semaphore()

    def remote(src, dst, send, recv, **place):
        return pltpu.make_async_remote_copy(
            src_ref=src, dst_ref=dst, send_sem=send, recv_sem=recv,
            device_id=place, device_id_type=MESH)

    def greet():
        for d in range(1, peers):
            pl.semaphore_signal(barrier, inc=1, device_id={"ctx": (me + d) % peers}, device_id_type=MESH)
        pl.semaphore_signal(barrier, inc=1, device_id={"head": inner}, device_id_type=MESH)

        @pl.when(has_outer)
        def _():
            pl.semaphore_signal(barrier, inc=1, device_id={"head": outer}, device_id_type=MESH)

    def met():
        pl.semaphore_wait(barrier, peers + jnp.where(has_outer, 1, 0))

    def load(e, group):
        at = pl.ds(pl.multiple_of(group * wide, wide), wide)
        return pltpu.make_async_copy((k.g_hbm, k.x_hbm)[e].at[:, at], k.src.at[e, group], k.load_sem.at[e, group])

    def small_loads():
        pairs = ((k.raw_hbm, k.raw), (k.bias_hbm, k.bias), (k.rate_hbm, k.rate), (k.skip_hbm, k.skip),
                 (k.b_hbm, k.b), (k.c_hbm, k.c))
        return [pltpu.make_async_copy(src, dst, k.small_sem.at[i]) for i, (src, dst) in enumerate(pairs)]

    def start_small():
        for copy in small_loads():
            copy.start()

    def start_loads(first, last):
        for group in range(first, last):
            load(1, group).start()
            load(0, group).start()

    def prepare():
        for copy in small_loads():
            copy.wait()
        start_loads(1, groups)
        dt = softplus(k.raw[...] + column_of(k.bias[...]))
        k.dt[...] = dt
        log_decay = -column_of(k.rate[...]) * dt
        ones = triangle(False).astype(F32)
        cums = [jnp.dot(log_decay[:, span_of(c)], ones, precision=HIGH) for c in range(chunks)]
        ends = [lanes(cum[:, CHUNK - 1:]) for cum in cums]
        before, after = jnp.zeros_like(ends[0]), jnp.zeros_like(ends[0])
        for c in range(chunks):
            k.edge[0, c] = jnp.exp(before)
            before = before + ends[c]
            k.edge[1, chunks - 1 - c] = jnp.exp(after)
            after = after + ends[chunks - 1 - c]
        k.whole[...] = jnp.exp(before)
        k.ends[me] = before
        k.end_rows[me] = row_of(before[:, 0:1])
        for c in range(chunks):
            k.cum[:, span_of(c)] = cums[c]
            k.scale[0, :, span_of(c)] = jnp.exp(cums[c])
            k.scale[1, :, span_of(c)] = jnp.exp(ends[c] - cums[c]) * dt[:, span_of(c)]
            k.step[c] = jnp.exp(ends[c])
        k.dg[...] = jnp.zeros_like(k.dg)
        k.skips[...] = lanes(column_of(k.skip[...]))

    def end_copy(d, place):
        slot = jnp.where(d == peers - mate_step, 1, 0)
        return remote(k.end_rows.at[place], k.end_rows.at[place], k.end_send, k.end_recv.at[slot],
                      ctx=(me + d) % peers)

    def end_arrival(slot, count):
        some = k.end_rows.at[pl.ds(0, count)]
        remote(some, some, k.end_send, k.end_recv.at[slot], ctx=mate).wait_recv()

    def send_ends():
        for d in range(1, peers):
            end_copy(d, me).start()

    mine = pl.ds(pl.multiple_of(odd * half, half), half)
    theirs = pl.ds(pl.multiple_of((1 - odd) * half, half), half)

    def pair_copy(e, group):
        return remote(k.total.at[e, group, :, theirs, :], k.pair_in.at[e, group],
                      k.pair_send, k.pair_recv.at[e, group], ctx=mate)

    def chip_copy(step, group):
        what = jnp.where(chip + step < chips, 0, 1)
        return remote(k.agg.at[what, group], k.chip_in.at[step, group],
                      k.chip_send.at[step], k.chip_recv.at[step - 1, group], ctx=(me + 2 * step) % peers)

    def tree_copy(slot, group, source):
        place = across_place if slot == 2 else pair_place
        return remote(source, k.chip_in.at[slot, group],
                      k.chip_send.at[slot], k.chip_recv.at[slot - 1, group], ctx=place)

    def tree_arrival(slot, group):
        tree_copy(slot, group, k.post.at[group]).wait_recv()

    def tree_exchange(group):
        near = jnp.where(is_outer, early, late)
        if group < forwarded:
            tree_copy(1, group, k.agg.at[near, group]).start()
            return

        @pl.when(is_outer)
        def _():
            tree_copy(1, group, k.agg.at[early, group]).start()

        @pl.when(is_inner)
        def _():
            tree_copy(3, group, k.agg.at[early, group]).start()
            if group == groups - 1:
                for other in range(forwarded, groups):
                    tree_copy(1, other, k.agg.at[late, other]).start()

    def hand(group):
        link = k.link[rows_of(group)]

        @pl.when(is_inner)
        def _():
            tree_arrival(1, group)
            k.post[group] = k.agg[early, group] + scaled(link, k.chip_in[1, group])
            tree_copy(2, group, k.post.at[group]).start()

        if group >= forwarded:
            @pl.when(is_outer)
            def _():
                tree_arrival(3, group)
                k.post[group] = k.chip_in[3, group] + scaled(link, k.agg[early, group])
                tree_copy(2, group, k.post.at[group]).start()

    def forward(group):
        @pl.when(is_outer)
        def _():
            tree_arrival(2, group)
            tree_copy(3, group, k.chip_in.at[2, group]).start()

    def tree_early(group):
        @pl.when(is_inner)
        def _():
            k.pre[early, group] = k.chip_in[1, group]

        @pl.when(is_outer)
        def _():
            k.pre[early, group] = jnp.zeros((GROUP, half, state), F32)

        hand_back(early, group)

    def tree_late(group):
        @pl.when(is_inner)
        def _():
            slot = 3 if group < forwarded else 2
            tree_arrival(slot, group)
            k.pre[late, group] = k.chip_in[slot, group]

        @pl.when(is_outer)
        def _():
            tree_arrival(1, group)
            if group >= forwarded:
                tree_arrival(2, group)
            k.pre[late, group] = k.chip_in[1, group] + scaled(k.link[rows_of(group)], k.chip_in[2, group])

        hand_back(late, group)

    def sent(slot, count):
        some = k.chip_in.at[slot, pl.ds(0, count)]
        remote(some, some, k.chip_send.at[slot], k.chip_recv.at[slot - 1, 0], ctx=mate).wait_send()

    def tree_drain():
        sent(1, groups)

        @pl.when(is_inner)
        def _():
            sent(2, groups)
            if forwarded < groups:
                sent(3, groups - forwarded)

        @pl.when(is_outer)
        def _():
            if forwarded < groups:
                sent(2, groups - forwarded)
            if forwarded:
                sent(3, forwarded)

    def back_copy(e, group, rows):
        return remote(k.give.at[e, group], k.state_in.at[e, group, :, rows, :],
                      k.back_send, k.back_recv.at[e, group], ctx=mate)

    def rows_of(group):
        return pl.ds(pl.multiple_of(group * GROUP, GROUP), GROUP)

    def carry_local(e, group, order, source, operand):
        at_rows = rows_of(group)
        value = None
        for c in order:
            at = span_of(c)
            k.local[e, group, c] = jnp.zeros((wide, state), F32) if value is None else value
            high, low = split(per_head(k.scale[1 - e, at_rows, at], source[group, :, at].astype(F32)))
            added = mm(jnp.concatenate([high, low], axis=1), twice(operand[at, :], 0))
            value = added if value is None else per_head(k.step[c, at_rows], value) + added
        k.total[e, group] = value.reshape(GROUP, size, state)

    def states(group):
        load(1, group).wait()
        k.xt[group] = k.src[1, group].T
        carry_local(0, group, range(chunks), k.xt, k.b)

    def backs(group):
        load(0, group).wait()
        k.gt[group] = k.src[0, group].T
        carry_local(1, group, reversed(range(chunks)), k.gt, k.c)

    def make_coefs():
        if peers > 2:
            end_arrival(0, peers - 2)
            for d in range(peers):
                k.ends[d] = lanes(column_of(k.end_rows[d]))
        s_log = jnp.zeros((heads, CHUNK), F32)
        r_log = jnp.zeros((heads, CHUNK), F32)
        for step in range(1, chips):
            k.coef[0, step] = jnp.exp(s_log)
            k.coef[1, step] = jnp.exp(r_log)
            low = (chip - step + chips) % chips
            high = (chip + step) % chips
            s_log = s_log + (k.ends[2 * low] + k.ends[2 * low + 1])
            r_log = r_log + (k.ends[2 * high] + k.ends[2 * high + 1])
        if tree:
            k.link[...] = jnp.exp(k.ends[2 * inner_chip] + k.ends[2 * inner_chip + 1])

    def scaled(coef, block):
        return coef[:, None, :] * block

    def downstream(e):
        return jnp.where(e == 0, odd, 1 - odd) == 1

    def own_and_mate(group):
        at_rows = rows_of(group)
        own = jnp.exp(k.ends[me, at_rows])
        return own, jnp.exp(k.ends[mate, at_rows]), jnp.ones_like(own), jnp.zeros_like(own)

    def combine(group):
        if group == 0:
            end_arrival(1, 1)
            k.ends[mate] = lanes(column_of(k.end_rows[mate]))

        own_e, mate_e, one, _ = own_and_mate(group)
        for e in range(2):
            down = downstream(e)
            pair_copy(e, group).wait_recv()
            k.agg[e, group] = (scaled(jnp.where(down, one, mate_e), k.total[e, group, :, mine, :])
                               + scaled(jnp.where(down, own_e, one), k.pair_in[e, group]))

    def gather(e, group):
        at_rows = rows_of(group)
        k.pre[e, group] = jnp.zeros((GROUP, half, state), F32)
        for step in range(1, chips):
            slot = jnp.where(e == 0, step, chips - step)

            @pl.when(jnp.where(e == 0, chip, chips - 1 - chip) >= step)
            def _():
                chip_copy(slot, group).wait_recv()
                k.pre[e, group] += scaled(k.coef[e, step, at_rows], k.chip_in[slot, group])

        hand_back(e, group)

    def hand_back(e, group):
        own_e, mate_e, one, zero = own_and_mate(group)
        down = downstream(e)
        pre = k.pre[e, group]
        k.give[e, group] = (scaled(jnp.where(down, one, own_e), pre)
                            + scaled(jnp.where(down, zero, one), k.total[e, group, :, mine, :]))
        k.state_in[e, group, :, mine, :] = (scaled(jnp.where(down, mate_e, one), pre)
                                            + scaled(jnp.where(down, one, zero), k.pair_in[e, group]))
        back_copy(e, group, mine).start()

    causal = triangle(False)

    def within(group):
        for c in range(chunks):
            at = span_of(c)
            scores = mm_nt(k.b[at, :], k.c[at, :])
            dt = k.dt[rows_of(group), at]
            cum = k.cum[rows_of(group), at] * LOG2_E
            shifted = (cum - jnp.log2(dt)).T
            total = k.dg[c]
            rows, cols = [], []
            for pair in range(GROUP // 2):
                x_pair = k.src[1, group, at, pair * 2 * size:(pair + 1) * 2 * size]
                places = [slice((2 * pair + j) * size, (2 * pair + j + 1) * size) for j in range(2)]
                products = mm(x_pair, pair_blocks(k.gt[group, places[0], at], k.gt[group, places[1], at]))
                for j in range(2):
                    h = 2 * pair + j
                    gap = cum[h:h + 1, :] - shifted[:, h:h + 1]
                    decay = jnp.exp2(jnp.where(causal, gap, -1e30))
                    both = products[:, j * CHUNK:(j + 1) * CHUNK] * decay
                    total = total + both
                    rows.append(jnp.sum(both * scores, axis=0, keepdims=True))
                    high, low = split(decay * scores)
                    dx_h = mm_nt(twice(k.gt[group, places[j], at], 1), jnp.concatenate([high, low], axis=1))
                    k.dxt[group, c, places[j], :] = dx_h
                    x_h = k.xt[group, places[j], at]
                    cols.append(jnp.sum(dx_h * x_h.astype(F32), axis=0, keepdims=True))
            k.row[group, c] = jnp.concatenate(rows, axis=0)
            k.col[group, c] = jnp.concatenate(cols, axis=0)
            k.dg[c] = total

    def score_parts():
        for c in range(chunks):
            at = span_of(c)
            for e, dg, operand in ((0, k.dg[c].T, k.b), (1, k.dg[c], k.c)):
                high, low = split(dg)
                k.zown[e, c] = mm(jnp.concatenate([high, low], axis=1), twice(operand[at, :], 0))

    def projections(e, c, members):
        at = span_of(c)
        total = k.zown[e, c]
        for group in members:
            if c == 0:
                back_copy(e, group, theirs).wait_recv()
            at_rows = rows_of(group)
            incoming = k.state_in[e, group].reshape(wide, state)
            high, low = split(per_head(k.edge[e, c, at_rows], incoming) + k.local[e, group, c])
            k.parts[e, group, c, 0] = high
            k.parts[e, group, c, 1] = low
            column = k.scale[e, at_rows, at].T
            for pair in range(GROUP // 2):
                wide_at = slice(pair * 2 * size, (pair + 1) * 2 * size)
                one = slice(2 * pair * size, (2 * pair + 1) * size)
                two = slice((2 * pair + 1) * size, (2 * pair + 2) * size)
                both = mm(twice(k.src[e, group, at, wide_at], 1),
                          jnp.concatenate([pair_blocks(high[one], high[two]),
                                           pair_blocks(low[one], low[two])], axis=0))
                for j in range(2):
                    h = 2 * pair + j
                    total = total + both[:, j * state:(j + 1) * state] * column[:, h:h + 1]
        k.zown[e, c] = total

    def inward(e, c, source):
        return remote(source.at[e, c], k.zin.at[in_slot, e, c],
                      k.in_send, k.z_recv.at[in_slot, e, c], head=inner)

    def outward(e, c, slot=1):
        return remote(k.ztot.at[e, c], k.zin.at[slot, e, c],
                      k.out_send, k.z_recv.at[slot, e, c], head=outer)

    def publish(e, c):
        @pl.when(jnp.logical_not(has_outer))
        def _():
            inward(e, c, k.zown).start()

    def relay(e, c):
        @pl.when(has_outer)
        def _():
            outward(e, c, 0).wait_recv()
            k.zsum[e, c] = k.zown[e, c] + k.zin[0, e, c]
            inward(e, c, k.zsum).start()

    def settle(e, c):
        outward(e, c).wait_recv()

        @pl.when(jnp.logical_and(is_mid, has_outer))
        def _():
            k.ztot[e, c] = k.zsum[e, c] + k.zin[1, e, c]

        @pl.when(jnp.logical_and(is_mid, jnp.logical_not(has_outer)))
        def _():
            k.ztot[e, c] = k.zown[e, c] + k.zin[1, e, c]

        @pl.when(jnp.logical_not(is_mid))
        def _():
            k.ztot[e, c] = k.zin[1, e, c]

        @pl.when(has_outer)
        def _():
            outward(e, c).start()

    def settle_mid(e, c):
        @pl.when(is_mid)
        def _():
            settle(e, c)

    def settle_rest(e, c):
        @pl.when(jnp.logical_not(is_mid))
        def _():
            settle(e, c)

    def inputs_step(c, group):
        at, at_rows = span_of(c), rows_of(group)
        bb, cc = twice(k.b[at, :], 1), twice(k.c[at, :], 1)
        reach, weight = k.scale[0, at_rows, at], k.scale[1, at_rows, at]
        xt, gt = k.xt[group, :, at].astype(F32), k.gt[group, :, at].astype(F32)
        parts = [jnp.concatenate([k.parts[e, group, c, 0], k.parts[e, group, c, 1]], axis=1) for e in range(2)]
        y = mm_nt(parts[0], cc)
        k.row[group, c] += head_sums(y * gt, GROUP) * reach
        dx = per_head(weight, mm_nt(parts[1], bb))
        k.col[group, c] += head_sums(dx * xt, GROUP)
        product = head_sums(xt * gt, GROUP)
        k.cross[group] = product if c == 0 else k.cross[group] + product
        dx = dx + k.dxt[group, c] + per_head(k.skips[at_rows], gt)
        k.gx[group, c] = dx.astype(BF16).T

    def step_sizes():
        rate, bias = column_of(k.rate[...]), column_of(k.bias[...])
        beyond = []
        for group in range(groups):
            last = k.total[0, group] + scaled(k.whole[rows_of(group)], k.state_in[0, group])
            sums = jnp.sum(last * k.state_in[1, group], axis=1)
            beyond.append(jnp.sum(sums, axis=1, keepdims=True))
        beyond = lanes(jnp.concatenate(beyond, axis=0))
        suffix = triangle(True).astype(F32)
        g_rate = jnp.zeros((heads, 1), F32)
        g_bias = jnp.zeros((heads, 1), F32)
        for c in reversed(range(chunks)):
            at = span_of(c)
            row = jnp.concatenate([k.row[group, c] for group in range(groups)], axis=0)
            col = jnp.concatenate([k.col[group, c] for group in range(groups)], axis=0)
            change = row - col
            d_log = jnp.dot(change, suffix, precision=HIGH) + beyond
            beyond = beyond + lanes(jnp.sum(change, axis=1, keepdims=True))
            dt = k.dt[:, at]
            g_dt = col / dt - rate * d_log
            g_raw = g_dt / (1.0 + jnp.exp(-(k.raw[:, at] + bias)))
            k.graw[:, at] = g_raw
            g_rate = g_rate - jnp.sum(dt * d_log, axis=1, keepdims=True)
            g_bias = g_bias + jnp.sum(g_raw, axis=1, keepdims=True)
        cross = jnp.concatenate([k.cross[group] for group in range(groups)], axis=0)
        g_skip = jnp.sum(cross, axis=1, keepdims=True)
        lane = lax.broadcasted_iota(jnp.int32, (heads, CHUNK), 1)
        k.params_in[me] = jnp.where(lane == 0, g_rate, jnp.where(lane == 1, g_skip, g_bias))

    def params_copy(d, place):
        return remote(k.params_in.at[place], k.params_in.at[place], k.param_send, k.param_recv,
                      ctx=(me + d) % peers)

    def every_param():
        some = k.params_in.at[pl.ds(0, peers - 1)]
        return remote(some, some, k.param_send, k.param_recv, ctx=mate)

    def gather_params():
        every_param().wait_recv()
        total = k.params_in[0]
        for d in range(1, peers):
            total = total + k.params_in[d]
        k.grate[...] = row_of(total[:, 0:1])
        k.gskip[...] = row_of(total[:, 1:2])
        k.gbias[...] = row_of(total[:, 2:3])

    def nth_step(n):
        return jnp.where(chip < chips // 2, n, chips - n)

    def exchange(group):
        combine(group)
        if tree:
            tree_exchange(group)
            return
        for n in range(1, chips):
            chip_copy(nth_step(n), group).start()

    start_small()
    start_loads(0, 1)
    greet()
    prepare()
    met()
    send_ends()
    for group in range(groups):
        states(group)
        pair_copy(0, group).start()
        backs(group)
        pair_copy(1, group).start()
        if group > 0:
            exchange(group - 1)
    pieces = [(e, c) for e in (early, late) for c in range(chunks)]
    relayed, settled = 0, 0

    def tend(relays, settles):
        nonlocal relayed, settled
        while relayed < min(relays, len(pieces)):
            relay(*pieces[relayed])
            relayed += 1
        while settled < min(settles, relayed):
            settle_mid(*pieces[settled])
            settled += 1

    everyone = list(range(groups))
    if tree:
        handed, returned, passed = 0, 0, 0

        def pass_on(hands, returns, forwards):
            nonlocal handed, returned, passed
            while handed < min(hands, groups):
                hand(handed)
                handed += 1
            while returned < min(returns, groups):
                tree_early(returned)
                returned += 1
            while passed < min(forwards, forwarded):
                forward(passed)
                passed += 1

        for group in everyone:
            within(group)
            if group == 0:
                exchange(groups - 1)
                make_coefs()
            pass_on(HANDS[min(group, 3)], HANDS[min(group, 3)], 0)
        score_parts()
        first = everyone[:groups - 2]
        pass_on(groups - 2, groups - 2, 0)
        for c in range(chunks):
            projections(early, c, first)
            if c == chunks // 2 - 1:
                pass_on(groups - 1, groups - 1, 1)
        pass_on(groups, groups, 1)
        sooner = everyone[0::2][:groups - 1]
        later = [group for group in everyone if group not in sooner]
        for c in range(chunks):
            if c == chunks - 1:
                for group in sooner:
                    tree_late(group)
            projections(early, c, everyone[len(first):])
            publish(early, c)
            if c == 0:
                pass_on(groups, groups, groups)
        for c in range(chunks):
            projections(late, c, sooner)
            if c == chunks // 2 - 1:
                for group in later:
                    tree_late(group)
                tend(1, 0)
        tend(2, 0)
        for c in range(chunks):
            projections(late, c, later)
            publish(late, c)
            tend((3, 3, 4, 4)[min(c, 3)], (0, 0, 0, 1)[min(c, 3)])
    else:
        for group in everyone:
            within(group)
            if group == 0:
                exchange(groups - 1)
                make_coefs()
        score_parts()
        for e in (early, late):
            for group in everyone:
                gather(e, group)
            for c in range(chunks):
                projections(e, c, everyone)
                publish(e, c)
        tend(chunks, 1)
    turns = [(c, group) for c in range(chunks) for group in everyone]
    for j, turn in enumerate(turns):
        inputs_step(*turn)
        part = 16 * (j + 1) // len(turns)
        for n, at in enumerate((2, 6, 10, 15)):
            if part >= at:
                tend(chunks + 1 + n, chunks - 2 + n)
    step_sizes()
    for d in range(1, peers):
        params_copy(d, me).start()
    tend(len(pieces), len(pieces))
    for piece in pieces:
        settle_rest(*piece)
    gather_params()

    def drain():
        remote(k.pair_in, k.pair_in, k.pair_send, k.pair_recv.at[0, 0], ctx=mate).wait_send()
        remote(k.give, k.give, k.back_send, k.back_recv.at[0, 0], ctx=mate).wait_send()
        if tree:
            tree_drain()
        else:
            for step in range(1, chips):
                sent(step, groups)
        remote(k.zown, k.zown, k.in_send, k.z_recv.at[0, 0, 0], head=inner).wait_send()

        @pl.when(has_outer)
        def _():
            remote(k.zown, k.zown, k.out_send, k.z_recv.at[0, 0, 0], head=outer).wait_send()

        some = k.end_rows.at[pl.ds(0, peers - 1)]
        remote(some, some, k.end_send, k.end_recv.at[0], ctx=mate).wait_send()
        every_param().wait_send()

    drain()


def finish_kernel(groups, chunks, gx, graw, ztot, grate, gskip, gbias,
                  gx_out, graw_out, gb_out, gc_out, grate_out, gskip_out, gbias_out, sems):
    wide = gx.shape[3]
    copies = [(gx.at[group, c], gx_out.at[span_of(c), group * wide:(group + 1) * wide])
              for group in range(groups) for c in range(chunks)]
    copies += [(ztot.at[1 - i, c], ref.at[span_of(c), :]) for i, ref in enumerate((gb_out, gc_out))
               for c in range(chunks)]
    copies += [(graw, graw_out), (grate, grate_out), (gskip, gskip_out), (gbias, gbias_out)]
    copies = [pltpu.make_async_copy(src, dst, sems.at[i]) for i, (src, dst) in enumerate(copies)]
    for copy in copies:
        copy.start()
    for copy in copies:
        copy.wait()


def on_device(peers, line, tokens_x, raw_dt, in_b, in_c, decay_rate, skip_gain, step_bias, grad_y):
    heads, tokens = raw_dt.shape
    width = tokens_x.shape[1]
    size = width // heads
    state = in_b.shape[1]
    groups, chunks = heads // GROUP, tokens // CHUNK
    scratch = scratch_of(heads, tokens, size, state, peers)
    names = inputs_and_outputs() + tuple(scratch)

    def shape(*dims, dtype=F32):
        return jax.ShapeDtypeStruct(dims, dtype)

    hbm, vmem = pl.BlockSpec(memory_space=pl.ANY), pl.BlockSpec(memory_space=pltpu.VMEM)
    row = shape(1, heads)
    results = pl.pallas_call(
        functools.partial(kernel, names, peers, line),
        in_specs=[pl.BlockSpec(memory_space=pltpu.HBM)] * 8,
        out_specs=[vmem] * 6,
        out_shape=[shape(groups, chunks, CHUNK, GROUP * size, dtype=BF16), shape(heads, tokens),
                   shape(2, chunks, CHUNK, state), row, row, row],
        scratch_shapes=list(scratch.values()),
        compiler_params=pltpu.CompilerParams(
            collective_id=0, has_side_effects=True, vmem_limit_bytes=VMEM_LIMIT),
        name="layer",
    )(*[pltpu.with_memory_space_constraint(a, pltpu.HBM) for a in (
        tokens_x, grad_y, raw_dt, step_bias[None], decay_rate[None], skip_gain[None], in_b, in_c)])
    gx, graw, gb, gc, grate, gskip, gbias = pl.pallas_call(
        functools.partial(finish_kernel, groups, chunks),
        in_specs=[vmem] * 6,
        out_specs=[hbm] * 7,
        out_shape=[shape(tokens, width, dtype=BF16), shape(heads, tokens), shape(tokens, state),
                   shape(tokens, state), row, row, row],
        scratch_shapes=[pltpu.SemaphoreType.DMA((groups * chunks + 2 * chunks + 4,))],
        compiler_params=pltpu.CompilerParams(vmem_limit_bytes=4 << 20),
        name="finish",
    )(*results)
    return gx, graw, gb, gc, grate[0], gskip[0], gbias[0]


def solution(mesh):
    return jax.shard_map(
        functools.partial(on_device, mesh.shape["ctx"], mesh.shape["head"]),
        mesh=mesh,
        in_specs=(
            P("ctx", "head"),
            P("head", "ctx"),
            P("ctx", None),
            P("ctx", None),
            P("head"),
            P("head"),
            P("head"),
            P("ctx", "head"),
        ),
        out_specs=(
            P("ctx", "head"),
            P("head", "ctx"),
            P("ctx", None),
            P("ctx", None),
            P("head"),
            P("head"),
            P("head"),
        ),
        check_vma=False,
    )
```

```python
import functools
import types

import jax
import jax.numpy as jnp
from jax import lax
from jax.experimental import pallas as pl
from jax.experimental.pallas import tpu as pltpu
from jax.sharding import PartitionSpec as P

CHUNK = 128
GROUP = 8
F32 = jnp.float32
BF16 = jnp.bfloat16
HIGH = lax.Precision.HIGHEST
NT = (((1,), (1,)), ((), ()))
MESH = pl.DeviceIdType.MESH
VMEM_LIMIT = 50 << 20
LOG2_E = 1.4426950408889634
HANDS = (1, 1, 2, 2)
LATE_TURNS = ((1, 0, 1), (2, 1, 1), (4, 2, 2), (6, 3, 2), (8, 4, 2), (9, 4, 3), (10, 5, 3), (12, 6, 3), (13, 6, 4), (14, 7, 4), (16, 8, 5))


def mm(a, b):
    return jnp.dot(a, b, preferred_element_type=F32)


def mm_nt(a, b):
    return lax.dot_general(a, b, NT, preferred_element_type=F32)


def split(a):
    high = a.astype(BF16)
    return high, (a - high.astype(F32)).astype(BF16)


def twice(a, axis):
    return jnp.concatenate([a, a], axis=axis)


def softplus(v):
    return jnp.maximum(v, 0.0) + jnp.log1p(jnp.exp(-jnp.abs(v)))


def lanes(column, width=CHUNK):
    return jnp.broadcast_to(column, (column.shape[0], width))


def per_head(rows, matrix):
    heads = rows.shape[0]
    shaped = matrix.reshape(heads, matrix.shape[0] // heads, matrix.shape[1])
    return (shaped * rows[:, None, :]).reshape(matrix.shape)


def head_sums(matrix, heads):
    return jnp.sum(matrix.reshape(heads, matrix.shape[0] // heads, matrix.shape[1]), axis=1)


def pair_blocks(first, second):
    zero = jnp.zeros_like(first)
    return jnp.concatenate(
        [jnp.concatenate([first, zero], axis=1), jnp.concatenate([zero, second], axis=1)], axis=0
    )


def triangle(lower):
    row = lax.broadcasted_iota(jnp.int32, (CHUNK, CHUNK), 0)
    col = lax.broadcasted_iota(jnp.int32, (CHUNK, CHUNK), 1)
    return (row >= col) if lower else (row <= col)


def eye(n):
    row = lax.broadcasted_iota(jnp.int32, (n, n), 0)
    col = lax.broadcasted_iota(jnp.int32, (n, n), 1)
    return row == col


def column_of(row):
    n = row.shape[1]
    return jnp.sum(jnp.where(eye(n), jnp.broadcast_to(row, (n, n)), 0.0), axis=1, keepdims=True)


def row_of(column):
    n = column.shape[0]
    return jnp.sum(jnp.where(eye(n), jnp.broadcast_to(column, (n, n)), 0.0), axis=0, keepdims=True)


def span_of(c):
    return slice(c * CHUNK, (c + 1) * CHUNK)


def inputs_and_outputs():
    return ("x_hbm", "g_hbm", "raw_hbm", "bias_hbm", "rate_hbm", "skip_hbm", "b_hbm", "c_hbm",
            "gx", "graw", "ztot", "grate", "gskip", "gbias")


def scratch_of(heads, tokens, size, state, peers):
    groups, chunks, chips = heads // GROUP, tokens // CHUNK, peers // 2
    wide, half = GROUP * size, size // 2
    vmem = pltpu.VMEM
    dma = pltpu.SemaphoreType.DMA
    halves = (2, groups, GROUP, half, state)
    segments = (2, tokens, state)
    return dict(
        raw=vmem((heads, tokens), F32),
        bias=vmem((1, heads), F32),
        rate=vmem((1, heads), F32),
        skip=vmem((1, heads), F32),
        b=vmem((tokens, state), BF16),
        c=vmem((tokens, state), BF16),
        src=vmem((2, groups, tokens, wide), BF16),
        xt=vmem((groups, wide, tokens), BF16),
        gt=vmem((groups, wide, tokens), BF16),
        dt=vmem((heads, tokens), F32),
        cum=vmem((heads, tokens), F32),
        scale=vmem((2, heads, tokens), F32),
        step=vmem((chunks, heads, CHUNK), F32),
        edge=vmem((2, chunks, heads, CHUNK), F32),
        whole=vmem((heads, CHUNK), F32),
        skips=vmem((heads, CHUNK), F32),
        local=vmem((2, groups, chunks, wide, state), F32),
        total=vmem((2, groups, GROUP, size, state), F32),
        ends=vmem((peers, heads, CHUNK), F32),
        end_rows=vmem((peers, 1, heads), F32),
        coef=vmem((2, chips, heads, CHUNK), F32),
        pair_in=vmem(halves, F32),
        agg=vmem(halves, F32),
        chip_in=vmem((chips,) + halves[1:], F32),
        pre=vmem(halves, F32),
        post=vmem(halves[1:], F32),
        link=vmem((heads, CHUNK), F32),
        give=vmem(halves, F32),
        state_in=vmem((2, groups, GROUP, size, state), F32),
        dxt=vmem((groups, chunks, wide, CHUNK), F32),
        row=vmem((groups, chunks, GROUP, CHUNK), F32),
        col=vmem((groups, chunks, GROUP, CHUNK), F32),
        cross=vmem((groups, GROUP, CHUNK), F32),
        dg=vmem((chunks, CHUNK, CHUNK), F32),
        parts=vmem((2, groups, chunks, 2, wide, state), BF16),
        zown=vmem(segments, F32),
        zsum=vmem(segments, F32),
        zin=vmem((2,) + segments, F32),
        params_in=vmem((peers, heads, CHUNK), F32),
        small_sem=dma((6,)),
        load_sem=dma((2, groups)),
        end_send=dma(()),
        end_recv=dma((2,)),
        pair_send=dma(()),
        pair_recv=dma((2, groups)),
        chip_send=dma((chips,)),
        chip_recv=dma((chips - 1, groups)),
        back_send=dma(()),
        back_recv=dma((2, groups)),
        in_send=dma(()),
        out_send=dma(()),
        z_recv=dma((2, 3 * chunks)),
        param_send=dma(()),
        param_recv=dma(()),
    )


def kernel(names, peers, line, *refs):
    k = types.SimpleNamespace(**dict(zip(names, refs)))
    heads, tokens = k.raw.shape
    state = k.b.shape[1]
    groups, chunks, chips = heads // GROUP, tokens // CHUNK, peers // 2
    wide = k.src.shape[3]
    size = wide // GROUP
    half = size // 2
    me, zpos = lax.axis_index("ctx"), lax.axis_index("head")
    odd, chip = me % 2, me // 2
    mate = me + 1 - 2 * odd
    mate_step = jnp.where(odd == 1, 1, peers - 1)
    early = jnp.where(chip < chips // 2, 0, 1)
    late = 1 - early

    tree = chips == 4
    is_inner = jnp.logical_or(chip == 1, chip == 2)
    is_outer = jnp.logical_not(is_inner)
    inner_chip = jnp.where(chip < 2, 1, 2)
    pair_place = me + 2 - 4 * (chip % 2)
    across_place = me + 4 - 8 * (chip // 2)
    forwarded = groups // 2

    left = zpos < line // 2
    inner = jnp.where(left, zpos + 1, zpos - 1)
    outer = jnp.where(left, zpos - 1, zpos + 1)
    has_outer = jnp.logical_and(zpos > 0, zpos < line - 1)
    is_mid = jnp.logical_or(zpos == line // 2 - 1, zpos == line // 2)
    in_slot = jnp.where(is_mid, 1, 0)

    barrier = pltpu.get_barrier_semaphore()

    def remote(src, dst, send, recv, **place):
        return pltpu.make_async_remote_copy(
            src_ref=src, dst_ref=dst, send_sem=send, recv_sem=recv,
            device_id=place, device_id_type=MESH)

    def greet():
        for d in range(1, peers):
            pl.semaphore_signal(barrier, inc=1, device_id={"ctx": (me + d) % peers}, device_id_type=MESH)
        pl.semaphore_signal(barrier, inc=1, device_id={"head": inner}, device_id_type=MESH)

        @pl.when(has_outer)
        def _():
            pl.semaphore_signal(barrier, inc=1, device_id={"head": outer}, device_id_type=MESH)

    def met():
        pl.semaphore_wait(barrier, peers + jnp.where(has_outer, 1, 0))

    def load(e, group):
        at = pl.ds(pl.multiple_of(group * wide, wide), wide)
        return pltpu.make_async_copy((k.g_hbm, k.x_hbm)[e].at[:, at], k.src.at[e, group], k.load_sem.at[e, group])

    def small_loads():
        pairs = ((k.raw_hbm, k.raw), (k.bias_hbm, k.bias), (k.rate_hbm, k.rate), (k.skip_hbm, k.skip),
                 (k.b_hbm, k.b), (k.c_hbm, k.c))
        return [pltpu.make_async_copy(src, dst, k.small_sem.at[i]) for i, (src, dst) in enumerate(pairs)]

    def start_small():
        for copy in small_loads():
            copy.start()

    def start_loads(first, last):
        for group in range(first, last):
            load(1, group).start()
            load(0, group).start()

    def prepare():
        for copy in small_loads():
            copy.wait()
        start_loads(1, groups)
        dt = softplus(k.raw[...] + column_of(k.bias[...]))
        k.dt[...] = dt
        log_decay = -column_of(k.rate[...]) * dt
        ones = triangle(False).astype(F32)
        cums = [jnp.dot(log_decay[:, span_of(c)], ones, precision=HIGH) for c in range(chunks)]
        ends = [lanes(cum[:, CHUNK - 1:]) for cum in cums]
        before, after = jnp.zeros_like(ends[0]), jnp.zeros_like(ends[0])
        for c in range(chunks):
            k.edge[0, c] = jnp.exp(before)
            before = before + ends[c]
            k.edge[1, chunks - 1 - c] = jnp.exp(after)
            after = after + ends[chunks - 1 - c]
        k.whole[...] = jnp.exp(before)
        k.ends[me] = before
        k.end_rows[me] = row_of(before[:, 0:1])
        for c in range(chunks):
            k.cum[:, span_of(c)] = cums[c]
            k.scale[0, :, span_of(c)] = jnp.exp(cums[c])
            k.scale[1, :, span_of(c)] = jnp.exp(ends[c] - cums[c]) * dt[:, span_of(c)]
            k.step[c] = jnp.exp(ends[c])

    def end_copy(d, place):
        slot = jnp.where(d == peers - mate_step, 1, 0)
        return remote(k.end_rows.at[place], k.end_rows.at[place], k.end_send, k.end_recv.at[slot],
                      ctx=(me + d) % peers)

    def end_arrival(slot, count):
        some = k.end_rows.at[pl.ds(0, count)]
        remote(some, some, k.end_send, k.end_recv.at[slot], ctx=mate).wait_recv()

    def send_ends():
        for d in range(1, peers):
            end_copy(d, me).start()

    mine = pl.ds(pl.multiple_of(odd * half, half), half)
    theirs = pl.ds(pl.multiple_of((1 - odd) * half, half), half)

    def pair_copy(e, group):
        return remote(k.total.at[e, group, :, theirs, :], k.pair_in.at[e, group],
                      k.pair_send, k.pair_recv.at[e, group], ctx=mate)

    def chip_copy(step, group):
        what = jnp.where(chip + step < chips, 0, 1)
        return remote(k.agg.at[what, group], k.chip_in.at[step, group],
                      k.chip_send.at[step], k.chip_recv.at[step - 1, group], ctx=(me + 2 * step) % peers)

    def tree_copy(slot, group, source):
        place = across_place if slot == 2 else pair_place
        return remote(source, k.chip_in.at[slot, group],
                      k.chip_send.at[slot], k.chip_recv.at[slot - 1, group], ctx=place)

    def tree_arrival(slot, group):
        tree_copy(slot, group, k.post.at[group]).wait_recv()

    def tree_exchange(group):
        near = jnp.where(is_outer, early, late)
        if group < forwarded:
            tree_copy(1, group, k.agg.at[near, group]).start()
            return

        @pl.when(is_outer)
        def _():
            tree_copy(1, group, k.agg.at[early, group]).start()

        @pl.when(is_inner)
        def _():
            tree_copy(3, group, k.agg.at[early, group]).start()
            if group == groups - 1:
                for other in range(forwarded, groups):
                    tree_copy(1, other, k.agg.at[late, other]).start()

    def hand(group):
        link = k.link[rows_of(group)]

        @pl.when(is_inner)
        def _():
            tree_arrival(1, group)
            k.post[group] = k.agg[early, group] + scaled(link, k.chip_in[1, group])
            tree_copy(2, group, k.post.at[group]).start()

        if group >= forwarded:
            @pl.when(is_outer)
            def _():
                tree_arrival(3, group)
                k.post[group] = k.chip_in[3, group] + scaled(link, k.agg[early, group])
                tree_copy(2, group, k.post.at[group]).start()

    def forward(group):
        @pl.when(is_outer)
        def _():
            tree_arrival(2, group)
            tree_copy(3, group, k.chip_in.at[2, group]).start()

    def tree_early(group):
        @pl.when(is_inner)
        def _():
            k.pre[early, group] = k.chip_in[1, group]

        @pl.when(is_outer)
        def _():
            k.pre[early, group] = jnp.zeros((GROUP, half, state), F32)

        hand_back(early, group)

    def tree_late(group):
        @pl.when(is_inner)
        def _():
            slot = 3 if group < forwarded else 2
            tree_arrival(slot, group)
            k.pre[late, group] = k.chip_in[slot, group]

        @pl.when(is_outer)
        def _():
            tree_arrival(1, group)
            if group >= forwarded:
                tree_arrival(2, group)
            k.pre[late, group] = k.chip_in[1, group] + scaled(k.link[rows_of(group)], k.chip_in[2, group])

        hand_back(late, group)

    def sent(slot, count):
        some = k.chip_in.at[slot, pl.ds(0, count)]
        remote(some, some, k.chip_send.at[slot], k.chip_recv.at[slot - 1, 0], ctx=mate).wait_send()

    def tree_drain():
        sent(1, groups)

        @pl.when(is_inner)
        def _():
            sent(2, groups)
            if forwarded < groups:
                sent(3, groups - forwarded)

        @pl.when(is_outer)
        def _():
            if forwarded < groups:
                sent(2, groups - forwarded)
            if forwarded:
                sent(3, forwarded)

    def back_copy(e, group, rows):
        return remote(k.give.at[e, group], k.state_in.at[e, group, :, rows, :],
                      k.back_send, k.back_recv.at[e, group], ctx=mate)

    def rows_of(group):
        return pl.ds(pl.multiple_of(group * GROUP, GROUP), GROUP)

    def carry_local(e, group, order, source, operand):
        at_rows = rows_of(group)
        value = None
        for c in order:
            at = span_of(c)
            k.local[e, group, c] = jnp.zeros((wide, state), F32) if value is None else value
            high, low = split(per_head(k.scale[1 - e, at_rows, at], source[group, :, at].astype(F32)))
            added = mm(jnp.concatenate([high, low], axis=1), twice(operand[at, :], 0))
            value = added if value is None else per_head(k.step[c, at_rows], value) + added
        k.total[e, group] = value.reshape(GROUP, size, state)

    def states(group):
        load(1, group).wait()
        k.xt[group] = k.src[1, group].T
        carry_local(0, group, range(chunks), k.xt, k.b)

    def backs(group):
        load(0, group).wait()
        k.gt[group] = k.src[0, group].T
        carry_local(1, group, reversed(range(chunks)), k.gt, k.c)

    def make_coefs():
        if peers > 2:
            end_arrival(0, peers - 2)
            for d in range(peers):
                k.ends[d] = lanes(column_of(k.end_rows[d]))
        s_log = jnp.zeros((heads, CHUNK), F32)
        r_log = jnp.zeros((heads, CHUNK), F32)
        for step in range(1, chips):
            k.coef[0, step] = jnp.exp(s_log)
            k.coef[1, step] = jnp.exp(r_log)
            low = (chip - step + chips) % chips
            high = (chip + step) % chips
            s_log = s_log + (k.ends[2 * low] + k.ends[2 * low + 1])
            r_log = r_log + (k.ends[2 * high] + k.ends[2 * high + 1])
        if tree:
            k.link[...] = jnp.exp(k.ends[2 * inner_chip] + k.ends[2 * inner_chip + 1])

    def scaled(coef, block):
        return coef[:, None, :] * block

    def downstream(e):
        return jnp.where(e == 0, odd, 1 - odd) == 1

    def own_and_mate(group):
        at_rows = rows_of(group)
        own = jnp.exp(k.ends[me, at_rows])
        return own, jnp.exp(k.ends[mate, at_rows]), jnp.ones_like(own), jnp.zeros_like(own)

    def learn_mate():
        end_arrival(1, 1)
        k.ends[mate] = lanes(column_of(k.end_rows[mate]))
        k.skips[...] = lanes(column_of(k.skip[...]))

    def combine(e, group):
        own_e, mate_e, one, _ = own_and_mate(group)
        down = downstream(e)
        pair_copy(e, group).wait_recv()
        k.agg[e, group] = (scaled(jnp.where(down, one, mate_e), k.total[e, group, :, mine, :])
                           + scaled(jnp.where(down, own_e, one), k.pair_in[e, group]))

    def gather(e, group):
        at_rows = rows_of(group)
        k.pre[e, group] = jnp.zeros((GROUP, half, state), F32)
        for step in range(1, chips):
            slot = jnp.where(e == 0, step, chips - step)

            @pl.when(jnp.where(e == 0, chip, chips - 1 - chip) >= step)
            def _():
                chip_copy(slot, group).wait_recv()
                k.pre[e, group] += scaled(k.coef[e, step, at_rows], k.chip_in[slot, group])

        hand_back(e, group)

    def hand_back(e, group):
        own_e, mate_e, one, zero = own_and_mate(group)
        down = downstream(e)
        pre = k.pre[e, group]
        k.give[e, group] = (scaled(jnp.where(down, one, own_e), pre)
                            + scaled(jnp.where(down, zero, one), k.total[e, group, :, mine, :]))
        k.state_in[e, group, :, mine, :] = (scaled(jnp.where(down, mate_e, one), pre)
                                            + scaled(jnp.where(down, one, zero), k.pair_in[e, group]))
        back_copy(e, group, mine).start()

    causal = triangle(False)

    def within(group):
        for c in range(chunks):
            at = span_of(c)
            scores = mm_nt(k.b[at, :], k.c[at, :])
            dt = k.dt[rows_of(group), at]
            cum = k.cum[rows_of(group), at] * LOG2_E
            shifted = (cum - jnp.log2(dt)).T
            total = k.dg[c] if group else jnp.zeros((CHUNK, CHUNK), F32)
            rows, cols = [], []
            for pair in range(GROUP // 2):
                x_pair = k.src[1, group, at, pair * 2 * size:(pair + 1) * 2 * size]
                places = [slice((2 * pair + j) * size, (2 * pair + j + 1) * size) for j in range(2)]
                products = mm(x_pair, pair_blocks(k.gt[group, places[0], at], k.gt[group, places[1], at]))
                for j in range(2):
                    h = 2 * pair + j
                    gap = cum[h:h + 1, :] - shifted[:, h:h + 1]
                    decay = jnp.exp2(jnp.where(causal, gap, -1e30))
                    both = products[:, j * CHUNK:(j + 1) * CHUNK] * decay
                    total = total + both
                    rows.append(jnp.sum(both * scores, axis=0, keepdims=True))
                    high, low = split(decay * scores)
                    dx_h = mm_nt(twice(k.gt[group, places[j], at], 1), jnp.concatenate([high, low], axis=1))
                    k.dxt[group, c, places[j], :] = dx_h
                    x_h = k.xt[group, places[j], at]
                    cols.append(jnp.sum(dx_h * x_h.astype(F32), axis=0, keepdims=True))
            k.row[group, c] = jnp.concatenate(rows, axis=0)
            k.col[group, c] = jnp.concatenate(cols, axis=0)
            k.dg[c] = total

    def score_parts():
        for c in range(chunks):
            at = span_of(c)
            for e, dg, operand in ((0, k.dg[c].T, k.b), (1, k.dg[c], k.c)):
                high, low = split(dg)
                k.zown[e, at] = mm(jnp.concatenate([high, low], axis=1), twice(operand[at, :], 0))

    def projections(e, c, members):
        at = span_of(c)
        total = k.zown[e, at]
        for group in members:
            if c == 0:
                back_copy(e, group, theirs).wait_recv()
            at_rows = rows_of(group)
            incoming = k.state_in[e, group].reshape(wide, state)
            high, low = split(per_head(k.edge[e, c, at_rows], incoming) + k.local[e, group, c])
            k.parts[e, group, c, 0] = high
            k.parts[e, group, c, 1] = low
            column = k.scale[e, at_rows, at].T
            for pair in range(GROUP // 2):
                wide_at = slice(pair * 2 * size, (pair + 1) * 2 * size)
                one = slice(2 * pair * size, (2 * pair + 1) * size)
                two = slice((2 * pair + 1) * size, (2 * pair + 2) * size)
                both = mm(twice(k.src[e, group, at, wide_at], 1),
                          jnp.concatenate([pair_blocks(high[one], high[two]),
                                           pair_blocks(low[one], low[two])], axis=0))
                for j in range(2):
                    h = 2 * pair + j
                    total = total + both[:, j * state:(j + 1) * state] * column[:, h:h + 1]
        k.zown[e, at] = total

    pieces = [(early, slice(c * CHUNK, (c + 1) * CHUNK)) for c in range(chunks)]
    pieces += [(late, slice(r * (CHUNK // 2), (r + 1) * (CHUNK // 2))) for r in range(2 * chunks)]

    def inward(n, source):
        e, at = pieces[n]
        return remote(source.at[e, at], k.zin.at[in_slot, e, at], k.in_send, k.z_recv.at[in_slot, n], head=inner)

    def outward(n, slot=1):
        e, at = pieces[n]
        return remote(k.ztot.at[e, at], k.zin.at[slot, e, at], k.out_send, k.z_recv.at[slot, n], head=outer)

    def publish(first, last):
        @pl.when(jnp.logical_not(has_outer))
        def _():
            for n in range(first, last):
                inward(n, k.zown).start()

    def relay(n):
        e, at = pieces[n]

        @pl.when(has_outer)
        def _():
            outward(n, 0).wait_recv()
            k.zsum[e, at] = k.zown[e, at] + k.zin[0, e, at]
            inward(n, k.zsum).start()

    def settle(n):
        e, at = pieces[n]
        outward(n).wait_recv()

        @pl.when(jnp.logical_and(is_mid, has_outer))
        def _():
            k.ztot[e, at] = k.zsum[e, at] + k.zin[1, e, at]

        @pl.when(jnp.logical_and(is_mid, jnp.logical_not(has_outer)))
        def _():
            k.ztot[e, at] = k.zown[e, at] + k.zin[1, e, at]

        @pl.when(jnp.logical_not(is_mid))
        def _():
            k.ztot[e, at] = k.zin[1, e, at]

        @pl.when(has_outer)
        def _():
            outward(n).start()

    def settle_mid(n):
        @pl.when(is_mid)
        def _():
            settle(n)

    def settle_rest(n):
        @pl.when(jnp.logical_not(is_mid))
        def _():
            settle(n)

    def inputs_step(c, group):
        at, at_rows = span_of(c), rows_of(group)
        bb, cc = twice(k.b[at, :], 1), twice(k.c[at, :], 1)
        reach, weight = k.scale[0, at_rows, at], k.scale[1, at_rows, at]
        xt, gt = k.xt[group, :, at].astype(F32), k.gt[group, :, at].astype(F32)
        parts = [jnp.concatenate([k.parts[e, group, c, 0], k.parts[e, group, c, 1]], axis=1) for e in range(2)]
        y = mm_nt(parts[0], cc)
        k.row[group, c] += head_sums(y * gt, GROUP) * reach
        dx = per_head(weight, mm_nt(parts[1], bb))
        k.col[group, c] += head_sums(dx * xt, GROUP)
        product = head_sums(xt * gt, GROUP)
        k.cross[group] = product if c == 0 else k.cross[group] + product
        dx = dx + k.dxt[group, c] + per_head(k.skips[at_rows], gt)
        k.gx[group, at] = dx.astype(BF16).T

    def step_sizes():
        rate, bias = column_of(k.rate[...]), column_of(k.bias[...])
        beyond = []
        for group in range(groups):
            last = k.total[0, group] + scaled(k.whole[rows_of(group)], k.state_in[0, group])
            sums = jnp.sum(last * k.state_in[1, group], axis=1)
            beyond.append(jnp.sum(sums, axis=1, keepdims=True))
        beyond = lanes(jnp.concatenate(beyond, axis=0))
        suffix = triangle(True).astype(F32)
        g_rate = jnp.zeros((heads, 1), F32)
        g_bias = jnp.zeros((heads, 1), F32)
        for c in reversed(range(chunks)):
            at = span_of(c)
            row = jnp.concatenate([k.row[group, c] for group in range(groups)], axis=0)
            col = jnp.concatenate([k.col[group, c] for group in range(groups)], axis=0)
            change = row - col
            d_log = jnp.dot(change, suffix, precision=HIGH) + beyond
            beyond = beyond + lanes(jnp.sum(change, axis=1, keepdims=True))
            dt = k.dt[:, at]
            g_dt = col / dt - rate * d_log
            g_raw = g_dt / (1.0 + jnp.exp(-(k.raw[:, at] + bias)))
            k.graw[:, at] = g_raw
            g_rate = g_rate - jnp.sum(dt * d_log, axis=1, keepdims=True)
            g_bias = g_bias + jnp.sum(g_raw, axis=1, keepdims=True)
        cross = jnp.concatenate([k.cross[group] for group in range(groups)], axis=0)
        g_skip = jnp.sum(cross, axis=1, keepdims=True)
        lane = lax.broadcasted_iota(jnp.int32, (heads, CHUNK), 1)
        k.params_in[me] = jnp.where(lane == 0, g_rate, jnp.where(lane == 1, g_skip, g_bias))

    def params_copy(d, place):
        return remote(k.params_in.at[place], k.params_in.at[place], k.param_send, k.param_recv,
                      ctx=(me + d) % peers)

    def every_param():
        some = k.params_in.at[pl.ds(0, peers - 1)]
        return remote(some, some, k.param_send, k.param_recv, ctx=mate)

    def gather_params():
        every_param().wait_recv()
        total = k.params_in[0]
        for d in range(1, peers):
            total = total + k.params_in[d]
        k.grate[...] = row_of(total[:, 0:1])
        k.gskip[...] = row_of(total[:, 1:2])
        k.gbias[...] = row_of(total[:, 2:3])

    def nth_step(n):
        return jnp.where(chip < chips // 2, n, chips - n)

    def exchange(group):
        if group:
            combine(0, group)
            combine(1, group)
        if tree:
            tree_exchange(group)
            return
        for n in range(1, chips):
            chip_copy(nth_step(n), group).start()

    start_small()
    start_loads(0, 1)
    greet()
    prepare()
    met()
    send_ends()
    def forth(group):
        states(group)
        pair_copy(0, group).start()

    def back(group):
        backs(group)
        pair_copy(1, group).start()

    @pl.when(chip % 2 == 0)
    def _():
        forth(0)
        back(0)

    @pl.when(chip % 2 == 1)
    def _():
        back(0)
        forth(0)

    learn_mate()
    forerunner = chip % 2
    combine(forerunner, 0)
    if tree and forwarded:
        exchange(0)
    for group in range(1, groups):
        forth(group)
        if group == 1:
            combine(1 - forerunner, 0)
            if not tree:
                exchange(0)
        back(group)
        if group > 1:
            exchange(group - 1)
    if groups == 1:
        combine(1 - forerunner, 0)

    relayed, settled = 0, 0

    def tend(relays, settles):
        nonlocal relayed, settled
        while relayed < min(relays, len(pieces)):
            relay(relayed)
            relayed += 1
        while settled < min(settles, relayed):
            settle_mid(settled)
            settled += 1

    everyone = list(range(groups))
    if tree:
        handed, returned, passed = 0, 0, 0

        def pass_on(hands, returns, forwards):
            nonlocal handed, returned, passed
            while handed < min(hands, groups):
                hand(handed)
                handed += 1
            while returned < min(returns, groups):
                tree_early(returned)
                returned += 1
            while passed < min(forwards, forwarded):
                forward(passed)
                passed += 1

        for group in everyone:
            within(group)
            if group == 0:
                exchange(groups - 1)
                make_coefs()
            pass_on(HANDS[min(group, 3)], HANDS[min(group, 3)], 0)
        score_parts()
        first = everyone[:groups - 2]
        pass_on(groups - 1, groups - 1, 1)
        for c in range(chunks):
            projections(early, c, first)
        pass_on(groups, groups, groups)
        sooner = everyone[0::2][:groups - 1]
        later = [group for group in everyone if group not in sooner]
        for c in range(chunks):
            if c == chunks - 1:
                for group in sooner:
                    tree_late(group)
            projections(early, c, everyone[len(first):])
            publish(c, c + 1)
            if c == 0:
                pass_on(groups, groups, groups)
        for c in range(chunks):
            projections(late, c, sooner)
            if c == chunks // 2 - 1:
                tend(1, 0)
                for group in later:
                    tree_late(group)
            tend(max(0, c - 1), 0)
        for c in range(chunks):
            projections(late, c, later)
            publish(chunks + 2 * c, chunks + 2 * c + 2)
            tend((3, 3, 3, 4)[min(c, 3)], 0)
    else:
        for group in everyone:
            within(group)
            if group == 0:
                exchange(groups - 1)
                make_coefs()
        score_parts()
        for e in (early, late):
            for group in everyone:
                gather(e, group)
            for c in range(chunks):
                projections(e, c, everyone)
        publish(0, len(pieces))
        tend(chunks, 1)
    turns = [(c, group) for c in range(chunks) for group in everyone]
    for j, turn in enumerate(turns):
        inputs_step(*turn)
        part = 16 * (j + 1) // len(turns)
        for at, relays, settles in LATE_TURNS:
            if part >= at:
                tend(chunks + relays, settles)
    step_sizes()
    for d in range(1, peers):
        params_copy(d, me).start()
    tend(len(pieces), len(pieces))
    for n in range(len(pieces)):
        settle_rest(n)
    gather_params()

    def drain():
        remote(k.pair_in, k.pair_in, k.pair_send, k.pair_recv.at[0, 0], ctx=mate).wait_send()
        remote(k.give, k.give, k.back_send, k.back_recv.at[0, 0], ctx=mate).wait_send()
        if tree:
            tree_drain()
        else:
            for step in range(1, chips):
                sent(step, groups)
        remote(k.zown, k.zown, k.in_send, k.z_recv.at[0, 0], head=inner).wait_send()

        @pl.when(has_outer)
        def _():
            remote(k.zown, k.zown, k.out_send, k.z_recv.at[0, 0], head=outer).wait_send()

        some = k.end_rows.at[pl.ds(0, peers - 1)]
        remote(some, some, k.end_send, k.end_recv.at[0], ctx=mate).wait_send()
        every_param().wait_send()

    drain()


def finish_kernel(groups, gx, graw, ztot, grate, gskip, gbias,
                  gx_out, graw_out, gb_out, gc_out, grate_out, gskip_out, gbias_out, sems):
    wide = gx.shape[2]
    copies = [(gx.at[group], gx_out.at[:, group * wide:(group + 1) * wide]) for group in range(groups)]
    copies += [(ztot.at[1], gb_out), (ztot.at[0], gc_out), (graw, graw_out), (grate, grate_out), (gskip, gskip_out), (gbias, gbias_out)]
    copies = [pltpu.make_async_copy(src, dst, sems.at[i]) for i, (src, dst) in enumerate(copies)]
    for copy in copies:
        copy.start()
    for copy in copies:
        copy.wait()


def on_device(peers, line, tokens_x, raw_dt, in_b, in_c, decay_rate, skip_gain, step_bias, grad_y):
    heads, tokens = raw_dt.shape
    width = tokens_x.shape[1]
    size = width // heads
    state = in_b.shape[1]
    groups = heads // GROUP
    scratch = scratch_of(heads, tokens, size, state, peers)
    names = inputs_and_outputs() + tuple(scratch)

    def shape(*dims, dtype=F32):
        return jax.ShapeDtypeStruct(dims, dtype)

    hbm, vmem = pl.BlockSpec(memory_space=pl.ANY), pl.BlockSpec(memory_space=pltpu.VMEM)
    row = shape(1, heads)
    results = pl.pallas_call(
        functools.partial(kernel, names, peers, line),
        in_specs=[pl.BlockSpec(memory_space=pltpu.HBM)] * 8,
        out_specs=[vmem] * 6,
        out_shape=[shape(groups, tokens, GROUP * size, dtype=BF16), shape(heads, tokens),
                   shape(2, tokens, state), row, row, row],
        scratch_shapes=list(scratch.values()),
        compiler_params=pltpu.CompilerParams(
            collective_id=0, has_side_effects=True, vmem_limit_bytes=VMEM_LIMIT),
        name="layer",
    )(*[pltpu.with_memory_space_constraint(a, pltpu.HBM) for a in (
        tokens_x, grad_y, raw_dt, step_bias[None], decay_rate[None], skip_gain[None], in_b, in_c)])
    gx, graw, gb, gc, grate, gskip, gbias = pl.pallas_call(
        functools.partial(finish_kernel, groups),
        in_specs=[vmem] * 6,
        out_specs=[hbm] * 7,
        out_shape=[shape(tokens, width, dtype=BF16), shape(heads, tokens), shape(tokens, state),
                   shape(tokens, state), row, row, row],
        scratch_shapes=[pltpu.SemaphoreType.DMA((groups + 6,))],
        compiler_params=pltpu.CompilerParams(vmem_limit_bytes=4 << 20),
        name="finish",
    )(*results)
    return gx, graw, gb, gc, grate[0], gskip[0], gbias[0]


def solution(mesh):
    return jax.shard_map(
        functools.partial(on_device, mesh.shape["ctx"], mesh.shape["head"]),
        mesh=mesh,
        in_specs=(
            P("ctx", "head"),
            P("head", "ctx"),
            P("ctx", None),
            P("ctx", None),
            P("head"),
            P("head"),
            P("head"),
            P("ctx", "head"),
        ),
        out_specs=(
            P("ctx", "head"),
            P("head", "ctx"),
            P("ctx", None),
            P("ctx", None),
            P("head"),
            P("head"),
            P("head"),
        ),
        check_vma=False,
    )
```

```python
import functools
import types

import jax
import jax.numpy as jnp
from jax import lax
from jax.experimental import pallas as pl
from jax.experimental.pallas import tpu as pltpu
from jax.sharding import PartitionSpec as P

CHUNK = 128
GROUP = 8
F32 = jnp.float32
BF16 = jnp.bfloat16
HIGH = lax.Precision.HIGHEST
NT = (((1,), (1,)), ((), ()))
MESH = pl.DeviceIdType.MESH
VMEM_LIMIT = 50 << 20
LOG2_E = 1.4426950408889634
HANDS = (1, 1, 2, 2)
LATE_TURNS = ((1, 0, 1), (2, 1, 1), (4, 2, 2), (6, 3, 2), (8, 4, 2), (9, 4, 3), (10, 5, 3), (12, 6, 3), (13, 6, 4), (14, 7, 4), (16, 8, 5))


def mm(a, b):
    return jnp.dot(a, b, preferred_element_type=F32)


def mm_nt(a, b):
    return lax.dot_general(a, b, NT, preferred_element_type=F32)


def split(a):
    high = a.astype(BF16)
    return high, (a - high.astype(F32)).astype(BF16)


def twice(a, axis):
    return jnp.concatenate([a, a], axis=axis)


def softplus(v):
    return jnp.maximum(v, 0.0) + jnp.log1p(jnp.exp(-jnp.abs(v)))


def lanes(column, width=CHUNK):
    return jnp.broadcast_to(column, (column.shape[0], width))


def per_head(rows, matrix):
    heads = rows.shape[0]
    shaped = matrix.reshape(heads, matrix.shape[0] // heads, matrix.shape[1])
    return (shaped * rows[:, None, :]).reshape(matrix.shape)


def head_sums(matrix, heads):
    return jnp.sum(matrix.reshape(heads, matrix.shape[0] // heads, matrix.shape[1]), axis=1)


def pair_blocks(first, second):
    zero = jnp.zeros_like(first)
    return jnp.concatenate(
        [jnp.concatenate([first, zero], axis=1), jnp.concatenate([zero, second], axis=1)], axis=0
    )


def triangle(lower):
    row = lax.broadcasted_iota(jnp.int32, (CHUNK, CHUNK), 0)
    col = lax.broadcasted_iota(jnp.int32, (CHUNK, CHUNK), 1)
    return (row >= col) if lower else (row <= col)


def eye(n):
    row = lax.broadcasted_iota(jnp.int32, (n, n), 0)
    col = lax.broadcasted_iota(jnp.int32, (n, n), 1)
    return row == col


def column_of(row):
    n = row.shape[1]
    return jnp.sum(jnp.where(eye(n), jnp.broadcast_to(row, (n, n)), 0.0), axis=1, keepdims=True)


def row_of(column):
    n = column.shape[0]
    return jnp.sum(jnp.where(eye(n), jnp.broadcast_to(column, (n, n)), 0.0), axis=0, keepdims=True)


def span_of(c):
    return slice(c * CHUNK, (c + 1) * CHUNK)


def inputs_and_outputs():
    return ("x_hbm", "g_hbm", "raw_hbm", "bias_hbm", "rate_hbm", "skip_hbm", "b_hbm", "c_hbm",
            "gx", "graw", "ztot", "grate", "gskip", "gbias")


def scratch_of(heads, tokens, size, state, peers):
    groups, chunks, chips = heads // GROUP, tokens // CHUNK, peers // 2
    wide, half = GROUP * size, size // 2
    vmem = pltpu.VMEM
    dma = pltpu.SemaphoreType.DMA
    halves = (2, groups, GROUP, half, state)
    segments = (2, tokens, state)
    return dict(
        raw=vmem((heads, tokens), F32),
        bias=vmem((1, heads), F32),
        rate=vmem((1, heads), F32),
        skip=vmem((1, heads), F32),
        b=vmem((tokens, state), BF16),
        c=vmem((tokens, state), BF16),
        src=vmem((2, groups, tokens, wide), BF16),
        xt=vmem((groups, wide, tokens), BF16),
        gt=vmem((groups, wide, tokens), BF16),
        dt=vmem((heads, tokens), F32),
        cum=vmem((heads, tokens), F32),
        scale=vmem((2, heads, tokens), F32),
        step=vmem((chunks, heads, CHUNK), F32),
        edge=vmem((2, chunks, heads, CHUNK), F32),
        whole=vmem((heads, CHUNK), F32),
        skips=vmem((heads, CHUNK), F32),
        local=vmem((2, groups, chunks, wide, state), F32),
        total=vmem((2, groups, GROUP, size, state), F32),
        ends=vmem((peers, heads, CHUNK), F32),
        end_rows=vmem((peers, 1, heads), F32),
        coef=vmem((2, chips, heads, CHUNK), F32),
        pair_in=vmem(halves, F32),
        agg=vmem(halves, F32),
        chip_in=vmem((chips,) + halves[1:], F32),
        pre=vmem(halves, F32),
        post=vmem(halves[1:], F32),
        link=vmem((heads, CHUNK), F32),
        give=vmem(halves, F32),
        state_in=vmem((2, groups, GROUP, size, state), F32),
        dxt=vmem((groups, chunks, wide, CHUNK), F32),
        row=vmem((groups, chunks, GROUP, CHUNK), F32),
        col=vmem((groups, chunks, GROUP, CHUNK), F32),
        cross=vmem((groups, GROUP, CHUNK), F32),
        dg=vmem((chunks, CHUNK, CHUNK), F32),
        parts=vmem((2, groups, chunks, 2, wide, state), BF16),
        zown=vmem(segments, F32),
        zsum=vmem(segments, F32),
        zin=vmem((2,) + segments, F32),
        params_in=vmem((peers, heads, CHUNK), F32),
        small_sem=dma((6,)),
        load_sem=dma((2, groups)),
        end_send=dma(()),
        end_recv=dma((2,)),
        pair_send=dma(()),
        pair_recv=dma((2, groups)),
        chip_send=dma((chips,)),
        chip_recv=dma((chips - 1, groups)),
        back_send=dma(()),
        back_recv=dma((2, groups)),
        in_send=dma(()),
        out_send=dma(()),
        z_recv=dma((2, 3 * chunks)),
        param_send=dma(()),
        param_recv=dma(()),
    )


def kernel(names, peers, line, *refs):
    k = types.SimpleNamespace(**dict(zip(names, refs)))
    heads, tokens = k.raw.shape
    state = k.b.shape[1]
    groups, chunks, chips = heads // GROUP, tokens // CHUNK, peers // 2
    wide = k.src.shape[3]
    size = wide // GROUP
    half = size // 2
    me, zpos = lax.axis_index("ctx"), lax.axis_index("head")
    odd, chip = me % 2, me // 2
    mate = me + 1 - 2 * odd
    mate_step = jnp.where(odd == 1, 1, peers - 1)
    early = jnp.where(chip < chips // 2, 0, 1)
    late = 1 - early

    tree = chips == 4
    is_inner = jnp.logical_or(chip == 1, chip == 2)
    is_outer = jnp.logical_not(is_inner)
    inner_chip = jnp.where(chip < 2, 1, 2)
    pair_place = me + 2 - 4 * (chip % 2)
    across_place = me + 4 - 8 * (chip // 2)
    forwarded = groups // 2

    left = zpos < line // 2
    inner = jnp.where(left, zpos + 1, zpos - 1)
    outer = jnp.where(left, zpos - 1, zpos + 1)
    has_outer = jnp.logical_and(zpos > 0, zpos < line - 1)
    is_mid = jnp.logical_or(zpos == line // 2 - 1, zpos == line // 2)
    in_slot = jnp.where(is_mid, 1, 0)

    barrier = pltpu.get_barrier_semaphore()

    def remote(src, dst, send, recv, **place):
        return pltpu.make_async_remote_copy(
            src_ref=src, dst_ref=dst, send_sem=send, recv_sem=recv,
            device_id=place, device_id_type=MESH)

    def greet():
        for d in range(1, peers):
            pl.semaphore_signal(barrier, inc=1, device_id={"ctx": (me + d) % peers}, device_id_type=MESH)
        pl.semaphore_signal(barrier, inc=1, device_id={"head": inner}, device_id_type=MESH)

        @pl.when(has_outer)
        def _():
            pl.semaphore_signal(barrier, inc=1, device_id={"head": outer}, device_id_type=MESH)

    def met():
        pl.semaphore_wait(barrier, peers + jnp.where(has_outer, 1, 0))

    def load(e, group):
        at = pl.ds(pl.multiple_of(group * wide, wide), wide)
        return pltpu.make_async_copy((k.g_hbm, k.x_hbm)[e].at[:, at], k.src.at[e, group], k.load_sem.at[e, group])

    def small_loads():
        pairs = ((k.raw_hbm, k.raw), (k.bias_hbm, k.bias), (k.rate_hbm, k.rate),
                 (k.b_hbm, k.b), (k.c_hbm, k.c), (k.skip_hbm, k.skip))
        return [pltpu.make_async_copy(src, dst, k.small_sem.at[i]) for i, (src, dst) in enumerate(pairs)]

    def start_small(first, last):
        for copy in small_loads()[first:last]:
            copy.start()

    def wait_small(first, last):
        for copy in small_loads()[first:last]:
            copy.wait()

    def start_loads(first, last):
        for group in range(first, last):
            load(1, group).start()
            load(0, group).start()

    def prepare():
        wait_small(0, 3)
        start_loads(1, groups)
        dt = softplus(k.raw[...] + column_of(k.bias[...]))
        k.dt[...] = dt
        log_decay = -column_of(k.rate[...]) * dt
        ones = triangle(False).astype(F32)
        stacked = jnp.concatenate([log_decay[:, span_of(c)] for c in range(chunks)], axis=0)
        stacked = jnp.dot(stacked, ones, precision=HIGH)
        cums = [stacked[c * heads:(c + 1) * heads] for c in range(chunks)]
        ends = [lanes(cum[:, CHUNK - 1:]) for cum in cums]
        before, after = jnp.zeros_like(ends[0]), jnp.zeros_like(ends[0])
        for c in range(chunks):
            k.edge[0, c] = jnp.exp(before)
            before = before + ends[c]
            k.edge[1, chunks - 1 - c] = jnp.exp(after)
            after = after + ends[chunks - 1 - c]
        k.whole[...] = jnp.exp(before)
        k.ends[me] = before
        k.end_rows[me] = row_of(before[:, 0:1])
        for c in range(chunks):
            k.cum[:, span_of(c)] = cums[c]
            k.scale[0, :, span_of(c)] = jnp.exp(cums[c])
            k.scale[1, :, span_of(c)] = jnp.exp(ends[c] - cums[c]) * dt[:, span_of(c)]
            k.step[c] = jnp.exp(ends[c])

    def end_copy(d, place):
        slot = jnp.where(d == peers - mate_step, 1, 0)
        return remote(k.end_rows.at[place], k.end_rows.at[place], k.end_send, k.end_recv.at[slot],
                      ctx=(me + d) % peers)

    def end_arrival(slot, count):
        some = k.end_rows.at[pl.ds(0, count)]
        remote(some, some, k.end_send, k.end_recv.at[slot], ctx=mate).wait_recv()

    def send_ends():
        for d in range(1, peers):
            end_copy(d, me).start()

    mine = pl.ds(pl.multiple_of(odd * half, half), half)
    theirs = pl.ds(pl.multiple_of((1 - odd) * half, half), half)

    def pair_copy(e, group):
        return remote(k.total.at[e, group, :, theirs, :], k.pair_in.at[e, group],
                      k.pair_send, k.pair_recv.at[e, group], ctx=mate)

    def chip_copy(step, group):
        what = jnp.where(chip + step < chips, 0, 1)
        return remote(k.agg.at[what, group], k.chip_in.at[step, group],
                      k.chip_send.at[step], k.chip_recv.at[step - 1, group], ctx=(me + 2 * step) % peers)

    def tree_copy(slot, group, source):
        place = across_place if slot == 2 else pair_place
        return remote(source, k.chip_in.at[slot, group],
                      k.chip_send.at[slot], k.chip_recv.at[slot - 1, group], ctx=place)

    def tree_arrival(slot, group):
        tree_copy(slot, group, k.post.at[group]).wait_recv()

    def tree_exchange(group):
        near = jnp.where(is_outer, early, late)
        if group < forwarded:
            tree_copy(1, group, k.agg.at[near, group]).start()
            return

        @pl.when(is_outer)
        def _():
            tree_copy(1, group, k.agg.at[early, group]).start()

        @pl.when(is_inner)
        def _():
            tree_copy(3, group, k.agg.at[early, group]).start()
            if group == groups - 1:
                for other in range(forwarded, groups):
                    tree_copy(1, other, k.agg.at[late, other]).start()

    def hand(group):
        link = k.link[rows_of(group)]

        @pl.when(is_inner)
        def _():
            tree_arrival(1, group)
            k.post[group] = k.agg[early, group] + scaled(link, k.chip_in[1, group])
            tree_copy(2, group, k.post.at[group]).start()

        if group >= forwarded:
            @pl.when(is_outer)
            def _():
                tree_arrival(3, group)
                k.post[group] = k.chip_in[3, group] + scaled(link, k.agg[early, group])
                tree_copy(2, group, k.post.at[group]).start()

    def forward(group):
        @pl.when(is_outer)
        def _():
            tree_arrival(2, group)
            tree_copy(3, group, k.chip_in.at[2, group]).start()

    def tree_early(group):
        @pl.when(is_inner)
        def _():
            k.pre[early, group] = k.chip_in[1, group]

        @pl.when(is_outer)
        def _():
            k.pre[early, group] = jnp.zeros((GROUP, half, state), F32)

        hand_back(early, group)

    def tree_late(group):
        @pl.when(is_inner)
        def _():
            slot = 3 if group < forwarded else 2
            tree_arrival(slot, group)
            k.pre[late, group] = k.chip_in[slot, group]

        @pl.when(is_outer)
        def _():
            tree_arrival(1, group)
            if group >= forwarded:
                tree_arrival(2, group)
            k.pre[late, group] = k.chip_in[1, group] + scaled(k.link[rows_of(group)], k.chip_in[2, group])

        hand_back(late, group)

    def sent(slot, count):
        some = k.chip_in.at[slot, pl.ds(0, count)]
        remote(some, some, k.chip_send.at[slot], k.chip_recv.at[slot - 1, 0], ctx=mate).wait_send()

    def tree_drain():
        sent(1, groups)

        @pl.when(is_inner)
        def _():
            sent(2, groups)
            if forwarded < groups:
                sent(3, groups - forwarded)

        @pl.when(is_outer)
        def _():
            if forwarded < groups:
                sent(2, groups - forwarded)
            if forwarded:
                sent(3, forwarded)

    def back_copy(e, group, rows):
        return remote(k.give.at[e, group], k.state_in.at[e, group, :, rows, :],
                      k.back_send, k.back_recv.at[e, group], ctx=mate)

    def rows_of(group):
        return pl.ds(pl.multiple_of(group * GROUP, GROUP), GROUP)

    def carry_local(e, group, order, source, operand):
        at_rows = rows_of(group)
        value = None
        for c in order:
            at = span_of(c)
            k.local[e, group, c] = jnp.zeros((wide, state), F32) if value is None else value
            high, low = split(per_head(k.scale[1 - e, at_rows, at], source[group, :, at].astype(F32)))
            added = mm(jnp.concatenate([high, low], axis=1), twice(operand[at, :], 0))
            value = added if value is None else per_head(k.step[c, at_rows], value) + added
        k.total[e, group] = value.reshape(GROUP, size, state)

    def states(group):
        load(1, group).wait()
        k.xt[group] = k.src[1, group].T
        carry_local(0, group, range(chunks), k.xt, k.b)

    def backs(group):
        load(0, group).wait()
        k.gt[group] = k.src[0, group].T
        carry_local(1, group, reversed(range(chunks)), k.gt, k.c)

    def make_coefs():
        if peers > 2:
            end_arrival(0, peers - 2)
            for d in range(peers):
                k.ends[d] = lanes(column_of(k.end_rows[d]))
        s_log = jnp.zeros((heads, CHUNK), F32)
        r_log = jnp.zeros((heads, CHUNK), F32)
        for step in range(1, chips):
            k.coef[0, step] = jnp.exp(s_log)
            k.coef[1, step] = jnp.exp(r_log)
            low = (chip - step + chips) % chips
            high = (chip + step) % chips
            s_log = s_log + (k.ends[2 * low] + k.ends[2 * low + 1])
            r_log = r_log + (k.ends[2 * high] + k.ends[2 * high + 1])
        if tree:
            k.link[...] = jnp.exp(k.ends[2 * inner_chip] + k.ends[2 * inner_chip + 1])

    def scaled(coef, block):
        return coef[:, None, :] * block

    def downstream(e):
        return jnp.where(e == 0, odd, 1 - odd) == 1

    def own_and_mate(group):
        at_rows = rows_of(group)
        own = jnp.exp(k.ends[me, at_rows])
        return own, jnp.exp(k.ends[mate, at_rows]), jnp.ones_like(own), jnp.zeros_like(own)

    def learn_mate():
        end_arrival(1, 1)
        k.ends[mate] = lanes(column_of(k.end_rows[mate]))
        k.skips[...] = lanes(column_of(k.skip[...]))

    def combine(e, group):
        own_e, mate_e, one, _ = own_and_mate(group)
        down = downstream(e)
        pair_copy(e, group).wait_recv()
        k.agg[e, group] = (scaled(jnp.where(down, one, mate_e), k.total[e, group, :, mine, :])
                           + scaled(jnp.where(down, own_e, one), k.pair_in[e, group]))

    def gather(e, group):
        at_rows = rows_of(group)
        k.pre[e, group] = jnp.zeros((GROUP, half, state), F32)
        for step in range(1, chips):
            slot = jnp.where(e == 0, step, chips - step)

            @pl.when(jnp.where(e == 0, chip, chips - 1 - chip) >= step)
            def _():
                chip_copy(slot, group).wait_recv()
                k.pre[e, group] += scaled(k.coef[e, step, at_rows], k.chip_in[slot, group])

        hand_back(e, group)

    def hand_back(e, group):
        own_e, mate_e, one, zero = own_and_mate(group)
        down = downstream(e)
        pre = k.pre[e, group]
        k.give[e, group] = (scaled(jnp.where(down, one, own_e), pre)
                            + scaled(jnp.where(down, zero, one), k.total[e, group, :, mine, :]))
        k.state_in[e, group, :, mine, :] = (scaled(jnp.where(down, mate_e, one), pre)
                                            + scaled(jnp.where(down, one, zero), k.pair_in[e, group]))
        back_copy(e, group, mine).start()

    causal = triangle(False)

    def within(group):
        for c in range(chunks):
            at = span_of(c)
            scores = mm_nt(k.b[at, :], k.c[at, :])
            dt = k.dt[rows_of(group), at]
            cum = k.cum[rows_of(group), at] * LOG2_E
            shifted = (cum - jnp.log2(dt)).T
            total = k.dg[c] if group else jnp.zeros((CHUNK, CHUNK), F32)
            rows, cols = [], []
            for pair in range(GROUP // 2):
                x_pair = k.src[1, group, at, pair * 2 * size:(pair + 1) * 2 * size]
                places = [slice((2 * pair + j) * size, (2 * pair + j + 1) * size) for j in range(2)]
                products = mm(x_pair, pair_blocks(k.gt[group, places[0], at], k.gt[group, places[1], at]))
                for j in range(2):
                    h = 2 * pair + j
                    gap = cum[h:h + 1, :] - shifted[:, h:h + 1]
                    decay = jnp.exp2(jnp.where(causal, gap, -1e30))
                    both = products[:, j * CHUNK:(j + 1) * CHUNK] * decay
                    total = total + both
                    rows.append(jnp.sum(both * scores, axis=0, keepdims=True))
                    high, low = split(decay * scores)
                    dx_h = mm_nt(twice(k.gt[group, places[j], at], 1), jnp.concatenate([high, low], axis=1))
                    k.dxt[group, c, places[j], :] = dx_h
                    x_h = k.xt[group, places[j], at]
                    cols.append(jnp.sum(dx_h * x_h.astype(F32), axis=0, keepdims=True))
            k.row[group, c] = jnp.concatenate(rows, axis=0)
            k.col[group, c] = jnp.concatenate(cols, axis=0)
            k.dg[c] = total

    def score_parts():
        for c in range(chunks):
            at = span_of(c)
            for e, dg, operand in ((0, k.dg[c].T, k.b), (1, k.dg[c], k.c)):
                high, low = split(dg)
                k.zown[e, at] = mm(jnp.concatenate([high, low], axis=1), twice(operand[at, :], 0))

    def projections(e, c, members):
        at = span_of(c)
        total = k.zown[e, at]
        for group in members:
            if c == 0:
                back_copy(e, group, theirs).wait_recv()
            at_rows = rows_of(group)
            incoming = k.state_in[e, group].reshape(wide, state)
            high, low = split(per_head(k.edge[e, c, at_rows], incoming) + k.local[e, group, c])
            k.parts[e, group, c, 0] = high
            k.parts[e, group, c, 1] = low
            column = k.scale[e, at_rows, at].T
            for pair in range(GROUP // 2):
                wide_at = slice(pair * 2 * size, (pair + 1) * 2 * size)
                one = slice(2 * pair * size, (2 * pair + 1) * size)
                two = slice((2 * pair + 1) * size, (2 * pair + 2) * size)
                both = mm(twice(k.src[e, group, at, wide_at], 1),
                          jnp.concatenate([pair_blocks(high[one], high[two]),
                                           pair_blocks(low[one], low[two])], axis=0))
                for j in range(2):
                    h = 2 * pair + j
                    total = total + both[:, j * state:(j + 1) * state] * column[:, h:h + 1]
        k.zown[e, at] = total

    pieces = [(early, slice(c * CHUNK, (c + 1) * CHUNK)) for c in range(chunks)]
    pieces += [(late, slice(r * (CHUNK // 2), (r + 1) * (CHUNK // 2))) for r in range(2 * chunks)]

    def inward(n, source):
        e, at = pieces[n]
        return remote(source.at[e, at], k.zin.at[in_slot, e, at], k.in_send, k.z_recv.at[in_slot, n], head=inner)

    def outward(n, slot=1):
        e, at = pieces[n]
        return remote(k.ztot.at[e, at], k.zin.at[slot, e, at], k.out_send, k.z_recv.at[slot, n], head=outer)

    def publish(first, last):
        @pl.when(jnp.logical_not(has_outer))
        def _():
            for n in range(first, last):
                inward(n, k.zown).start()

    def relay(n):
        e, at = pieces[n]

        @pl.when(has_outer)
        def _():
            outward(n, 0).wait_recv()
            k.zsum[e, at] = k.zown[e, at] + k.zin[0, e, at]
            inward(n, k.zsum).start()

    def settle(n):
        e, at = pieces[n]
        outward(n).wait_recv()

        @pl.when(jnp.logical_and(is_mid, has_outer))
        def _():
            k.ztot[e, at] = k.zsum[e, at] + k.zin[1, e, at]

        @pl.when(jnp.logical_and(is_mid, jnp.logical_not(has_outer)))
        def _():
            k.ztot[e, at] = k.zown[e, at] + k.zin[1, e, at]

        @pl.when(jnp.logical_not(is_mid))
        def _():
            k.ztot[e, at] = k.zin[1, e, at]

        @pl.when(has_outer)
        def _():
            outward(n).start()

    def settle_mid(n):
        @pl.when(is_mid)
        def _():
            settle(n)

    def settle_rest(n):
        @pl.when(jnp.logical_not(is_mid))
        def _():
            settle(n)

    def inputs_step(c, group):
        at, at_rows = span_of(c), rows_of(group)
        bb, cc = twice(k.b[at, :], 1), twice(k.c[at, :], 1)
        reach, weight = k.scale[0, at_rows, at], k.scale[1, at_rows, at]
        xt, gt = k.xt[group, :, at].astype(F32), k.gt[group, :, at].astype(F32)
        parts = [jnp.concatenate([k.parts[e, group, c, 0], k.parts[e, group, c, 1]], axis=1) for e in range(2)]
        y = mm_nt(parts[0], cc)
        k.row[group, c] += head_sums(y * gt, GROUP) * reach
        dx = per_head(weight, mm_nt(parts[1], bb))
        k.col[group, c] += head_sums(dx * xt, GROUP)
        product = head_sums(xt * gt, GROUP)
        k.cross[group] = product if c == 0 else k.cross[group] + product
        dx = dx + k.dxt[group, c] + per_head(k.skips[at_rows], gt)
        k.gx[group, at] = dx.astype(BF16).T

    def step_sizes():
        rate, bias = column_of(k.rate[...]), column_of(k.bias[...])
        beyond = []
        for group in range(groups):
            last = k.total[0, group] + scaled(k.whole[rows_of(group)], k.state_in[0, group])
            sums = jnp.sum(last * k.state_in[1, group], axis=1)
            beyond.append(jnp.sum(sums, axis=1, keepdims=True))
        beyond = lanes(jnp.concatenate(beyond, axis=0))
        suffix = triangle(True).astype(F32)
        g_rate = jnp.zeros((heads, 1), F32)
        g_bias = jnp.zeros((heads, 1), F32)
        for c in reversed(range(chunks)):
            at = span_of(c)
            row = jnp.concatenate([k.row[group, c] for group in range(groups)], axis=0)
            col = jnp.concatenate([k.col[group, c] for group in range(groups)], axis=0)
            change = row - col
            d_log = jnp.dot(change, suffix, precision=HIGH) + beyond
            beyond = beyond + lanes(jnp.sum(change, axis=1, keepdims=True))
            dt = k.dt[:, at]
            g_dt = col / dt - rate * d_log
            g_raw = g_dt / (1.0 + jnp.exp(-(k.raw[:, at] + bias)))
            k.graw[:, at] = g_raw
            g_rate = g_rate - jnp.sum(dt * d_log, axis=1, keepdims=True)
            g_bias = g_bias + jnp.sum(g_raw, axis=1, keepdims=True)
        cross = jnp.concatenate([k.cross[group] for group in range(groups)], axis=0)
        g_skip = jnp.sum(cross, axis=1, keepdims=True)
        lane = lax.broadcasted_iota(jnp.int32, (heads, CHUNK), 1)
        k.params_in[me] = jnp.where(lane == 0, g_rate, jnp.where(lane == 1, g_skip, g_bias))

    def params_copy(d, place):
        return remote(k.params_in.at[place], k.params_in.at[place], k.param_send, k.param_recv,
                      ctx=(me + d) % peers)

    def every_param():
        some = k.params_in.at[pl.ds(0, peers - 1)]
        return remote(some, some, k.param_send, k.param_recv, ctx=mate)

    def gather_params():
        every_param().wait_recv()
        total = k.params_in[0]
        for d in range(1, peers):
            total = total + k.params_in[d]
        k.grate[...] = row_of(total[:, 0:1])
        k.gskip[...] = row_of(total[:, 1:2])
        k.gbias[...] = row_of(total[:, 2:3])

    def nth_step(n):
        return jnp.where(chip < chips // 2, n, chips - n)

    def exchange(group):
        if group:
            combine(0, group)
            combine(1, group)
        if tree:
            tree_exchange(group)
            return
        for n in range(1, chips):
            chip_copy(nth_step(n), group).start()

    start_small(0, 3)
    start_loads(0, 1)
    start_small(3, 6)
    greet()
    prepare()
    wait_small(3, 6)
    def forth(group):
        states(group)
        pair_copy(0, group).start()

    def back(group):
        backs(group)
        pair_copy(1, group).start()

    forerunner = chip % 2

    @pl.when(forerunner == 0)
    def _():
        states(0)

    @pl.when(forerunner == 1)
    def _():
        backs(0)

    met()
    pair_copy(forerunner, 0).start()
    send_ends()

    @pl.when(forerunner == 0)
    def _():
        backs(0)

    @pl.when(forerunner == 1)
    def _():
        states(0)

    pair_copy(1 - forerunner, 0).start()
    learn_mate()
    combine(forerunner, 0)
    if tree and forwarded:
        exchange(0)
    for group in range(1, groups):
        forth(group)
        if group == 1:
            combine(1 - forerunner, 0)
            if not tree:
                exchange(0)
        back(group)
        if group > 1:
            exchange(group - 1)
    if groups == 1:
        combine(1 - forerunner, 0)

    relayed, settled = 0, 0

    def tend(relays, settles):
        nonlocal relayed, settled
        while relayed < min(relays, len(pieces)):
            relay(relayed)
            relayed += 1
        while settled < min(settles, relayed):
            settle_mid(settled)
            settled += 1

    everyone = list(range(groups))
    if tree:
        handed, returned, passed = 0, 0, 0

        def pass_on(hands, returns, forwards):
            nonlocal handed, returned, passed
            while handed < min(hands, groups):
                hand(handed)
                handed += 1
            while returned < min(returns, groups):
                tree_early(returned)
                returned += 1
            while passed < min(forwards, forwarded):
                forward(passed)
                passed += 1

        for group in everyone:
            within(group)
            if group == 0:
                exchange(groups - 1)
                make_coefs()
            pass_on(HANDS[min(group, 3)], HANDS[min(group, 3)], 0)
        score_parts()
        first = everyone[:groups - 2]
        pass_on(groups - 1, groups - 1, 1)
        for c in range(chunks):
            projections(early, c, first)
        pass_on(groups, groups, groups)
        sooner = everyone[0::2][:groups - 1]
        later = [group for group in everyone if group not in sooner]
        for c in range(chunks):
            if c == chunks - 1:
                for group in sooner:
                    tree_late(group)
            projections(early, c, everyone[len(first):])
            publish(c, c + 1)
            if c == 0:
                pass_on(groups, groups, groups)
        for c in range(chunks):
            projections(late, c, sooner)
            if c == chunks // 2 - 1:
                tend(1, 0)
                for group in later:
                    tree_late(group)
            tend(max(0, c - 1), 0)
        for c in range(chunks):
            projections(late, c, later)
            publish(chunks + 2 * c, chunks + 2 * c + 2)
            tend((3, 3, 3, 4)[min(c, 3)], 0)
    else:
        for group in everyone:
            within(group)
            if group == 0:
                exchange(groups - 1)
                make_coefs()
        score_parts()
        for e in (early, late):
            for group in everyone:
                gather(e, group)
            for c in range(chunks):
                projections(e, c, everyone)
        publish(0, len(pieces))
        tend(chunks, 1)
    turns = [(c, group) for c in range(chunks) for group in everyone]
    for j, turn in enumerate(turns):
        inputs_step(*turn)
        part = 16 * (j + 1) // len(turns)
        for at, relays, settles in LATE_TURNS:
            if part >= at:
                tend(chunks + relays, settles)
    step_sizes()
    for d in range(1, peers):
        params_copy(d, me).start()
    tend(len(pieces), len(pieces))
    for n in range(len(pieces)):
        settle_rest(n)
    gather_params()

    def drain():
        remote(k.pair_in, k.pair_in, k.pair_send, k.pair_recv.at[0, 0], ctx=mate).wait_send()
        remote(k.give, k.give, k.back_send, k.back_recv.at[0, 0], ctx=mate).wait_send()
        if tree:
            tree_drain()
        else:
            for step in range(1, chips):
                sent(step, groups)
        remote(k.zown, k.zown, k.in_send, k.z_recv.at[0, 0], head=inner).wait_send()

        @pl.when(has_outer)
        def _():
            remote(k.zown, k.zown, k.out_send, k.z_recv.at[0, 0], head=outer).wait_send()

        some = k.end_rows.at[pl.ds(0, peers - 1)]
        remote(some, some, k.end_send, k.end_recv.at[0], ctx=mate).wait_send()
        every_param().wait_send()

    drain()


def finish_kernel(groups, gx, graw, ztot, grate, gskip, gbias,
                  gx_out, graw_out, gb_out, gc_out, grate_out, gskip_out, gbias_out, sems):
    wide = gx.shape[2]
    copies = [(gx.at[group], gx_out.at[:, group * wide:(group + 1) * wide]) for group in range(groups)]
    copies += [(ztot.at[1], gb_out), (ztot.at[0], gc_out), (graw, graw_out), (grate, grate_out), (gskip, gskip_out), (gbias, gbias_out)]
    copies = [pltpu.make_async_copy(src, dst, sems.at[i]) for i, (src, dst) in enumerate(copies)]
    for copy in copies:
        copy.start()
    for copy in copies:
        copy.wait()


def on_device(peers, line, tokens_x, raw_dt, in_b, in_c, decay_rate, skip_gain, step_bias, grad_y):
    heads, tokens = raw_dt.shape
    width = tokens_x.shape[1]
    size = width // heads
    state = in_b.shape[1]
    groups = heads // GROUP
    scratch = scratch_of(heads, tokens, size, state, peers)
    names = inputs_and_outputs() + tuple(scratch)

    def shape(*dims, dtype=F32):
        return jax.ShapeDtypeStruct(dims, dtype)

    hbm, vmem = pl.BlockSpec(memory_space=pl.ANY), pl.BlockSpec(memory_space=pltpu.VMEM)
    row = shape(1, heads)
    results = pl.pallas_call(
        functools.partial(kernel, names, peers, line),
        in_specs=[pl.BlockSpec(memory_space=pltpu.HBM)] * 8,
        out_specs=[vmem] * 6,
        out_shape=[shape(groups, tokens, GROUP * size, dtype=BF16), shape(heads, tokens),
                   shape(2, tokens, state), row, row, row],
        scratch_shapes=list(scratch.values()),
        compiler_params=pltpu.CompilerParams(
            collective_id=0, has_side_effects=True, vmem_limit_bytes=VMEM_LIMIT),
        name="layer",
    )(*[pltpu.with_memory_space_constraint(a, pltpu.HBM) for a in (
        tokens_x, grad_y, raw_dt, step_bias[None], decay_rate[None], skip_gain[None], in_b, in_c)])
    gx, graw, gb, gc, grate, gskip, gbias = pl.pallas_call(
        functools.partial(finish_kernel, groups),
        in_specs=[vmem] * 6,
        out_specs=[hbm] * 7,
        out_shape=[shape(tokens, width, dtype=BF16), shape(heads, tokens), shape(tokens, state),
                   shape(tokens, state), row, row, row],
        scratch_shapes=[pltpu.SemaphoreType.DMA((groups + 6,))],
        compiler_params=pltpu.CompilerParams(vmem_limit_bytes=4 << 20),
        name="finish",
    )(*results)
    return gx, graw, gb, gc, grate[0], gskip[0], gbias[0]


def solution(mesh):
    return jax.shard_map(
        functools.partial(on_device, mesh.shape["ctx"], mesh.shape["head"]),
        mesh=mesh,
        in_specs=(
            P("ctx", "head"),
            P("head", "ctx"),
            P("ctx", None),
            P("ctx", None),
            P("head"),
            P("head"),
            P("head"),
            P("ctx", "head"),
        ),
        out_specs=(
            P("ctx", "head"),
            P("head", "ctx"),
            P("ctx", None),
            P("ctx", None),
            P("head"),
            P("head"),
            P("head"),
        ),
        check_vma=False,
    )
```

```python
import functools
import types

import jax
import jax.numpy as jnp
from jax import lax
from jax.experimental import pallas as pl
from jax.experimental.pallas import tpu as pltpu
from jax.sharding import PartitionSpec as P

CHUNK = 128
GROUP = 8
F32 = jnp.float32
BF16 = jnp.bfloat16
HIGH = lax.Precision.HIGHEST
NT = (((1,), (1,)), ((), ()))
MESH = pl.DeviceIdType.MESH
VMEM_LIMIT = 50 << 20
LOG2_E = 1.4426950408889634
HANDS = (1, 1, 2, 2)
LATE_TURNS = ((1, 0, 1), (2, 1, 1), (4, 2, 2), (6, 3, 2), (8, 4, 2), (9, 4, 3), (10, 5, 3), (12, 6, 3), (13, 6, 4), (14, 7, 4), (16, 8, 5))


def mm(a, b):
    return jnp.dot(a, b, preferred_element_type=F32)


def mm_nt(a, b):
    return lax.dot_general(a, b, NT, preferred_element_type=F32)


def split(a):
    high = a.astype(BF16)
    return high, (a - high.astype(F32)).astype(BF16)


def twice(a, axis):
    return jnp.concatenate([a, a], axis=axis)


def softplus(v):
    return jnp.maximum(v, 0.0) + jnp.log1p(jnp.exp(-jnp.abs(v)))


def lanes(column, width=CHUNK):
    return jnp.broadcast_to(column, (column.shape[0], width))


def per_head(rows, matrix):
    heads = rows.shape[0]
    shaped = matrix.reshape(heads, matrix.shape[0] // heads, matrix.shape[1])
    return (shaped * rows[:, None, :]).reshape(matrix.shape)


def head_sums(matrix, heads):
    return jnp.sum(matrix.reshape(heads, matrix.shape[0] // heads, matrix.shape[1]), axis=1)


def pair_blocks(first, second):
    zero = jnp.zeros_like(first)
    return jnp.concatenate(
        [jnp.concatenate([first, zero], axis=1), jnp.concatenate([zero, second], axis=1)], axis=0
    )


def triangle(lower):
    row = lax.broadcasted_iota(jnp.int32, (CHUNK, CHUNK), 0)
    col = lax.broadcasted_iota(jnp.int32, (CHUNK, CHUNK), 1)
    return (row >= col) if lower else (row <= col)


def eye(n):
    row = lax.broadcasted_iota(jnp.int32, (n, n), 0)
    col = lax.broadcasted_iota(jnp.int32, (n, n), 1)
    return row == col


def column_of(row):
    n = row.shape[1]
    return jnp.sum(jnp.where(eye(n), jnp.broadcast_to(row, (n, n)), 0.0), axis=1, keepdims=True)


def row_of(column):
    n = column.shape[0]
    return jnp.sum(jnp.where(eye(n), jnp.broadcast_to(column, (n, n)), 0.0), axis=0, keepdims=True)


def span_of(c):
    return slice(c * CHUNK, (c + 1) * CHUNK)


def inputs_and_outputs():
    return ("x_hbm", "g_hbm", "raw_hbm", "bias_hbm", "rate_hbm", "skip_hbm", "b_hbm", "c_hbm",
            "gx", "graw", "ztot", "grate", "gskip", "gbias")


def scratch_of(heads, tokens, size, state, peers):
    groups, chunks, chips = heads // GROUP, tokens // CHUNK, peers // 2
    wide, half = GROUP * size, size // 2
    vmem = pltpu.VMEM
    dma = pltpu.SemaphoreType.DMA
    halves = (2, groups, GROUP, half, state)
    segments = (2, tokens, state)
    return dict(
        raw=vmem((heads, tokens), F32),
        bias=vmem((1, heads), F32),
        rate=vmem((1, heads), F32),
        skip=vmem((1, heads), F32),
        b=vmem((tokens, state), BF16),
        c=vmem((tokens, state), BF16),
        src=vmem((2, groups, tokens, wide), BF16),
        xt=vmem((groups, wide, tokens), BF16),
        gt=vmem((groups, wide, tokens), BF16),
        dt=vmem((heads, tokens), F32),
        cum=vmem((heads, tokens), F32),
        scale=vmem((2, heads, tokens), F32),
        step=vmem((chunks, heads, CHUNK), F32),
        edge=vmem((2, chunks, heads, CHUNK), F32),
        whole=vmem((heads, CHUNK), F32),
        skips=vmem((heads, CHUNK), F32),
        local=vmem((2, groups, chunks, wide, state), F32),
        total=vmem((2, groups, GROUP, size, state), F32),
        ends=vmem((peers, heads, CHUNK), F32),
        end_rows=vmem((peers, 1, heads), F32),
        coef=vmem((2, chips, heads, CHUNK), F32),
        pair_in=vmem(halves, F32),
        agg=vmem(halves, F32),
        chip_in=vmem((chips,) + halves[1:], F32),
        pre=vmem(halves, F32),
        post=vmem(halves[1:], F32),
        link=vmem((heads, CHUNK), F32),
        give=vmem(halves, F32),
        state_in=vmem((2, groups, GROUP, size, state), F32),
        dxt=vmem((groups, chunks, wide, CHUNK), F32),
        row=vmem((groups, chunks, GROUP, CHUNK), F32),
        col=vmem((groups, chunks, GROUP, CHUNK), F32),
        cross=vmem((groups, GROUP, CHUNK), F32),
        dg=vmem((chunks, CHUNK, CHUNK), F32),
        parts=vmem((2, groups, chunks, 2, wide, state), BF16),
        zown=vmem(segments, F32),
        zsum=vmem(segments, F32),
        zin=vmem((2,) + segments, F32),
        params_in=vmem((peers, heads, CHUNK), F32),
        small_sem=dma((6,)),
        load_sem=dma((2, groups)),
        end_send=dma(()),
        end_recv=dma((2,)),
        pair_send=dma(()),
        pair_recv=dma((2, groups)),
        chip_send=dma((chips,)),
        chip_recv=dma((chips - 1, groups)),
        back_send=dma(()),
        back_recv=dma((2, groups)),
        in_send=dma(()),
        out_send=dma(()),
        z_recv=dma((2, 3 * chunks)),
        param_send=dma(()),
        param_recv=dma(()),
    )


def kernel(names, peers, line, *refs):
    k = types.SimpleNamespace(**dict(zip(names, refs)))
    heads, tokens = k.raw.shape
    state = k.b.shape[1]
    groups, chunks, chips = heads // GROUP, tokens // CHUNK, peers // 2
    wide = k.src.shape[3]
    size = wide // GROUP
    half = size // 2
    me, zpos = lax.axis_index("ctx"), lax.axis_index("head")
    odd, chip = me % 2, me // 2
    mate = me + 1 - 2 * odd
    mate_step = jnp.where(odd == 1, 1, peers - 1)
    early = jnp.where(chip < chips // 2, 0, 1)
    late = 1 - early

    tree = chips == 4
    is_inner = jnp.logical_or(chip == 1, chip == 2)
    is_outer = jnp.logical_not(is_inner)
    inner_chip = jnp.where(chip < 2, 1, 2)
    pair_place = me + 2 - 4 * (chip % 2)
    across_place = me + 4 - 8 * (chip // 2)
    forwarded = groups // 2

    left = zpos < line // 2
    inner = jnp.where(left, zpos + 1, zpos - 1)
    outer = jnp.where(left, zpos - 1, zpos + 1)
    has_outer = jnp.logical_and(zpos > 0, zpos < line - 1)
    is_mid = jnp.logical_or(zpos == line // 2 - 1, zpos == line // 2)
    in_slot = jnp.where(is_mid, 1, 0)

    barrier = pltpu.get_barrier_semaphore()

    def remote(src, dst, send, recv, **place):
        return pltpu.make_async_remote_copy(
            src_ref=src, dst_ref=dst, send_sem=send, recv_sem=recv,
            device_id=place, device_id_type=MESH)

    def greet():
        for d in range(1, peers):
            pl.semaphore_signal(barrier, inc=1, device_id={"ctx": (me + d) % peers}, device_id_type=MESH)
        pl.semaphore_signal(barrier, inc=1, device_id={"head": inner}, device_id_type=MESH)

        @pl.when(has_outer)
        def _():
            pl.semaphore_signal(barrier, inc=1, device_id={"head": outer}, device_id_type=MESH)

    def met():
        pl.semaphore_wait(barrier, peers + jnp.where(has_outer, 1, 0))

    def load(e, group):
        at = pl.ds(pl.multiple_of(group * wide, wide), wide)
        return pltpu.make_async_copy((k.g_hbm, k.x_hbm)[e].at[:, at], k.src.at[e, group], k.load_sem.at[e, group])

    def small_loads():
        pairs = ((k.raw_hbm, k.raw), (k.bias_hbm, k.bias), (k.rate_hbm, k.rate),
                 (k.b_hbm, k.b), (k.c_hbm, k.c), (k.skip_hbm, k.skip))
        return [pltpu.make_async_copy(src, dst, k.small_sem.at[i]) for i, (src, dst) in enumerate(pairs)]

    def start_small(first, last):
        for copy in small_loads()[first:last]:
            copy.start()

    def wait_small(first, last):
        for copy in small_loads()[first:last]:
            copy.wait()

    def start_loads(first, last):
        for group in range(first, last):
            load(1, group).start()
            load(0, group).start()

    def prepare():
        wait_small(0, 3)
        start_loads(1, groups)
        dt = softplus(k.raw[...] + column_of(k.bias[...]))
        k.dt[...] = dt
        log_decay = -column_of(k.rate[...]) * dt
        ones = triangle(False).astype(F32)
        stacked = jnp.concatenate([log_decay[:, span_of(c)] for c in range(chunks)], axis=0)
        stacked = jnp.dot(stacked, ones, precision=HIGH)
        cums = [stacked[c * heads:(c + 1) * heads] for c in range(chunks)]
        ends = [lanes(cum[:, CHUNK - 1:]) for cum in cums]
        before, after = jnp.zeros_like(ends[0]), jnp.zeros_like(ends[0])
        for c in range(chunks):
            k.edge[0, c] = jnp.exp(before)
            before = before + ends[c]
            k.edge[1, chunks - 1 - c] = jnp.exp(after)
            after = after + ends[chunks - 1 - c]
        k.whole[...] = jnp.exp(before)
        k.ends[me] = before
        k.end_rows[me] = row_of(before[:, 0:1])
        for c in range(chunks):
            k.cum[:, span_of(c)] = cums[c]
            k.scale[0, :, span_of(c)] = jnp.exp(cums[c])
            k.scale[1, :, span_of(c)] = jnp.exp(ends[c] - cums[c]) * dt[:, span_of(c)]
            k.step[c] = jnp.exp(ends[c])

    def end_copy(d, place):
        slot = jnp.where(d == peers - mate_step, 1, 0)
        return remote(k.end_rows.at[place], k.end_rows.at[place], k.end_send, k.end_recv.at[slot],
                      ctx=(me + d) % peers)

    def end_arrival(slot, count):
        some = k.end_rows.at[pl.ds(0, count)]
        remote(some, some, k.end_send, k.end_recv.at[slot], ctx=mate).wait_recv()

    def send_ends():
        for d in range(1, peers):
            end_copy(d, me).start()

    mine = pl.ds(pl.multiple_of(odd * half, half), half)
    theirs = pl.ds(pl.multiple_of((1 - odd) * half, half), half)

    def pair_copy(e, group):
        return remote(k.total.at[e, group, :, theirs, :], k.pair_in.at[e, group],
                      k.pair_send, k.pair_recv.at[e, group], ctx=mate)

    def chip_copy(step, group):
        what = jnp.where(chip + step < chips, 0, 1)
        return remote(k.agg.at[what, group], k.chip_in.at[step, group],
                      k.chip_send.at[step], k.chip_recv.at[step - 1, group], ctx=(me + 2 * step) % peers)

    def tree_copy(slot, group, source):
        place = across_place if slot == 2 else pair_place
        return remote(source, k.chip_in.at[slot, group],
                      k.chip_send.at[slot], k.chip_recv.at[slot - 1, group], ctx=place)

    def tree_arrival(slot, group):
        tree_copy(slot, group, k.post.at[group]).wait_recv()

    def tree_exchange(group):
        near = jnp.where(is_outer, early, late)
        if group < forwarded:
            tree_copy(1, group, k.agg.at[near, group]).start()
            return

        @pl.when(is_outer)
        def _():
            tree_copy(1, group, k.agg.at[early, group]).start()

        @pl.when(is_inner)
        def _():
            tree_copy(3, group, k.agg.at[early, group]).start()
            if group == groups - 1:
                for other in range(forwarded, groups):
                    tree_copy(1, other, k.agg.at[late, other]).start()

    def hand(group):
        link = k.link[rows_of(group)]

        @pl.when(is_inner)
        def _():
            tree_arrival(1, group)
            k.post[group] = k.agg[early, group] + scaled(link, k.chip_in[1, group])
            tree_copy(2, group, k.post.at[group]).start()

        if group >= forwarded:
            @pl.when(is_outer)
            def _():
                tree_arrival(3, group)
                k.post[group] = k.chip_in[3, group] + scaled(link, k.agg[early, group])
                tree_copy(2, group, k.post.at[group]).start()

    def forward(group):
        @pl.when(is_outer)
        def _():
            tree_arrival(2, group)
            tree_copy(3, group, k.chip_in.at[2, group]).start()

    def tree_early(group):
        @pl.when(is_inner)
        def _():
            k.pre[early, group] = k.chip_in[1, group]

        @pl.when(is_outer)
        def _():
            k.pre[early, group] = jnp.zeros((GROUP, half, state), F32)

        hand_back(early, group)

    def tree_late(group):
        @pl.when(is_inner)
        def _():
            slot = 3 if group < forwarded else 2
            tree_arrival(slot, group)
            k.pre[late, group] = k.chip_in[slot, group]

        @pl.when(is_outer)
        def _():
            tree_arrival(1, group)
            if group >= forwarded:
                tree_arrival(2, group)
            k.pre[late, group] = k.chip_in[1, group] + scaled(k.link[rows_of(group)], k.chip_in[2, group])

        hand_back(late, group)

    def sent(slot, count):
        some = k.chip_in.at[slot, pl.ds(0, count)]
        remote(some, some, k.chip_send.at[slot], k.chip_recv.at[slot - 1, 0], ctx=mate).wait_send()

    def tree_drain():
        sent(1, groups)

        @pl.when(is_inner)
        def _():
            sent(2, groups)
            if forwarded < groups:
                sent(3, groups - forwarded)

        @pl.when(is_outer)
        def _():
            if forwarded < groups:
                sent(2, groups - forwarded)
            if forwarded:
                sent(3, forwarded)

    def back_copy(e, group, rows):
        return remote(k.give.at[e, group], k.state_in.at[e, group, :, rows, :],
                      k.back_send, k.back_recv.at[e, group], ctx=mate)

    def rows_of(group):
        return pl.ds(pl.multiple_of(group * GROUP, GROUP), GROUP)

    def carry_local(e, group, order, source, operand):
        at_rows = rows_of(group)
        value = None
        for c in order:
            at = span_of(c)
            k.local[e, group, c] = jnp.zeros((wide, state), F32) if value is None else value
            high, low = split(per_head(k.scale[1 - e, at_rows, at], source[group, :, at].astype(F32)))
            added = mm(jnp.concatenate([high, low], axis=1), twice(operand[at, :], 0))
            value = added if value is None else per_head(k.step[c, at_rows], value) + added
        k.total[e, group] = value.reshape(GROUP, size, state)

    def states(group):
        load(1, group).wait()
        k.xt[group] = k.src[1, group].T
        carry_local(0, group, range(chunks), k.xt, k.b)

    def backs(group):
        load(0, group).wait()
        k.gt[group] = k.src[0, group].T
        carry_local(1, group, reversed(range(chunks)), k.gt, k.c)

    def make_coefs():
        if peers > 2:
            end_arrival(0, peers - 2)
            for d in range(peers):
                k.ends[d] = lanes(column_of(k.end_rows[d]))
        s_log = jnp.zeros((heads, CHUNK), F32)
        r_log = jnp.zeros((heads, CHUNK), F32)
        for step in range(1, chips):
            k.coef[0, step] = jnp.exp(s_log)
            k.coef[1, step] = jnp.exp(r_log)
            low = (chip - step + chips) % chips
            high = (chip + step) % chips
            s_log = s_log + (k.ends[2 * low] + k.ends[2 * low + 1])
            r_log = r_log + (k.ends[2 * high] + k.ends[2 * high + 1])
        if tree:
            k.link[...] = jnp.exp(k.ends[2 * inner_chip] + k.ends[2 * inner_chip + 1])

    def scaled(coef, block):
        return coef[:, None, :] * block

    def downstream(e):
        return jnp.where(e == 0, odd, 1 - odd) == 1

    def own_and_mate(group):
        at_rows = rows_of(group)
        own = jnp.exp(k.ends[me, at_rows])
        return own, jnp.exp(k.ends[mate, at_rows]), jnp.ones_like(own), jnp.zeros_like(own)

    def learn_mate():
        end_arrival(1, 1)
        k.ends[mate] = lanes(column_of(k.end_rows[mate]))
        k.skips[...] = lanes(column_of(k.skip[...]))

    def combine(e, group):
        own_e, mate_e, one, _ = own_and_mate(group)
        down = downstream(e)
        pair_copy(e, group).wait_recv()
        k.agg[e, group] = (scaled(jnp.where(down, one, mate_e), k.total[e, group, :, mine, :])
                           + scaled(jnp.where(down, own_e, one), k.pair_in[e, group]))

    def gather(e, group):
        at_rows = rows_of(group)
        k.pre[e, group] = jnp.zeros((GROUP, half, state), F32)
        for step in range(1, chips):
            slot = jnp.where(e == 0, step, chips - step)

            @pl.when(jnp.where(e == 0, chip, chips - 1 - chip) >= step)
            def _():
                chip_copy(slot, group).wait_recv()
                k.pre[e, group] += scaled(k.coef[e, step, at_rows], k.chip_in[slot, group])

        hand_back(e, group)

    def hand_back(e, group):
        own_e, mate_e, one, zero = own_and_mate(group)
        down = downstream(e)
        pre = k.pre[e, group]
        k.give[e, group] = (scaled(jnp.where(down, one, own_e), pre)
                            + scaled(jnp.where(down, zero, one), k.total[e, group, :, mine, :]))
        k.state_in[e, group, :, mine, :] = (scaled(jnp.where(down, mate_e, one), pre)
                                            + scaled(jnp.where(down, one, zero), k.pair_in[e, group]))
        back_copy(e, group, mine).start()

    causal = triangle(False)

    def within(group, first=0, last=chunks):
        for c in range(first, last):
            at = span_of(c)
            scores = mm_nt(k.b[at, :], k.c[at, :])
            dt = k.dt[rows_of(group), at]
            cum = k.cum[rows_of(group), at] * LOG2_E
            shifted = (cum - jnp.log2(dt)).T
            total = k.dg[c] if group else jnp.zeros((CHUNK, CHUNK), F32)
            rows, cols = [], []
            for pair in range(GROUP // 2):
                x_pair = k.src[1, group, at, pair * 2 * size:(pair + 1) * 2 * size]
                places = [slice((2 * pair + j) * size, (2 * pair + j + 1) * size) for j in range(2)]
                products = mm(x_pair, pair_blocks(k.gt[group, places[0], at], k.gt[group, places[1], at]))
                for j in range(2):
                    h = 2 * pair + j
                    gap = cum[h:h + 1, :] - shifted[:, h:h + 1]
                    decay = jnp.exp2(jnp.where(causal, gap, -1e30))
                    both = products[:, j * CHUNK:(j + 1) * CHUNK] * decay
                    total = total + both
                    rows.append(jnp.sum(both * scores, axis=0, keepdims=True))
                    high, low = split(decay * scores)
                    dx_h = mm_nt(twice(k.gt[group, places[j], at], 1), jnp.concatenate([high, low], axis=1))
                    k.dxt[group, c, places[j], :] = dx_h
                    x_h = k.xt[group, places[j], at]
                    cols.append(jnp.sum(dx_h * x_h.astype(F32), axis=0, keepdims=True))
            k.row[group, c] = jnp.concatenate(rows, axis=0)
            k.col[group, c] = jnp.concatenate(cols, axis=0)
            k.dg[c] = total

    def score_parts():
        for c in range(chunks):
            at = span_of(c)
            for e, dg, operand in ((0, k.dg[c].T, k.b), (1, k.dg[c], k.c)):
                high, low = split(dg)
                k.zown[e, at] = mm(jnp.concatenate([high, low], axis=1), twice(operand[at, :], 0))

    def projections(e, c, members):
        at = span_of(c)
        total = k.zown[e, at]
        for group in members:
            if c == 0:
                back_copy(e, group, theirs).wait_recv()
            at_rows = rows_of(group)
            incoming = k.state_in[e, group].reshape(wide, state)
            high, low = split(per_head(k.edge[e, c, at_rows], incoming) + k.local[e, group, c])
            k.parts[e, group, c, 0] = high
            k.parts[e, group, c, 1] = low
            column = k.scale[e, at_rows, at].T
            for pair in range(GROUP // 2):
                wide_at = slice(pair * 2 * size, (pair + 1) * 2 * size)
                one = slice(2 * pair * size, (2 * pair + 1) * size)
                two = slice((2 * pair + 1) * size, (2 * pair + 2) * size)
                both = mm(twice(k.src[e, group, at, wide_at], 1),
                          jnp.concatenate([pair_blocks(high[one], high[two]),
                                           pair_blocks(low[one], low[two])], axis=0))
                for j in range(2):
                    h = 2 * pair + j
                    total = total + both[:, j * state:(j + 1) * state] * column[:, h:h + 1]
        k.zown[e, at] = total

    pieces = [(early, slice(c * CHUNK, (c + 1) * CHUNK)) for c in range(chunks)]
    pieces += [(late, slice(r * (CHUNK // 2), (r + 1) * (CHUNK // 2))) for r in range(2 * chunks)]

    def inward(n, source):
        e, at = pieces[n]
        return remote(source.at[e, at], k.zin.at[in_slot, e, at], k.in_send, k.z_recv.at[in_slot, n], head=inner)

    def outward(n, slot=1):
        e, at = pieces[n]
        return remote(k.ztot.at[e, at], k.zin.at[slot, e, at], k.out_send, k.z_recv.at[slot, n], head=outer)

    def publish(first, last):
        @pl.when(jnp.logical_not(has_outer))
        def _():
            for n in range(first, last):
                inward(n, k.zown).start()

    def relay(n):
        e, at = pieces[n]

        @pl.when(has_outer)
        def _():
            outward(n, 0).wait_recv()
            k.zsum[e, at] = k.zown[e, at] + k.zin[0, e, at]
            inward(n, k.zsum).start()

    def settle(n):
        e, at = pieces[n]
        outward(n).wait_recv()

        @pl.when(jnp.logical_and(is_mid, has_outer))
        def _():
            k.ztot[e, at] = k.zsum[e, at] + k.zin[1, e, at]

        @pl.when(jnp.logical_and(is_mid, jnp.logical_not(has_outer)))
        def _():
            k.ztot[e, at] = k.zown[e, at] + k.zin[1, e, at]

        @pl.when(jnp.logical_not(is_mid))
        def _():
            k.ztot[e, at] = k.zin[1, e, at]

        @pl.when(has_outer)
        def _():
            outward(n).start()

    def settle_mid(n):
        @pl.when(is_mid)
        def _():
            settle(n)

    def settle_rest(n):
        @pl.when(jnp.logical_not(is_mid))
        def _():
            settle(n)

    def inputs_step(c, group):
        at, at_rows = span_of(c), rows_of(group)
        bb, cc = twice(k.b[at, :], 1), twice(k.c[at, :], 1)
        reach, weight = k.scale[0, at_rows, at], k.scale[1, at_rows, at]
        xt, gt = k.xt[group, :, at].astype(F32), k.gt[group, :, at].astype(F32)
        parts = [jnp.concatenate([k.parts[e, group, c, 0], k.parts[e, group, c, 1]], axis=1) for e in range(2)]
        y = mm_nt(parts[0], cc)
        k.row[group, c] += head_sums(y * gt, GROUP) * reach
        dx = per_head(weight, mm_nt(parts[1], bb))
        k.col[group, c] += head_sums(dx * xt, GROUP)
        product = head_sums(xt * gt, GROUP)
        k.cross[group] = product if c == 0 else k.cross[group] + product
        dx = dx + k.dxt[group, c] + per_head(k.skips[at_rows], gt)
        k.gx[group, at] = dx.astype(BF16).T

    def step_sizes():
        rate, bias = column_of(k.rate[...]), column_of(k.bias[...])
        beyond = []
        for group in range(groups):
            last = k.total[0, group] + scaled(k.whole[rows_of(group)], k.state_in[0, group])
            sums = jnp.sum(last * k.state_in[1, group], axis=1)
            beyond.append(jnp.sum(sums, axis=1, keepdims=True))
        beyond = lanes(jnp.concatenate(beyond, axis=0))
        suffix = triangle(True).astype(F32)
        g_rate = jnp.zeros((heads, 1), F32)
        g_bias = jnp.zeros((heads, 1), F32)
        for c in reversed(range(chunks)):
            at = span_of(c)
            row = jnp.concatenate([k.row[group, c] for group in range(groups)], axis=0)
            col = jnp.concatenate([k.col[group, c] for group in range(groups)], axis=0)
            change = row - col
            d_log = jnp.dot(change, suffix, precision=HIGH) + beyond
            beyond = beyond + lanes(jnp.sum(change, axis=1, keepdims=True))
            dt = k.dt[:, at]
            g_dt = col / dt - rate * d_log
            g_raw = g_dt / (1.0 + jnp.exp(-(k.raw[:, at] + bias)))
            k.graw[:, at] = g_raw
            g_rate = g_rate - jnp.sum(dt * d_log, axis=1, keepdims=True)
            g_bias = g_bias + jnp.sum(g_raw, axis=1, keepdims=True)
        cross = jnp.concatenate([k.cross[group] for group in range(groups)], axis=0)
        g_skip = jnp.sum(cross, axis=1, keepdims=True)
        lane = lax.broadcasted_iota(jnp.int32, (heads, CHUNK), 1)
        k.params_in[me] = jnp.where(lane == 0, g_rate, jnp.where(lane == 1, g_skip, g_bias))

    def params_copy(d, place):
        return remote(k.params_in.at[place], k.params_in.at[place], k.param_send, k.param_recv,
                      ctx=(me + d) % peers)

    def every_param():
        some = k.params_in.at[pl.ds(0, peers - 1)]
        return remote(some, some, k.param_send, k.param_recv, ctx=mate)

    def gather_params():
        every_param().wait_recv()
        total = k.params_in[0]
        for d in range(1, peers):
            total = total + k.params_in[d]
        k.grate[...] = row_of(total[:, 0:1])
        k.gskip[...] = row_of(total[:, 1:2])
        k.gbias[...] = row_of(total[:, 2:3])

    def nth_step(n):
        return jnp.where(chip < chips // 2, n, chips - n)

    def exchange(group):
        if group:
            combine(0, group)
            combine(1, group)
        if tree:
            tree_exchange(group)
            return
        for n in range(1, chips):
            chip_copy(nth_step(n), group).start()

    start_small(0, 3)
    start_loads(0, 1)
    start_small(3, 6)
    greet()
    prepare()
    wait_small(3, 6)
    def forth(group):
        states(group)
        pair_copy(0, group).start()

    def back(group):
        backs(group)
        pair_copy(1, group).start()

    forerunner = chip % 2

    @pl.when(forerunner == 0)
    def _():
        states(0)

    @pl.when(forerunner == 1)
    def _():
        backs(0)

    met()
    pair_copy(forerunner, 0).start()
    send_ends()

    @pl.when(forerunner == 0)
    def _():
        backs(0)

    @pl.when(forerunner == 1)
    def _():
        states(0)

    pair_copy(1 - forerunner, 0).start()
    learn_mate()
    combine(forerunner, 0)
    if tree and forwarded:
        exchange(0)
    for group in range(1, groups):
        forth(group)
        if group == 1:
            combine(1 - forerunner, 0)
            if not tree:
                exchange(0)
        back(group)
        if group > 1:
            exchange(group - 1)
    if groups == 1:
        combine(1 - forerunner, 0)

    relayed, settled = 0, 0

    def tend(relays, settles):
        nonlocal relayed, settled
        while relayed < min(relays, len(pieces)):
            relay(relayed)
            relayed += 1
        while settled < min(settles, relayed):
            settle_mid(settled)
            settled += 1

    everyone = list(range(groups))
    if tree:
        handed, returned, passed = 0, 0, 0

        def pass_on(hands, returns, forwards):
            nonlocal handed, returned, passed
            while handed < min(hands, groups):
                hand(handed)
                handed += 1
            while returned < min(returns, groups):
                tree_early(returned)
                returned += 1
            while passed < min(forwards, forwarded):
                forward(passed)
                passed += 1

        for group in everyone:
            if group == 2:
                within(group, 0, chunks - 1)
                pass_on(2, 1, 0)
                within(group, chunks - 1)
            else:
                within(group)
            if group == 0:
                exchange(groups - 1)
                make_coefs()
            pass_on(HANDS[min(group, 3)], HANDS[min(group, 3)], 0)
        score_parts()
        first = everyone[:groups - 2]
        pass_on(groups - 1, groups - 1, 1)
        for c in range(chunks):
            projections(early, c, first)
        pass_on(groups - 1, groups - 1, groups)
        pass_on(groups, groups, groups)
        sooner = everyone[0::2][:groups - 1]
        later = [group for group in everyone if group not in sooner]
        for c in range(chunks):
            if c == chunks - 1:
                for group in sooner:
                    tree_late(group)
            projections(early, c, everyone[len(first):])
            publish(c, c + 1)
            if c == 0:
                pass_on(groups, groups, groups)
        for c in range(chunks):
            projections(late, c, sooner)
            if c == chunks // 2 - 1:
                tend(1, 0)
                for group in later:
                    tree_late(group)
            tend(max(0, c - 1), 0)
        for c in range(chunks):
            projections(late, c, later)
            publish(chunks + 2 * c, chunks + 2 * c + 2)
            tend((3, 3, 3, 4)[min(c, 3)], 0)
    else:
        for group in everyone:
            within(group)
            if group == 0:
                exchange(groups - 1)
                make_coefs()
        score_parts()
        for e in (early, late):
            for group in everyone:
                gather(e, group)
            for c in range(chunks):
                projections(e, c, everyone)
        publish(0, len(pieces))
        tend(chunks, 1)
    turns = [(c, group) for c in range(chunks) for group in everyone]
    for j, turn in enumerate(turns):
        inputs_step(*turn)
        part = 16 * (j + 1) // len(turns)
        for at, relays, settles in LATE_TURNS:
            if part >= at:
                tend(chunks + relays, settles)
    step_sizes()
    for d in range(1, peers):
        params_copy(d, me).start()
    tend(len(pieces), len(pieces))
    for n in range(len(pieces)):
        settle_rest(n)
    gather_params()

    def drain():
        remote(k.pair_in, k.pair_in, k.pair_send, k.pair_recv.at[0, 0], ctx=mate).wait_send()
        remote(k.give, k.give, k.back_send, k.back_recv.at[0, 0], ctx=mate).wait_send()
        if tree:
            tree_drain()
        else:
            for step in range(1, chips):
                sent(step, groups)
        remote(k.zown, k.zown, k.in_send, k.z_recv.at[0, 0], head=inner).wait_send()

        @pl.when(has_outer)
        def _():
            remote(k.zown, k.zown, k.out_send, k.z_recv.at[0, 0], head=outer).wait_send()

        some = k.end_rows.at[pl.ds(0, peers - 1)]
        remote(some, some, k.end_send, k.end_recv.at[0], ctx=mate).wait_send()
        every_param().wait_send()

    drain()


def finish_kernel(groups, gx, graw, ztot, grate, gskip, gbias,
                  gx_out, graw_out, gb_out, gc_out, grate_out, gskip_out, gbias_out, sems):
    wide = gx.shape[2]
    copies = [(gx.at[group], gx_out.at[:, group * wide:(group + 1) * wide]) for group in range(groups)]
    copies += [(ztot.at[1], gb_out), (ztot.at[0], gc_out), (graw, graw_out), (grate, grate_out), (gskip, gskip_out), (gbias, gbias_out)]
    copies = [pltpu.make_async_copy(src, dst, sems.at[i]) for i, (src, dst) in enumerate(copies)]
    for copy in copies:
        copy.start()
    for copy in copies:
        copy.wait()


def on_device(peers, line, tokens_x, raw_dt, in_b, in_c, decay_rate, skip_gain, step_bias, grad_y):
    heads, tokens = raw_dt.shape
    width = tokens_x.shape[1]
    size = width // heads
    state = in_b.shape[1]
    groups = heads // GROUP
    scratch = scratch_of(heads, tokens, size, state, peers)
    names = inputs_and_outputs() + tuple(scratch)

    def shape(*dims, dtype=F32):
        return jax.ShapeDtypeStruct(dims, dtype)

    hbm, vmem = pl.BlockSpec(memory_space=pl.ANY), pl.BlockSpec(memory_space=pltpu.VMEM)
    row = shape(1, heads)
    results = pl.pallas_call(
        functools.partial(kernel, names, peers, line),
        in_specs=[pl.BlockSpec(memory_space=pltpu.HBM)] * 8,
        out_specs=[vmem] * 6,
        out_shape=[shape(groups, tokens, GROUP * size, dtype=BF16), shape(heads, tokens),
                   shape(2, tokens, state), row, row, row],
        scratch_shapes=list(scratch.values()),
        compiler_params=pltpu.CompilerParams(
            collective_id=0, has_side_effects=True, vmem_limit_bytes=VMEM_LIMIT),
        name="layer",
    )(*[pltpu.with_memory_space_constraint(a, pltpu.HBM) for a in (
        tokens_x, grad_y, raw_dt, step_bias[None], decay_rate[None], skip_gain[None], in_b, in_c)])
    gx, graw, gb, gc, grate, gskip, gbias = pl.pallas_call(
        functools.partial(finish_kernel, groups),
        in_specs=[vmem] * 6,
        out_specs=[hbm] * 7,
        out_shape=[shape(tokens, width, dtype=BF16), shape(heads, tokens), shape(tokens, state),
                   shape(tokens, state), row, row, row],
        scratch_shapes=[pltpu.SemaphoreType.DMA((groups + 6,))],
        compiler_params=pltpu.CompilerParams(vmem_limit_bytes=4 << 20),
        name="finish",
    )(*results)
    return gx, graw, gb, gc, grate[0], gskip[0], gbias[0]


def solution(mesh):
    return jax.shard_map(
        functools.partial(on_device, mesh.shape["ctx"], mesh.shape["head"]),
        mesh=mesh,
        in_specs=(
            P("ctx", "head"),
            P("head", "ctx"),
            P("ctx", None),
            P("ctx", None),
            P("head"),
            P("head"),
            P("head"),
            P("ctx", "head"),
        ),
        out_specs=(
            P("ctx", "head"),
            P("head", "ctx"),
            P("ctx", None),
            P("ctx", None),
            P("head"),
            P("head"),
            P("head"),
        ),
        check_vma=False,
    )
```
